512 devices in a mesh: dp: 32 (over z, x), param: 16 (over y, core).
Axes of the slice: x: 4, y: 8, z: 8, core: 2. Of those that a mesh axis runs over, the one named last changes fastest.
Arguments:
- features: bfloat16 [32768, 2048], P('dp'), may hold values from -24 to 24
- w_hidden: bfloat16 [2048, 2048], P(None, 'param'), may hold values from -0.125 to 0.125
- w_head: bfloat16 [2048, 36], P('param'), may hold values from -0.03125 to 0.03125
- base_mean: float32 [32768, 36], P('dp'), may hold values from -5 to 5
- actions: float32 [32768, 36], P('dp'), may hold values from -7 to 7
- advantages: float32 [32768], P('dp'), may hold values from -4 to 4
- log_std: float32 [36], replicated, may hold values from -1 to 0
Outputs:
- step_unit: float32 [2048, 2048], P('dp', 'param')
- kl_ratio: float32 [], replicated
The draws below stay inside these ranges and needn't reach their ends.
All inputs are finite; a program needn't handle non-finite values.
Results may differ from the reference program's by a relative error of at most 0.0049.
Values may be sent and summed in bfloat16 or wider, within the bound.
A program may use at most 64 MiB of HBM per device.

```python
import jax
import jax.numpy as jnp
from jax import lax

D = 2048
UNITS = 2048
ACT = 36
ITERS = 2
BATCH = 32768


def draw_features(key, part):
    key_scale = jax.random.fold_in(key, 11)
    key_body = jax.random.fold_in(key, 12)
    expo = jax.random.exponential(key_scale, (BATCH, 1), jnp.float32)
    row_scale = jnp.minimum(0.4 * jnp.exp(expo / 3.0), 4.0)
    values = jax.random.normal(key_body, (BATCH, D), jnp.float32) * row_scale
    return jnp.clip(values, -24.0, 24.0).astype(jnp.bfloat16)


def levels(rng, shape, pieces, least, largest):
    level, own = 1.0, jax.random.fold_in(rng, 6)
    for axis_at, blocks in pieces:
        heights = jnp.exp(jax.random.uniform(jax.random.fold_in(own, axis_at), (blocks,), jnp.float32, least / len(pieces), largest / len(pieces)))
        level = level * jnp.repeat(heights, shape[axis_at] // blocks).reshape([-1 if axis == axis_at else 1 for axis in range(len(shape))])
    return level


def gaussian(stream_key, extent, width, most, cuts=(), dtype=jnp.bfloat16):
    entries = jax.random.normal(stream_key, extent, jnp.float32) * width
    if len(cuts) > 0:
        entries = levels(stream_key, extent, cuts, -0.22, 0.18) * entries
    return jnp.clip(entries, min=-most, max=most).astype(dtype)


def setup_inputs(seed: int = 0) -> dict:
    keys = jax.random.split(jax.random.key(seed), 8)
    features = draw_features(jax.random.fold_in(keys[7], 71), 0)
    w_hidden = gaussian(keys[1], (D, UNITS), D ** -0.5, 0.125, ((1, 16),))
    w_head = gaussian(keys[2], (UNITS, ACT), (16 * UNITS) ** -0.5, 0.03125, ((0, 16),))
    base_mean = gaussian(keys[3], (BATCH, ACT), 1.0, 5.0, ((0, 32),), jnp.float32)
    actions = gaussian(keys[4], (BATCH, ACT), 1.5, 7.0, ((0, 32),), jnp.float32)
    advantages = gaussian(keys[5], (BATCH,), 1.0, 4.0, ((0, 32),), jnp.float32)
    log_std = jnp.clip(jax.random.uniform(keys[6], (ACT,), jnp.float32, -1.0, 0.0), -1.0, 0.0)
    return {"features": features, "w_hidden": w_hidden, "w_head": w_head, "base_mean": base_mean, "actions": actions, "advantages": advantages, "log_std": log_std}


DAMPING = 0.01
TRIAL_KL = 4.0

def reference(features, w_hidden, w_head, base_mean, actions, advantages, log_std):
    highest = lax.Precision.HIGHEST
    inv_var = jnp.exp(-2.0 * log_std)
    pre = jnp.dot(features, w_hidden, preferred_element_type=jnp.float32)
    hidden = jnp.tanh(pre)
    slope = 1.0 - hidden * hidden
    mean = base_mean + jnp.dot(hidden.astype(jnp.bfloat16), w_head, preferred_element_type=jnp.float32)
    delta = advantages[:, None] * (actions - mean) * inv_var
    head_t = w_head.astype(jnp.float32).T

    def pull(moment):
        return (jnp.dot(moment, head_t, precision=highest) * slope / BATCH).astype(jnp.bfloat16)

    def rowsum(grads):
        return lax.dot_general(features, grads, (((0,), (0,)), ((), ())), preferred_element_type=jnp.float32)

    def fisher(vector):
        change = jnp.dot(features, vector.astype(jnp.bfloat16), preferred_element_type=jnp.float32)
        dh = (change * slope).astype(jnp.bfloat16)
        dmu = jnp.dot(dh, w_head, preferred_element_type=jnp.float32)
        return rowsum(pull(dmu * inv_var)) + DAMPING * vector
    grad = rowsum(pull(delta))
    solution = jnp.zeros_like(grad)
    resid = grad
    direction = grad
    norm_now = jnp.sum(resid * resid)
    for turn in range(ITERS):
        image = fisher(direction)
        alpha = norm_now / jnp.sum(direction * image)
        solution = solution + alpha * direction
        resid = resid - alpha * image
        norm_next = jnp.sum(resid * resid)
        direction = resid + norm_next / norm_now * direction
        norm_now = norm_next
    shs = jnp.sum(solution * (grad - resid))
    step_unit = solution * jnp.sqrt(D * UNITS / shs)
    reach = jnp.sqrt(2.0 * TRIAL_KL / shs)
    moved = jnp.dot(features, (reach * solution).astype(jnp.bfloat16), preferred_element_type=jnp.float32)
    shift = (jnp.tanh(pre + moved) - hidden).astype(jnp.bfloat16)
    dmean = jnp.dot(shift, w_head, preferred_element_type=jnp.float32)
    kl_value = jnp.sum(dmean * dmean * inv_var) / (2.0 * BATCH)
    return (step_unit, kl_value / TRIAL_KL)
```

```python
import functools

import jax
import jax.numpy as jnp
from jax import lax
from jax.experimental import pallas as pl
from jax.experimental.pallas import tpu as pltpu
from jax.sharding import PartitionSpec as P

D = 2048
UNITS = 2048
ITERS = 2


DAMPING = 0.01
TRIAL_KL = 4.0

MESH = pl.DeviceIdType.MESH
AXES = ("dp", "param")


def _device(axis, partner):
    return tuple(partner if name == axis else lax.axis_index(name) for name in AXES)


def _partners(axis, n):
    me = lax.axis_index(axis)
    out = []
    step = 1
    while step < n:
        bit = lax.rem(me // step, 2)
        out.append((me + step - 2 * step * bit, bit))
        step *= 2
    return out


def _greet(axis, partners):
    barrier = pltpu.get_barrier_semaphore()
    for partner, _ in partners:
        pl.semaphore_signal(barrier, inc=1, device_id=_device(axis, partner), device_id_type=MESH)
    pl.semaphore_wait(barrier, len(partners))


def _halving_kernel(axis, n, x_ref, o_ref, recv, work, gat, send_a, recv_a, send_b, recv_b):
    rows = x_ref.shape[0]
    partners = _partners(axis, n)
    k = len(partners)
    _greet(axis, partners)
    cur = x_ref
    off = 0
    offs = []
    for r, (partner, bit) in enumerate(partners):
        half = rows >> (r + 1)
        keep = off + bit * half
        give = off + (1 - bit) * half
        cp = pltpu.make_async_remote_copy(
            src_ref=cur.at[pl.ds(pl.multiple_of(give, 8), half)],
            dst_ref=recv.at[pl.ds(0, half)] if r == 0 else recv.at[pl.ds(rows - (rows >> r), half)],
            send_sem=send_a.at[r],
            recv_sem=recv_a.at[r],
            device_id=_device(axis, partner),
            device_id_type=MESH,
        )
        cp.start()
        cp.wait()
        slot = pl.ds(0, half) if r == 0 else pl.ds(rows - (rows >> r), half)
        kept = pl.ds(pl.multiple_of(keep, 8), half)
        work[kept] = cur[kept] + recv[slot]
        cur = work
        offs.append(off)
        off = keep
    own = rows >> k
    gat[pl.ds(pl.multiple_of(off, 8), own)] = work[pl.ds(pl.multiple_of(off, 8), own)]
    for r in reversed(range(k)):
        partner, bit = partners[r]
        size = rows >> (r + 1)
        cp = pltpu.make_async_remote_copy(
            src_ref=gat.at[pl.ds(pl.multiple_of(off, 8), size)],
            dst_ref=gat.at[pl.ds(pl.multiple_of(off, 8), size)],
            send_sem=send_b.at[r],
            recv_sem=recv_b.at[r],
            device_id=_device(axis, partner),
            device_id_type=MESH,
        )
        cp.start()
        cp.wait()
        off = offs[r]
    o_ref[...] = gat[...]


def _butterfly_kernel(axis, n, x_ref, o_ref, recv, acc, send_sem, recv_sem):
    partners = _partners(axis, n)
    k = len(partners)
    _greet(axis, partners)
    cur = x_ref
    for r, (partner, _) in enumerate(partners):
        cp = pltpu.make_async_remote_copy(
            src_ref=cur,
            dst_ref=recv.at[r],
            send_sem=send_sem.at[r],
            recv_sem=recv_sem.at[r],
            device_id=_device(axis, partner),
            device_id_type=MESH,
        )
        cp.start()
        cp.wait()
        dst = o_ref if r == k - 1 else acc.at[r % 2]
        dst[...] = cur[...] + recv[r]
        cur = dst


_IDS = {}


def _collective_id(key):
    if key not in _IDS:
        _IDS[key] = len(_IDS)
    return _IDS[key]


def allreduce(x, axis, n):
    rows, cols = x.shape
    k = n.bit_length() - 1
    vspec = pl.BlockSpec(memory_space=pltpu.VMEM)
    if rows % (8 * n) == 0:
        kernel = functools.partial(_halving_kernel, axis, n)
        scratch = [
            pltpu.VMEM((rows, cols), jnp.float32),
            pltpu.VMEM((rows, cols), jnp.float32),
            pltpu.VMEM((rows, cols), jnp.float32),
            pltpu.SemaphoreType.DMA((k,)),
            pltpu.SemaphoreType.DMA((k,)),
            pltpu.SemaphoreType.DMA((k,)),
            pltpu.SemaphoreType.DMA((k,)),
        ]
        name = "halving"
    else:
        kernel = functools.partial(_butterfly_kernel, axis, n)
        scratch = [
            pltpu.VMEM((k, rows, cols), jnp.float32),
            pltpu.VMEM((2, rows, cols), jnp.float32),
            pltpu.SemaphoreType.DMA((k,)),
            pltpu.SemaphoreType.DMA((k,)),
        ]
        name = "butterfly"
    cid = _collective_id((name, axis, rows, cols))
    return pl.pallas_call(
        kernel,
        out_shape=jax.ShapeDtypeStruct((rows, cols), jnp.float32),
        in_specs=[vspec],
        out_specs=vspec,
        scratch_shapes=scratch,
        compiler_params=pltpu.CompilerParams(collective_id=cid, has_side_effects=True),
        name=f"allreduce_{name}_{axis}_{rows}x{cols}",
    )(x)


def scalar_sum(s, axis, n):
    tile = jnp.broadcast_to(s.astype(jnp.float32), (8, 128))
    return allreduce(tile, axis, n)[0, 0]


def shards(features, w_hidden, w_head, base_mean, actions, advantages, log_std):
    highest = lax.Precision.HIGHEST
    rows = features.shape[0]
    width = features.shape[1]
    dp_count = lax.axis_size("dp")
    param_count = lax.axis_size("param")
    batch = rows * dp_count
    inv_var = jnp.exp(-2.0 * log_std)
    pre = jnp.dot(features, w_hidden, preferred_element_type=jnp.float32)
    hidden = jnp.tanh(pre)
    slope = 1.0 - hidden * hidden

    def head_total(part):
        return allreduce(jnp.dot(part, w_head, preferred_element_type=jnp.float32), "param", param_count)

    mean = base_mean + head_total(hidden.astype(jnp.bfloat16))
    delta = advantages[:, None] * (actions - mean) * inv_var
    head_t = w_head.astype(jnp.float32).T

    def pull(moment):
        return (jnp.dot(moment, head_t, precision=highest) * slope / batch).astype(jnp.bfloat16)

    def rowsum(grads):
        term = lax.dot_general(
            features, grads, (((0,), (0,)), ((), ())), preferred_element_type=jnp.float32
        )
        return allreduce(term, "dp", dp_count)

    def expand(vector_b):
        return jnp.dot(features, vector_b, preferred_element_type=jnp.float32)

    def total(values):
        return (scalar_sum(values[0], "param", param_count),)

    grad = rowsum(pull(delta))
    solution = jnp.zeros_like(grad)
    resid = grad
    direction = grad
    (norm_now,) = total((jnp.sum(resid * resid),))
    for turn in range(ITERS):
        change = expand(direction.astype(jnp.bfloat16))
        dmu = head_total((change * slope).astype(jnp.bfloat16))
        image = rowsum(pull(dmu * inv_var)) + DAMPING * direction
        (curv,) = total((jnp.sum(direction * image),))
        alpha = norm_now / curv
        solution = solution + alpha * direction
        resid = resid - alpha * image
        (norm_next,) = total((jnp.sum(resid * resid),))
        direction = resid + norm_next / norm_now * direction
        norm_now = norm_next
    (shs,) = total((jnp.sum(solution * (grad - resid)),))
    block = width // dp_count
    step_unit = lax.dynamic_slice_in_dim(
        solution * jnp.sqrt(D * UNITS / shs), lax.axis_index("dp") * block, block, 0
    )
    reach = jnp.sqrt(2.0 * TRIAL_KL / shs)
    moved = expand((reach * solution).astype(jnp.bfloat16))
    shift = (jnp.tanh(pre + moved) - hidden).astype(jnp.bfloat16)
    dmean = head_total(shift)
    kl_value = scalar_sum(jnp.sum(dmean * dmean * inv_var) / (2.0 * batch), "dp", dp_count)
    return (step_unit, kl_value / TRIAL_KL)


def solution(mesh):
    _IDS.clear()
    return jax.shard_map(
        shards,
        mesh=mesh,
        in_specs=(
            P("dp", None),
            P(None, "param"),
            P("param", None),
            P("dp", None),
            P("dp", None),
            P("dp"),
            P(),
        ),
        out_specs=(P("dp", "param"), P()),
        check_vma=False,
    )
```

```python
import functools

import jax
import jax.numpy as jnp
from jax import lax
from jax.experimental import pallas as pl
from jax.experimental.pallas import tpu as pltpu
from jax.sharding import PartitionSpec as P

D = 2048
UNITS = 2048
ITERS = 2


DAMPING = 0.01
TRIAL_KL = 4.0

MESH = pl.DeviceIdType.MESH
AXES = ("dp", "param")


def _device(axis, partner):
    return tuple(partner if name == axis else lax.axis_index(name) for name in AXES)


def _partners(axis, n):
    me = lax.axis_index(axis)
    out = []
    step = 1
    while step < n:
        bit = lax.rem(me // step, 2)
        out.append((me + step - 2 * step * bit, bit))
        step *= 2
    return out


def _greet(axis, partners):
    barrier = pltpu.get_barrier_semaphore()
    for partner, _ in partners:
        pl.semaphore_signal(barrier, inc=1, device_id=_device(axis, partner), device_id_type=MESH)
    pl.semaphore_wait(barrier, len(partners))


def _halving_kernel(axis, n, x_ref, o_ref, recv, work, gat, send_a, recv_a, send_b, recv_b):
    rows = x_ref.shape[0]
    partners = _partners(axis, n)
    k = len(partners)
    _greet(axis, partners)
    cur = x_ref
    off = 0
    offs = []
    for r, (partner, bit) in enumerate(partners):
        half = rows >> (r + 1)
        keep = off + bit * half
        give = off + (1 - bit) * half
        cp = pltpu.make_async_remote_copy(
            src_ref=cur.at[pl.ds(pl.multiple_of(give, 8), half)],
            dst_ref=recv.at[pl.ds(0, half)] if r == 0 else recv.at[pl.ds(rows - (rows >> r), half)],
            send_sem=send_a.at[r],
            recv_sem=recv_a.at[r],
            device_id=_device(axis, partner),
            device_id_type=MESH,
        )
        cp.start()
        cp.wait()
        slot = pl.ds(0, half) if r == 0 else pl.ds(rows - (rows >> r), half)
        kept = pl.ds(pl.multiple_of(keep, 8), half)
        work[kept] = cur[kept] + recv[slot]
        cur = work
        offs.append(off)
        off = keep
    own = rows >> k
    gat[pl.ds(pl.multiple_of(off, 8), own)] = work[pl.ds(pl.multiple_of(off, 8), own)]
    for r in reversed(range(k)):
        partner, bit = partners[r]
        size = rows >> (r + 1)
        cp = pltpu.make_async_remote_copy(
            src_ref=gat.at[pl.ds(pl.multiple_of(off, 8), size)],
            dst_ref=gat.at[pl.ds(pl.multiple_of(off, 8), size)],
            send_sem=send_b.at[r],
            recv_sem=recv_b.at[r],
            device_id=_device(axis, partner),
            device_id_type=MESH,
        )
        cp.start()
        cp.wait()
        off = offs[r]
    o_ref[...] = gat[...]


def _butterfly_kernel(axis, n, x_ref, o_ref, recv, acc, send_sem, recv_sem):
    partners = _partners(axis, n)
    k = len(partners)
    _greet(axis, partners)
    cur = x_ref
    for r, (partner, _) in enumerate(partners):
        cp = pltpu.make_async_remote_copy(
            src_ref=cur,
            dst_ref=recv.at[r],
            send_sem=send_sem.at[r],
            recv_sem=recv_sem.at[r],
            device_id=_device(axis, partner),
            device_id_type=MESH,
        )
        cp.start()
        cp.wait()
        dst = o_ref if r == k - 1 else acc.at[r % 2]
        dst[...] = cur[...] + recv[r]
        cur = dst


def _direct_kernel(axis, n, x_ref, o_ref, recv, gat, send_a, recv_a, send_b, recv_b):
    rows = x_ref.shape[0]
    c = rows // n
    me = lax.axis_index(axis)
    peers = [(j, lax.rem(me + j, n)) for j in range(1, n)]
    _greet(axis, [(p, None) for _, p in peers])
    sends = []
    for j, p in peers:
        cp = pltpu.make_async_remote_copy(
            src_ref=x_ref.at[pl.ds(pl.multiple_of(p * c, 8), c)],
            dst_ref=recv.at[me],
            send_sem=send_a.at[j],
            recv_sem=recv_a.at[j],
            device_id=_device(axis, p),
            device_id_type=MESH,
        )
        cp.start()
        sends.append(cp)
    for cp in sends:
        cp.wait()
    mine = pl.ds(pl.multiple_of(me * c, 8), c)
    recv[me] = x_ref[mine]
    acc = recv[0]
    for s in range(1, n):
        acc = acc + recv[s]
    gat[mine] = acc
    sends = []
    for j, p in peers:
        cp = pltpu.make_async_remote_copy(
            src_ref=gat.at[mine],
            dst_ref=gat.at[mine],
            send_sem=send_b.at[j],
            recv_sem=recv_b.at[j],
            device_id=_device(axis, p),
            device_id_type=MESH,
        )
        cp.start()
        sends.append(cp)
    for cp in sends:
        cp.wait()
    o_ref[...] = gat[...]


def _gather_sum_kernel(axis, n, x_ref, o_ref, recv, send_a, recv_a):
    me = lax.axis_index(axis)
    peers = [(j, lax.rem(me + j, n)) for j in range(1, n)]
    _greet(axis, [(p, None) for _, p in peers])
    sends = []
    for j, p in peers:
        cp = pltpu.make_async_remote_copy(
            src_ref=x_ref,
            dst_ref=recv.at[me],
            send_sem=send_a.at[j],
            recv_sem=recv_a.at[j],
            device_id=_device(axis, p),
            device_id_type=MESH,
        )
        cp.start()
        sends.append(cp)
    for cp in sends:
        cp.wait()
    recv[me] = x_ref[...]
    acc = recv[0]
    for s in range(1, n):
        acc = acc + recv[s]
    o_ref[...] = acc


_IDS = {}


def _collective_id(key):
    if key not in _IDS:
        _IDS[key] = len(_IDS)
    return _IDS[key]


def allreduce(x, axis, n, mode="direct"):
    rows, cols = x.shape
    k = n.bit_length() - 1
    vspec = pl.BlockSpec(memory_space=pltpu.VMEM)
    if rows % (8 * n) != 0:
        mode = "gather"
    if mode == "direct":
        kernel = functools.partial(_direct_kernel, axis, n)
        scratch = [
            pltpu.VMEM((n, rows // n, cols), jnp.float32),
            pltpu.VMEM((rows, cols), jnp.float32),
            pltpu.SemaphoreType.DMA((n,)),
            pltpu.SemaphoreType.DMA((n,)),
            pltpu.SemaphoreType.DMA((n,)),
            pltpu.SemaphoreType.DMA((n,)),
        ]
    elif mode == "halving":
        kernel = functools.partial(_halving_kernel, axis, n)
        scratch = [
            pltpu.VMEM((rows, cols), jnp.float32),
            pltpu.VMEM((rows, cols), jnp.float32),
            pltpu.VMEM((rows, cols), jnp.float32),
            pltpu.SemaphoreType.DMA((k,)),
            pltpu.SemaphoreType.DMA((k,)),
            pltpu.SemaphoreType.DMA((k,)),
            pltpu.SemaphoreType.DMA((k,)),
        ]
    else:
        kernel = functools.partial(_gather_sum_kernel, axis, n)
        scratch = [
            pltpu.VMEM((n, rows, cols), jnp.float32),
            pltpu.SemaphoreType.DMA((n,)),
            pltpu.SemaphoreType.DMA((n,)),
        ]
    cid = _collective_id((mode, axis, rows, cols))
    return pl.pallas_call(
        kernel,
        out_shape=jax.ShapeDtypeStruct((rows, cols), jnp.float32),
        in_specs=[vspec],
        out_specs=vspec,
        scratch_shapes=scratch,
        compiler_params=pltpu.CompilerParams(collective_id=cid, has_side_effects=True),
        name=f"allreduce_{mode}_{axis}_{rows}x{cols}",
    )(x)


def scalar_sum(s, axis, n):
    tile = jnp.broadcast_to(s.astype(jnp.float32), (8, 128))
    return allreduce(tile, axis, n)[0, 0]


def shards(features, w_hidden, w_head, base_mean, actions, advantages, log_std):
    highest = lax.Precision.HIGHEST
    rows = features.shape[0]
    width = features.shape[1]
    dp_count = lax.axis_size("dp")
    param_count = lax.axis_size("param")
    batch = rows * dp_count
    inv_var = jnp.exp(-2.0 * log_std)
    pre = jnp.dot(features, w_hidden, preferred_element_type=jnp.float32)
    hidden = jnp.tanh(pre)
    slope = 1.0 - hidden * hidden

    def head_total(part):
        return allreduce(jnp.dot(part, w_head, preferred_element_type=jnp.float32), "param", param_count)

    mean = base_mean + head_total(hidden.astype(jnp.bfloat16))
    delta = advantages[:, None] * (actions - mean) * inv_var
    head_t = w_head.astype(jnp.float32).T

    def pull(moment):
        return (jnp.dot(moment, head_t, precision=highest) * slope / batch).astype(jnp.bfloat16)

    def rowsum(grads):
        term = lax.dot_general(
            features, grads, (((0,), (0,)), ((), ())), preferred_element_type=jnp.float32
        )
        return allreduce(term, "dp", dp_count)

    def expand(vector_b):
        return jnp.dot(features, vector_b, preferred_element_type=jnp.float32)

    def total(values):
        return (scalar_sum(values[0], "param", param_count),)

    grad = rowsum(pull(delta))
    solution = jnp.zeros_like(grad)
    resid = grad
    direction = grad
    (norm_now,) = total((jnp.sum(resid * resid),))
    for turn in range(ITERS):
        change = expand(direction.astype(jnp.bfloat16))
        dmu = head_total((change * slope).astype(jnp.bfloat16))
        image = rowsum(pull(dmu * inv_var)) + DAMPING * direction
        (curv,) = total((jnp.sum(direction * image),))
        alpha = norm_now / curv
        solution = solution + alpha * direction
        resid = resid - alpha * image
        if turn + 1 < ITERS:
            (norm_next,) = total((jnp.sum(resid * resid),))
            direction = resid + norm_next / norm_now * direction
            norm_now = norm_next
    (shs,) = total((jnp.sum(solution * (grad - resid)),))
    block = width // dp_count
    step_unit = lax.dynamic_slice_in_dim(
        solution * jnp.sqrt(D * UNITS / shs), lax.axis_index("dp") * block, block, 0
    )
    reach = jnp.sqrt(2.0 * TRIAL_KL / shs)
    moved = expand((reach * solution).astype(jnp.bfloat16))
    shift = (jnp.tanh(pre + moved) - hidden).astype(jnp.bfloat16)
    dmean = head_total(shift)
    kl_value = scalar_sum(jnp.sum(dmean * dmean * inv_var) / (2.0 * batch), "dp", dp_count)
    return (step_unit, kl_value / TRIAL_KL)


def solution(mesh):
    _IDS.clear()
    return jax.shard_map(
        shards,
        mesh=mesh,
        in_specs=(
            P("dp", None),
            P(None, "param"),
            P("param", None),
            P("dp", None),
            P("dp", None),
            P("dp"),
            P(),
        ),
        out_specs=(P("dp", "param"), P()),
        check_vma=False,
    )
```

```python
import functools

import jax
import jax.numpy as jnp
from jax import lax
from jax.experimental import pallas as pl
from jax.experimental.pallas import tpu as pltpu
from jax.sharding import PartitionSpec as P

D = 2048
UNITS = 2048
ITERS = 2


DAMPING = 0.01
TRIAL_KL = 4.0

MESH = pl.DeviceIdType.MESH
AXES = ("dp", "param")


def _device(axis, partner):
    return tuple(partner if name == axis else lax.axis_index(name) for name in AXES)


def _partners(axis, n):
    me = lax.axis_index(axis)
    out = []
    step = 1
    while step < n:
        bit = lax.rem(me // step, 2)
        out.append((me + step - 2 * step * bit, bit))
        step *= 2
    return out


def _greet(axis, partners):
    barrier = pltpu.get_barrier_semaphore()
    for partner, _ in partners:
        pl.semaphore_signal(barrier, inc=1, device_id=_device(axis, partner), device_id_type=MESH)
    pl.semaphore_wait(barrier, len(partners))


def _halving_kernel(axis, n, x_ref, o_ref, recv, work, gat, send_a, recv_a, send_b, recv_b):
    rows = x_ref.shape[0]
    partners = _partners(axis, n)
    k = len(partners)
    _greet(axis, partners)
    cur = x_ref
    off = 0
    offs = []
    for r, (partner, bit) in enumerate(partners):
        half = rows >> (r + 1)
        keep = off + bit * half
        give = off + (1 - bit) * half
        cp = pltpu.make_async_remote_copy(
            src_ref=cur.at[pl.ds(pl.multiple_of(give, 8), half)],
            dst_ref=recv.at[pl.ds(0, half)] if r == 0 else recv.at[pl.ds(rows - (rows >> r), half)],
            send_sem=send_a.at[r],
            recv_sem=recv_a.at[r],
            device_id=_device(axis, partner),
            device_id_type=MESH,
        )
        cp.start()
        cp.wait()
        slot = pl.ds(0, half) if r == 0 else pl.ds(rows - (rows >> r), half)
        kept = pl.ds(pl.multiple_of(keep, 8), half)
        work[kept] = cur[kept] + recv[slot]
        cur = work
        offs.append(off)
        off = keep
    own = rows >> k
    gat[pl.ds(pl.multiple_of(off, 8), own)] = work[pl.ds(pl.multiple_of(off, 8), own)]
    for r in reversed(range(k)):
        partner, bit = partners[r]
        size = rows >> (r + 1)
        cp = pltpu.make_async_remote_copy(
            src_ref=gat.at[pl.ds(pl.multiple_of(off, 8), size)],
            dst_ref=gat.at[pl.ds(pl.multiple_of(off, 8), size)],
            send_sem=send_b.at[r],
            recv_sem=recv_b.at[r],
            device_id=_device(axis, partner),
            device_id_type=MESH,
        )
        cp.start()
        cp.wait()
        off = offs[r]
    o_ref[...] = gat[...]


def _butterfly_kernel(axis, n, x_ref, o_ref, recv, acc, send_sem, recv_sem):
    partners = _partners(axis, n)
    k = len(partners)
    _greet(axis, partners)
    cur = x_ref
    for r, (partner, _) in enumerate(partners):
        cp = pltpu.make_async_remote_copy(
            src_ref=cur,
            dst_ref=recv.at[r],
            send_sem=send_sem.at[r],
            recv_sem=recv_sem.at[r],
            device_id=_device(axis, partner),
            device_id_type=MESH,
        )
        cp.start()
        cp.wait()
        dst = o_ref if r == k - 1 else acc.at[r % 2]
        dst[...] = cur[...] + recv[r]
        cur = dst


def _direct_kernel(axis, n, x_ref, o_ref, recv, gat, send_a, recv_a, send_b, recv_b):
    rows = x_ref.shape[0]
    c = rows // n
    me = lax.axis_index(axis)
    peers = [(j, lax.rem(me + j, n)) for j in range(1, n)]
    _greet(axis, [(p, None) for _, p in peers])
    sends = []
    for j, p in peers:
        cp = pltpu.make_async_remote_copy(
            src_ref=x_ref.at[pl.ds(pl.multiple_of(p * c, 8), c)],
            dst_ref=recv.at[me],
            send_sem=send_a.at[j],
            recv_sem=recv_a.at[j],
            device_id=_device(axis, p),
            device_id_type=MESH,
        )
        cp.start()
        sends.append(cp)
    for cp in sends:
        cp.wait()
    mine = pl.ds(pl.multiple_of(me * c, 8), c)
    recv[me] = x_ref[mine]
    acc = recv[0]
    for s in range(1, n):
        acc = acc + recv[s]
    gat[mine] = acc
    sends = []
    for j, p in peers:
        cp = pltpu.make_async_remote_copy(
            src_ref=gat.at[mine],
            dst_ref=gat.at[mine],
            send_sem=send_b.at[j],
            recv_sem=recv_b.at[j],
            device_id=_device(axis, p),
            device_id_type=MESH,
        )
        cp.start()
        sends.append(cp)
    for cp in sends:
        cp.wait()
    o_ref[...] = gat[...]


def _gather_sum_kernel(axis, n, x_ref, o_ref, recv, send_a, recv_a):
    me = lax.axis_index(axis)
    peers = [(j, lax.rem(me + j, n)) for j in range(1, n)]
    _greet(axis, [(p, None) for _, p in peers])
    sends = []
    for j, p in peers:
        cp = pltpu.make_async_remote_copy(
            src_ref=x_ref,
            dst_ref=recv.at[me],
            send_sem=send_a.at[j],
            recv_sem=recv_a.at[j],
            device_id=_device(axis, p),
            device_id_type=MESH,
        )
        cp.start()
        sends.append(cp)
    for cp in sends:
        cp.wait()
    recv[me] = x_ref[...]
    acc = recv[0]
    for s in range(1, n):
        acc = acc + recv[s]
    o_ref[...] = acc


_IDS = {}


def _collective_id(key):
    if key not in _IDS:
        _IDS[key] = len(_IDS)
    return _IDS[key]


def allreduce(x, axis, n, mode="direct"):
    rows, cols = x.shape
    k = n.bit_length() - 1
    vspec = pl.BlockSpec(memory_space=pltpu.VMEM)
    if rows % (8 * n) != 0:
        mode = "gather"
    if mode == "direct":
        kernel = functools.partial(_direct_kernel, axis, n)
        scratch = [
            pltpu.VMEM((n, rows // n, cols), jnp.float32),
            pltpu.VMEM((rows, cols), jnp.float32),
            pltpu.SemaphoreType.DMA((n,)),
            pltpu.SemaphoreType.DMA((n,)),
            pltpu.SemaphoreType.DMA((n,)),
            pltpu.SemaphoreType.DMA((n,)),
        ]
    elif mode == "halving":
        kernel = functools.partial(_halving_kernel, axis, n)
        scratch = [
            pltpu.VMEM((rows, cols), jnp.float32),
            pltpu.VMEM((rows, cols), jnp.float32),
            pltpu.VMEM((rows, cols), jnp.float32),
            pltpu.SemaphoreType.DMA((k,)),
            pltpu.SemaphoreType.DMA((k,)),
            pltpu.SemaphoreType.DMA((k,)),
            pltpu.SemaphoreType.DMA((k,)),
        ]
    else:
        kernel = functools.partial(_gather_sum_kernel, axis, n)
        scratch = [
            pltpu.VMEM((n, rows, cols), jnp.float32),
            pltpu.SemaphoreType.DMA((n,)),
            pltpu.SemaphoreType.DMA((n,)),
        ]
    cid = _collective_id((mode, axis, rows, cols))
    return pl.pallas_call(
        kernel,
        out_shape=jax.ShapeDtypeStruct((rows, cols), jnp.float32),
        in_specs=[vspec],
        out_specs=vspec,
        scratch_shapes=scratch,
        compiler_params=pltpu.CompilerParams(collective_id=cid, has_side_effects=True),
        name=f"allreduce_{mode}_{axis}_{rows}x{cols}",
    )(x)


def _tile_sum(x):
    return jnp.sum(jnp.sum(x, axis=0, keepdims=True), axis=1, keepdims=True)


def _cg_kernel(mode, n_dp, n_pa, *refs):
    if mode == "first":
        part_ref = refs[0]
        ins = 1
    elif mode == "iter":
        part_ref, p_ref, r_ref, x_ref, rr_ref = refs[:5]
        ins = 5
    else:
        part_ref, p_ref, r_ref, x_ref, rr_ref, g_ref = refs[:6]
        ins = 6
    nout = {"first": 3, "iter": 5, "last": 2}[mode]
    outs = refs[ins:ins + nout]
    recv, gat, tiles, srecv, send_a, recv_a, send_b, recv_b, send_s, recv_s = refs[ins + nout:]
    rows = part_ref.shape[0]
    c = rows // n_dp
    me = lax.axis_index("dp")
    mp = lax.axis_index("param")
    dpeers = [(j, lax.rem(me + j, n_dp)) for j in range(1, n_dp)]
    ppeers = [(j, lax.rem(mp + j, n_pa)) for j in range(1, n_pa)]
    barrier = pltpu.get_barrier_semaphore()
    for _, p in dpeers:
        pl.semaphore_signal(barrier, inc=1, device_id=_device("dp", p), device_id_type=MESH)
    for _, p in ppeers:
        pl.semaphore_signal(barrier, inc=1, device_id=_device("param", p), device_id_type=MESH)
    pl.semaphore_wait(barrier, len(dpeers) + len(ppeers))
    sends = []
    for j, p in dpeers:
        cp = pltpu.make_async_remote_copy(
            src_ref=part_ref.at[pl.ds(pl.multiple_of(p * c, 8), c)],
            dst_ref=recv.at[me],
            send_sem=send_a.at[j],
            recv_sem=recv_a.at[j],
            device_id=_device("dp", p),
            device_id_type=MESH,
        )
        cp.start()
        sends.append(cp)
    for cp in sends:
        cp.wait()
    mine = pl.ds(pl.multiple_of(me * c, 8), c)
    recv[me] = part_ref[mine]
    acc = recv[0]
    for s in range(1, n_dp):
        acc = acc + recv[s]
    gat[mine] = acc
    sends = []
    for j, p in dpeers:
        cp = pltpu.make_async_remote_copy(
            src_ref=gat.at[mine],
            dst_ref=gat.at[mine],
            send_sem=send_b.at[j],
            recv_sem=recv_b.at[j],
            device_id=_device("dp", p),
            device_id_type=MESH,
        )
        cp.start()
        sends.append(cp)
    for cp in sends:
        cp.wait()

    def psum_param(k, value):
        tiles[k] = jnp.broadcast_to(value, tiles.shape[1:])
        sends = []
        for j, p in ppeers:
            cp = pltpu.make_async_remote_copy(
                src_ref=tiles.at[k],
                dst_ref=srecv.at[k, mp],
                send_sem=send_s.at[k, j],
                recv_sem=recv_s.at[k, j],
                device_id=_device("param", p),
                device_id_type=MESH,
            )
            cp.start()
            sends.append(cp)
        for cp in sends:
            cp.wait()
        srecv[k, mp] = tiles[k]
        total = srecv[k, 0]
        for s in range(1, n_pa):
            total = total + srecv[k, s]
        return total[0:1, 0:1]

    if mode == "first":
        grad_out, pb_out, rr_out = outs
        grad = gat[...]
        grad_out[...] = grad
        pb_out[...] = grad.astype(jnp.bfloat16)
        rr = psum_param(0, _tile_sum(grad * grad))
        rr_out[...] = jnp.broadcast_to(rr, rr_out.shape)
        return
    direction = p_ref[...]
    rr = rr_ref[0:1, 0:1]
    image = gat[...] + DAMPING * direction
    curv = psum_param(0, _tile_sum(direction * image))
    alpha = rr / curv
    x_new = x_ref[...] + alpha * direction
    r_new = r_ref[...] - alpha * image
    if mode == "iter":
        x_out, r_out, p_out, pb_out, rr_out = outs
        x_out[...] = x_new
        r_out[...] = r_new
        rr_next = psum_param(1, _tile_sum(r_new * r_new))
        p_new = r_new + rr_next / rr * direction
        p_out[...] = p_new
        pb_out[...] = p_new.astype(jnp.bfloat16)
        rr_out[...] = jnp.broadcast_to(rr_next, rr_out.shape)
        return
    step_out, moved_out = outs
    shs = psum_param(1, _tile_sum(x_new * (g_ref[...] - r_new)))
    gat[...] = x_new
    blk = step_out.shape[0]
    step_out[...] = gat[pl.ds(pl.multiple_of(me * blk, 8), blk)] * jnp.sqrt(D * UNITS / shs)
    reach = jnp.sqrt(2.0 * TRIAL_KL / shs)
    moved_out[...] = (reach * x_new).astype(jnp.bfloat16)


def cg_step(mode, n_dp, n_pa, block, *args):
    rows, cols = args[0].shape
    f32, bf16 = jnp.float32, jnp.bfloat16
    big = jax.ShapeDtypeStruct((rows, cols), f32)
    tile = jax.ShapeDtypeStruct((8, 128), f32)
    if mode == "first":
        out_shape = (big, jax.ShapeDtypeStruct((rows, cols), bf16), tile)
    elif mode == "iter":
        out_shape = (big, big, big, jax.ShapeDtypeStruct((rows, cols), bf16), tile)
    else:
        out_shape = (jax.ShapeDtypeStruct((block, cols), f32), jax.ShapeDtypeStruct((rows, cols), bf16))
    vspec = pl.BlockSpec(memory_space=pltpu.VMEM)
    scratch = [
        pltpu.VMEM((n_dp, rows // n_dp, cols), f32),
        pltpu.VMEM((rows, cols), f32),
        pltpu.VMEM((2, 8, 128), f32),
        pltpu.VMEM((2, n_pa, 8, 128), f32),
        pltpu.SemaphoreType.DMA((n_dp,)),
        pltpu.SemaphoreType.DMA((n_dp,)),
        pltpu.SemaphoreType.DMA((n_dp,)),
        pltpu.SemaphoreType.DMA((n_dp,)),
        pltpu.SemaphoreType.DMA((2, n_pa)),
        pltpu.SemaphoreType.DMA((2, n_pa)),
    ]
    cid = _collective_id(("cg", mode, rows, cols))
    return pl.pallas_call(
        functools.partial(_cg_kernel, mode, n_dp, n_pa),
        out_shape=out_shape,
        in_specs=[vspec] * len(args),
        out_specs=tuple([vspec] * len(out_shape)),
        scratch_shapes=scratch,
        compiler_params=pltpu.CompilerParams(collective_id=cid, has_side_effects=True),
        name=f"cg_{mode}",
    )(*args)


def scalar_sum(s, axis, n):
    tile = jnp.broadcast_to(s.astype(jnp.float32), (8, 128))
    return allreduce(tile, axis, n)[0, 0]


def shards(features, w_hidden, w_head, base_mean, actions, advantages, log_std):
    highest = lax.Precision.HIGHEST
    rows = features.shape[0]
    width = features.shape[1]
    dp_count = lax.axis_size("dp")
    param_count = lax.axis_size("param")
    batch = rows * dp_count
    inv_var = jnp.exp(-2.0 * log_std)
    pre = jnp.dot(features, w_hidden, preferred_element_type=jnp.float32)
    hidden = jnp.tanh(pre)
    slope = 1.0 - hidden * hidden

    def head_total(part):
        local = jnp.dot(part, w_head, preferred_element_type=jnp.float32)
        shape = local.shape
        flat = local.reshape(-1, 128)
        lanes = flat.shape[0]
        tall = -(-lanes // (8 * param_count)) * 8 * param_count
        flat = jnp.pad(flat, ((0, tall - lanes), (0, 0)))
        return allreduce(flat, "param", param_count)[:lanes].reshape(shape)

    mean = base_mean + head_total(hidden.astype(jnp.bfloat16))
    delta = advantages[:, None] * (actions - mean) * inv_var
    head_t = w_head.astype(jnp.float32).T

    def pull(moment):
        return (jnp.dot(moment, head_t, precision=highest) * slope / batch).astype(jnp.bfloat16)

    def rowsum(grads):
        return lax.dot_general(
            features, grads, (((0,), (0,)), ((), ())), preferred_element_type=jnp.float32
        )

    def expand(vector_b):
        return jnp.dot(features, vector_b, preferred_element_type=jnp.float32)

    block = width // dp_count
    grad, direction_b, rr = cg_step("first", dp_count, param_count, block, rowsum(pull(delta)))
    direction = grad
    resid = grad
    solution = jnp.zeros_like(grad)
    for turn in range(ITERS):
        change = expand(direction_b)
        dmu = head_total((change * slope).astype(jnp.bfloat16))
        partial = rowsum(pull(dmu * inv_var))
        if turn + 1 < ITERS:
            solution, resid, direction, direction_b, rr = cg_step(
                "iter", dp_count, param_count, block, partial, direction, resid, solution, rr
            )
        else:
            step_unit, moved_b = cg_step(
                "last", dp_count, param_count, block, partial, direction, resid, solution, rr, grad
            )
    moved = expand(moved_b)
    shift = (jnp.tanh(pre + moved) - hidden).astype(jnp.bfloat16)
    dmean = head_total(shift)
    kl_value = scalar_sum(jnp.sum(dmean * dmean * inv_var) / (2.0 * batch), "dp", dp_count)
    return (step_unit, kl_value / TRIAL_KL)


def solution(mesh):
    _IDS.clear()
    return jax.shard_map(
        shards,
        mesh=mesh,
        in_specs=(
            P("dp", None),
            P(None, "param"),
            P("param", None),
            P("dp", None),
            P("dp", None),
            P("dp"),
            P(),
        ),
        out_specs=(P("dp", "param"), P()),
        check_vma=False,
    )
```

```python
import functools

import jax
import jax.numpy as jnp
from jax import lax
from jax.experimental import pallas as pl
from jax.experimental.pallas import tpu as pltpu
from jax.sharding import PartitionSpec as P

D = 2048
UNITS = 2048
ITERS = 2


DAMPING = 0.01
TRIAL_KL = 4.0

MESH = pl.DeviceIdType.MESH
AXES = ("dp", "param")


def _device(axis, partner):
    return tuple(partner if name == axis else lax.axis_index(name) for name in AXES)


def _partners(axis, n):
    me = lax.axis_index(axis)
    out = []
    step = 1
    while step < n:
        bit = lax.rem(me // step, 2)
        out.append((me + step - 2 * step * bit, bit))
        step *= 2
    return out


def _greet(axis, partners):
    barrier = pltpu.get_barrier_semaphore()
    for partner, _ in partners:
        pl.semaphore_signal(barrier, inc=1, device_id=_device(axis, partner), device_id_type=MESH)
    pl.semaphore_wait(barrier, len(partners))


def _halving_kernel(axis, n, x_ref, o_ref, recv, work, gat, send_a, recv_a, send_b, recv_b):
    rows = x_ref.shape[0]
    partners = _partners(axis, n)
    k = len(partners)
    _greet(axis, partners)
    cur = x_ref
    off = 0
    offs = []
    for r, (partner, bit) in enumerate(partners):
        half = rows >> (r + 1)
        keep = off + bit * half
        give = off + (1 - bit) * half
        cp = pltpu.make_async_remote_copy(
            src_ref=cur.at[pl.ds(pl.multiple_of(give, 8), half)],
            dst_ref=recv.at[pl.ds(0, half)] if r == 0 else recv.at[pl.ds(rows - (rows >> r), half)],
            send_sem=send_a.at[r],
            recv_sem=recv_a.at[r],
            device_id=_device(axis, partner),
            device_id_type=MESH,
        )
        cp.start()
        cp.wait()
        slot = pl.ds(0, half) if r == 0 else pl.ds(rows - (rows >> r), half)
        kept = pl.ds(pl.multiple_of(keep, 8), half)
        work[kept] = cur[kept] + recv[slot]
        cur = work
        offs.append(off)
        off = keep
    own = rows >> k
    gat[pl.ds(pl.multiple_of(off, 8), own)] = work[pl.ds(pl.multiple_of(off, 8), own)]
    for r in reversed(range(k)):
        partner, bit = partners[r]
        size = rows >> (r + 1)
        cp = pltpu.make_async_remote_copy(
            src_ref=gat.at[pl.ds(pl.multiple_of(off, 8), size)],
            dst_ref=gat.at[pl.ds(pl.multiple_of(off, 8), size)],
            send_sem=send_b.at[r],
            recv_sem=recv_b.at[r],
            device_id=_device(axis, partner),
            device_id_type=MESH,
        )
        cp.start()
        cp.wait()
        off = offs[r]
    o_ref[...] = gat[...]


def _butterfly_kernel(axis, n, x_ref, o_ref, recv, acc, send_sem, recv_sem):
    partners = _partners(axis, n)
    k = len(partners)
    _greet(axis, partners)
    cur = x_ref
    for r, (partner, _) in enumerate(partners):
        cp = pltpu.make_async_remote_copy(
            src_ref=cur,
            dst_ref=recv.at[r],
            send_sem=send_sem.at[r],
            recv_sem=recv_sem.at[r],
            device_id=_device(axis, partner),
            device_id_type=MESH,
        )
        cp.start()
        cp.wait()
        dst = o_ref if r == k - 1 else acc.at[r % 2]
        dst[...] = cur[...] + recv[r]
        cur = dst


def _direct_kernel(axis, n, x_ref, o_ref, recv, gat, send_a, recv_a, send_b, recv_b):
    rows = x_ref.shape[0]
    c = rows // n
    me = lax.axis_index(axis)
    peers = [(j, lax.rem(me + j, n)) for j in range(1, n)]
    _greet(axis, [(p, None) for _, p in peers])
    sends = []
    for j, p in peers:
        cp = pltpu.make_async_remote_copy(
            src_ref=x_ref.at[pl.ds(pl.multiple_of(p * c, 8), c)],
            dst_ref=recv.at[me],
            send_sem=send_a.at[j],
            recv_sem=recv_a.at[j],
            device_id=_device(axis, p),
            device_id_type=MESH,
        )
        cp.start()
        sends.append(cp)
    for cp in sends:
        cp.wait()
    mine = pl.ds(pl.multiple_of(me * c, 8), c)
    recv[me] = x_ref[mine]
    acc = recv[0]
    for s in range(1, n):
        acc = acc + recv[s]
    gat[mine] = acc
    sends = []
    for j, p in peers:
        cp = pltpu.make_async_remote_copy(
            src_ref=gat.at[mine],
            dst_ref=gat.at[mine],
            send_sem=send_b.at[j],
            recv_sem=recv_b.at[j],
            device_id=_device(axis, p),
            device_id_type=MESH,
        )
        cp.start()
        sends.append(cp)
    for cp in sends:
        cp.wait()
    o_ref[...] = gat[...]


def _gather_sum_kernel(axis, n, x_ref, o_ref, recv, send_a, recv_a):
    me = lax.axis_index(axis)
    peers = [(j, lax.rem(me + j, n)) for j in range(1, n)]
    _greet(axis, [(p, None) for _, p in peers])
    sends = []
    for j, p in peers:
        cp = pltpu.make_async_remote_copy(
            src_ref=x_ref,
            dst_ref=recv.at[me],
            send_sem=send_a.at[j],
            recv_sem=recv_a.at[j],
            device_id=_device(axis, p),
            device_id_type=MESH,
        )
        cp.start()
        sends.append(cp)
    for cp in sends:
        cp.wait()
    recv[me] = x_ref[...]
    acc = recv[0]
    for s in range(1, n):
        acc = acc + recv[s]
    o_ref[...] = acc


_IDS = {}


def _collective_id(key):
    if key not in _IDS:
        _IDS[key] = len(_IDS)
    return _IDS[key]


def allreduce(x, axis, n, mode="direct"):
    rows, cols = x.shape
    k = n.bit_length() - 1
    vspec = pl.BlockSpec(memory_space=pltpu.VMEM)
    if rows % (8 * n) != 0:
        mode = "gather"
    if mode == "direct":
        kernel = functools.partial(_direct_kernel, axis, n)
        scratch = [
            pltpu.VMEM((n, rows // n, cols), jnp.float32),
            pltpu.VMEM((rows, cols), jnp.float32),
            pltpu.SemaphoreType.DMA((n,)),
            pltpu.SemaphoreType.DMA((n,)),
            pltpu.SemaphoreType.DMA((n,)),
            pltpu.SemaphoreType.DMA((n,)),
        ]
    elif mode == "halving":
        kernel = functools.partial(_halving_kernel, axis, n)
        scratch = [
            pltpu.VMEM((rows, cols), jnp.float32),
            pltpu.VMEM((rows, cols), jnp.float32),
            pltpu.VMEM((rows, cols), jnp.float32),
            pltpu.SemaphoreType.DMA((k,)),
            pltpu.SemaphoreType.DMA((k,)),
            pltpu.SemaphoreType.DMA((k,)),
            pltpu.SemaphoreType.DMA((k,)),
        ]
    else:
        kernel = functools.partial(_gather_sum_kernel, axis, n)
        scratch = [
            pltpu.VMEM((n, rows, cols), jnp.float32),
            pltpu.SemaphoreType.DMA((n,)),
            pltpu.SemaphoreType.DMA((n,)),
        ]
    cid = _collective_id((mode, axis, rows, cols))
    return pl.pallas_call(
        kernel,
        out_shape=jax.ShapeDtypeStruct((rows, cols), jnp.float32),
        in_specs=[vspec],
        out_specs=vspec,
        scratch_shapes=scratch,
        compiler_params=pltpu.CompilerParams(collective_id=cid, has_side_effects=True),
        name=f"allreduce_{mode}_{axis}_{rows}x{cols}",
    )(x)


def _tile_sum(x):
    return jnp.sum(jnp.sum(x, axis=0, keepdims=True), axis=1, keepdims=True)


def _cg_kernel(mode, n_dp, n_pa, *refs):
    if mode == "first":
        part_ref = refs[0]
        ins = 1
    elif mode == "iter":
        part_ref, p_ref, r_ref, x_ref, rr_ref = refs[:5]
        ins = 5
    else:
        part_ref, p_ref, r_ref, x_ref, rr_ref, g_ref = refs[:6]
        ins = 6
    nout = {"first": 3, "iter": 5, "last": 2}[mode]
    outs = refs[ins:ins + nout]
    recv, gat, tiles, srecv, send_a, recv_a, send_b, recv_b, send_s, recv_s = refs[ins + nout:]
    rows = part_ref.shape[0]
    c = rows // n_dp
    me = lax.axis_index("dp")
    mp = lax.axis_index("param")
    dpeers = [(j, lax.rem(me + j, n_dp)) for j in range(1, n_dp)]
    ppeers = [(j, lax.rem(mp + j, n_pa)) for j in range(1, n_pa)]
    if mode == "first":
        ppeers = []
    barrier = pltpu.get_barrier_semaphore()
    for _, p in dpeers:
        pl.semaphore_signal(barrier, inc=1, device_id=_device("dp", p), device_id_type=MESH)
    for _, p in ppeers:
        pl.semaphore_signal(barrier, inc=1, device_id=_device("param", p), device_id_type=MESH)
    pl.semaphore_wait(barrier, len(dpeers) + len(ppeers))
    sends = []
    for j, p in dpeers:
        cp = pltpu.make_async_remote_copy(
            src_ref=part_ref.at[pl.ds(pl.multiple_of(p * c, 8), c)],
            dst_ref=recv.at[me],
            send_sem=send_a.at[j],
            recv_sem=recv_a.at[j],
            device_id=_device("dp", p),
            device_id_type=MESH,
        )
        cp.start()
        sends.append(cp)
    for cp in sends:
        cp.wait()
    mine = pl.ds(pl.multiple_of(me * c, 8), c)
    recv[me] = part_ref[mine]
    acc = recv[0]
    for s in range(1, n_dp):
        acc = acc + recv[s]
    gat[mine] = acc
    sends = []
    for j, p in dpeers:
        cp = pltpu.make_async_remote_copy(
            src_ref=gat.at[mine],
            dst_ref=gat.at[mine],
            send_sem=send_b.at[j],
            recv_sem=recv_b.at[j],
            device_id=_device("dp", p),
            device_id_type=MESH,
        )
        cp.start()
        sends.append(cp)
    for cp in sends:
        cp.wait()

    def psum_param(k, values):
        row = lax.broadcasted_iota(jnp.int32, tiles.shape[1:], 0)
        tile = jnp.zeros(tiles.shape[1:], jnp.float32)
        for i, v in enumerate(values):
            tile = jnp.where(row == i, jnp.broadcast_to(v, tile.shape), tile)
        tiles[k] = tile
        sends = []
        for j, p in ppeers:
            cp = pltpu.make_async_remote_copy(
                src_ref=tiles.at[k],
                dst_ref=srecv.at[k, mp],
                send_sem=send_s.at[k, j],
                recv_sem=recv_s.at[k, j],
                device_id=_device("param", p),
                device_id_type=MESH,
            )
            cp.start()
            sends.append(cp)
        for cp in sends:
            cp.wait()
        srecv[k, mp] = tiles[k]
        total = srecv[k, 0]
        for s in range(1, n_pa):
            total = total + srecv[k, s]
        return [total[i:i + 1, 0:1] for i in range(len(values))]

    if mode == "first":
        grad_out, pb_out, rr_out = outs
        grad = gat[...]
        grad_out[...] = grad
        pb_out[...] = grad.astype(jnp.bfloat16)
        rr_out[...] = jnp.broadcast_to(_tile_sum(grad * grad), rr_out.shape)
        return
    direction = p_ref[...]
    resid = r_ref[...]
    rr = rr_ref[0:1, 0:1]
    image = gat[...] + DAMPING * direction
    if mode == "iter":
        curv, r_img, img_img = psum_param(
            0, [_tile_sum(direction * image), _tile_sum(resid * image), _tile_sum(image * image)]
        )
        alpha = rr / curv
        x_out, r_out, p_out, pb_out, rr_out = outs
        x_out[...] = x_ref[...] + alpha * direction
        r_new = resid - alpha * image
        r_out[...] = r_new
        rr_next = rr - 2.0 * alpha * r_img + alpha * alpha * img_img
        p_new = r_new + rr_next / rr * direction
        p_out[...] = p_new
        pb_out[...] = p_new.astype(jnp.bfloat16)
        rr_out[...] = jnp.broadcast_to(rr_next, rr_out.shape)
        return
    sol = x_ref[...]
    gap = g_ref[...] - resid
    curv, x_gap, x_img, p_gap = psum_param(
        0,
        [_tile_sum(direction * image), _tile_sum(sol * gap), _tile_sum(sol * image), _tile_sum(direction * gap)],
    )
    alpha = rr / curv
    x_new = sol + alpha * direction
    shs = x_gap + alpha * (x_img + p_gap) + alpha * alpha * curv
    step_out, moved_out = outs
    gat[...] = x_new
    blk = step_out.shape[0]
    step_out[...] = gat[pl.ds(pl.multiple_of(me * blk, 8), blk)] * jnp.sqrt(D * UNITS / shs)
    reach = jnp.sqrt(2.0 * TRIAL_KL / shs)
    moved_out[...] = (reach * x_new).astype(jnp.bfloat16)


def cg_step(mode, n_dp, n_pa, block, *args):
    rows, cols = args[0].shape
    f32, bf16 = jnp.float32, jnp.bfloat16
    big = jax.ShapeDtypeStruct((rows, cols), f32)
    tile = jax.ShapeDtypeStruct((8, 128), f32)
    if mode == "first":
        out_shape = (big, jax.ShapeDtypeStruct((rows, cols), bf16), tile)
    elif mode == "iter":
        out_shape = (big, big, big, jax.ShapeDtypeStruct((rows, cols), bf16), tile)
    else:
        out_shape = (jax.ShapeDtypeStruct((block, cols), f32), jax.ShapeDtypeStruct((rows, cols), bf16))
    vspec = pl.BlockSpec(memory_space=pltpu.VMEM)
    scratch = [
        pltpu.VMEM((n_dp, rows // n_dp, cols), f32),
        pltpu.VMEM((rows, cols), f32),
        pltpu.VMEM((2, 8, 128), f32),
        pltpu.VMEM((2, n_pa, 8, 128), f32),
        pltpu.SemaphoreType.DMA((n_dp,)),
        pltpu.SemaphoreType.DMA((n_dp,)),
        pltpu.SemaphoreType.DMA((n_dp,)),
        pltpu.SemaphoreType.DMA((n_dp,)),
        pltpu.SemaphoreType.DMA((2, n_pa)),
        pltpu.SemaphoreType.DMA((2, n_pa)),
    ]
    cid = _collective_id(("cg", mode, rows, cols))
    return pl.pallas_call(
        functools.partial(_cg_kernel, mode, n_dp, n_pa),
        out_shape=out_shape,
        in_specs=[vspec] * len(args),
        out_specs=tuple([vspec] * len(out_shape)),
        scratch_shapes=scratch,
        compiler_params=pltpu.CompilerParams(collective_id=cid, has_side_effects=True),
        name=f"cg_{mode}",
    )(*args)


def _head_kernel(n, n_dp, extra, kl, *refs):
    refs = list(refs)
    x_ref = refs.pop(0)
    e_ref = refs.pop(0) if extra else None
    iv_ref = refs.pop(0) if kl else None
    o_ref = refs.pop(0)
    eo_ref = refs.pop(0) if (extra or kl) else None
    recv, gat, erecv, send_a, recv_a, send_b, recv_b, send_e, recv_e = refs
    rows = x_ref.shape[0]
    c = rows // n
    me = lax.axis_index("param")
    md = lax.axis_index("dp")
    peers = [(j, lax.rem(me + j, n)) for j in range(1, n)]
    dpeers = [(j, lax.rem(md + j, n_dp)) for j in range(1, n_dp)] if kl else []
    barrier = pltpu.get_barrier_semaphore()
    for _, p in peers:
        pl.semaphore_signal(barrier, inc=1, device_id=_device("param", p), device_id_type=MESH)
    for _, p in dpeers:
        pl.semaphore_signal(barrier, inc=1, device_id=_device("dp", p), device_id_type=MESH)
    pl.semaphore_wait(barrier, len(peers) + len(dpeers))
    sends = []
    for j, p in peers:
        cp = pltpu.make_async_remote_copy(
            src_ref=x_ref.at[pl.ds(pl.multiple_of(p * c, 8), c)],
            dst_ref=recv.at[me],
            send_sem=send_a.at[j],
            recv_sem=recv_a.at[j],
            device_id=_device("param", p),
            device_id_type=MESH,
        )
        cp.start()
        sends.append(cp)
        if extra:
            cp = pltpu.make_async_remote_copy(
                src_ref=e_ref,
                dst_ref=erecv.at[me],
                send_sem=send_e.at[j],
                recv_sem=recv_e.at[j],
                device_id=_device("param", p),
                device_id_type=MESH,
            )
            cp.start()
            sends.append(cp)
    for cp in sends:
        cp.wait()
    mine = pl.ds(pl.multiple_of(me * c, 8), c)
    recv[me] = x_ref[mine]
    acc = recv[0]
    for s in range(1, n):
        acc = acc + recv[s]
    gat[mine] = acc
    if extra:
        erecv[me] = e_ref[...]
        etot = erecv[0]
        for s in range(1, n):
            etot = etot + erecv[s]
        eo_ref[...] = etot
    sends = []
    for j, p in peers:
        cp = pltpu.make_async_remote_copy(
            src_ref=gat.at[mine],
            dst_ref=gat.at[mine],
            send_sem=send_b.at[j],
            recv_sem=recv_b.at[j],
            device_id=_device("param", p),
            device_id_type=MESH,
        )
        cp.start()
        sends.append(cp)
    for cp in sends:
        cp.wait()
    total = gat[...]
    o_ref[...] = total
    if kl:
        local = _tile_sum(total * total * iv_ref[...])
        erecv[0] = jnp.broadcast_to(local, erecv.shape[1:])
        sends = []
        for j, p in dpeers:
            cp = pltpu.make_async_remote_copy(
                src_ref=erecv.at[0],
                dst_ref=erecv.at[1 + md],
                send_sem=send_e.at[j],
                recv_sem=recv_e.at[j],
                device_id=_device("dp", p),
                device_id_type=MESH,
            )
            cp.start()
            sends.append(cp)
        for cp in sends:
            cp.wait()
        erecv[1 + md] = erecv[0]
        ktot = erecv[1]
        for s in range(1, n_dp):
            ktot = ktot + erecv[1 + s]
        eo_ref[...] = ktot


def head_allreduce(flat, n, n_dp, tile=None, ivflat=None):
    rows, cols = flat.shape
    f32 = jnp.float32
    extra = tile is not None
    kl = ivflat is not None
    args = [flat] + ([tile] if extra else []) + ([ivflat] if kl else [])
    out_shape = [jax.ShapeDtypeStruct((rows, cols), f32)]
    if extra or kl:
        out_shape.append(jax.ShapeDtypeStruct((8, 128), f32))
    m = max(n, n_dp + 1) if kl else n
    vspec = pl.BlockSpec(memory_space=pltpu.VMEM)
    scratch = [
        pltpu.VMEM((n, rows // n, cols), f32),
        pltpu.VMEM((rows, cols), f32),
        pltpu.VMEM((m, 8, 128), f32),
        pltpu.SemaphoreType.DMA((n,)),
        pltpu.SemaphoreType.DMA((n,)),
        pltpu.SemaphoreType.DMA((n,)),
        pltpu.SemaphoreType.DMA((n,)),
        pltpu.SemaphoreType.DMA((max(n, n_dp),)),
        pltpu.SemaphoreType.DMA((max(n, n_dp),)),
    ]
    cid = _collective_id(("head", extra, kl, rows, cols))
    return pl.pallas_call(
        functools.partial(_head_kernel, n, n_dp, extra, kl),
        out_shape=tuple(out_shape),
        in_specs=[vspec] * len(args),
        out_specs=tuple([vspec] * len(out_shape)),
        scratch_shapes=scratch,
        compiler_params=pltpu.CompilerParams(collective_id=cid, has_side_effects=True),
        name=f"head_allreduce_{int(extra)}{int(kl)}",
    )(*args)


def scalar_sum(s, axis, n):
    tile = jnp.broadcast_to(s.astype(jnp.float32), (8, 128))
    return allreduce(tile, axis, n)[0, 0]


def shards(features, w_hidden, w_head, base_mean, actions, advantages, log_std):
    highest = lax.Precision.HIGHEST
    rows = features.shape[0]
    width = features.shape[1]
    dp_count = lax.axis_size("dp")
    param_count = lax.axis_size("param")
    batch = rows * dp_count
    inv_var = jnp.exp(-2.0 * log_std)
    pre = jnp.dot(features, w_hidden, preferred_element_type=jnp.float32)
    hidden = jnp.tanh(pre)
    slope = 1.0 - hidden * hidden

    def to_flat(local):
        flat = local.reshape(-1, 128)
        lanes = flat.shape[0]
        tall = -(-lanes // (8 * param_count)) * 8 * param_count
        return jnp.pad(flat, ((0, tall - lanes), (0, 0)))

    def head_total(part, tile=None, ivflat=None):
        local = jnp.dot(part, w_head, preferred_element_type=jnp.float32)
        res = head_allreduce(to_flat(local), param_count, dp_count, tile, ivflat)
        lanes = local.size // 128
        return (res[0][:lanes].reshape(local.shape),) + tuple(res[1:])

    mean = base_mean + head_total(hidden.astype(jnp.bfloat16))[0]
    delta = advantages[:, None] * (actions - mean) * inv_var
    head_t = w_head.astype(jnp.float32).T

    def pull(moment):
        return (jnp.dot(moment, head_t, precision=highest) * slope / batch).astype(jnp.bfloat16)

    def rowsum(grads):
        return lax.dot_general(
            features, grads, (((0,), (0,)), ((), ())), preferred_element_type=jnp.float32
        )

    def expand(vector_b):
        return jnp.dot(features, vector_b, preferred_element_type=jnp.float32)

    block = width // dp_count
    grad, direction_b, rr_part = cg_step("first", dp_count, param_count, block, rowsum(pull(delta)))
    direction = grad
    resid = grad
    solution = jnp.zeros_like(grad)
    for turn in range(ITERS):
        change = expand(direction_b)
        if turn == 0:
            dmu, rr = head_total((change * slope).astype(jnp.bfloat16), tile=rr_part)
        else:
            (dmu,) = head_total((change * slope).astype(jnp.bfloat16))
        partial = rowsum(pull(dmu * inv_var))
        if turn + 1 < ITERS:
            solution, resid, direction, direction_b, rr = cg_step(
                "iter", dp_count, param_count, block, partial, direction, resid, solution, rr
            )
        else:
            step_unit, moved_b = cg_step(
                "last", dp_count, param_count, block, partial, direction, resid, solution, rr, grad
            )
    moved = expand(moved_b)
    shift = (jnp.tanh(pre + moved) - hidden).astype(jnp.bfloat16)
    ivflat = to_flat(jnp.broadcast_to(inv_var, (rows, inv_var.shape[0])))
    _, kl_tile = head_total(shift, ivflat=ivflat)
    kl_value = kl_tile[0, 0] / (2.0 * batch)
    return (step_unit, kl_value / TRIAL_KL)


def solution(mesh):
    _IDS.clear()
    return jax.shard_map(
        shards,
        mesh=mesh,
        in_specs=(
            P("dp", None),
            P(None, "param"),
            P("param", None),
            P("dp", None),
            P("dp", None),
            P("dp"),
            P(),
        ),
        out_specs=(P("dp", "param"), P()),
        check_vma=False,
    )
```

```python
import functools

import jax
import jax.numpy as jnp
from jax import lax
from jax.experimental import pallas as pl
from jax.experimental.pallas import tpu as pltpu
from jax.sharding import PartitionSpec as P

D = 2048
UNITS = 2048
ITERS = 2


DAMPING = 0.01
TRIAL_KL = 4.0

MESH = pl.DeviceIdType.MESH
AXES = ("dp", "param")
ACT_PAD = 48
HEAD_ROWS = 24
HIGHEST = lax.Precision.HIGHEST


def _device(axis, partner):
    return tuple(partner if name == axis else lax.axis_index(name) for name in AXES)


def _tile_sum(x):
    return jnp.sum(jnp.sum(x, axis=0, keepdims=True), axis=1, keepdims=True)


def _scratch_plan(n_dp, n_pa, rows, width, units, iters):
    f32, bf16 = jnp.float32, jnp.bfloat16
    groups = n_pa // (ACT_PAD // HEAD_ROWS)
    lanes = rows // groups
    dma = pltpu.SemaphoreType.DMA(())
    plan = [
        ("pre", pltpu.VMEM((rows, units), f32)),
        ("hid", pltpu.VMEM((rows, units), f32)),
        ("slope", pltpu.VMEM((rows, units), f32)),
        ("gb", pltpu.VMEM((rows, units), bf16)),
        ("chg", pltpu.VMEM((rows, units), f32)),
        ("part", pltpu.VMEM((width, units), f32)),
        ("grad", pltpu.VMEM((width, units), f32)),
        ("x", pltpu.VMEM((width, units), f32)),
        ("r", pltpu.VMEM((width, units), f32)),
        ("p", pltpu.VMEM((width, units), f32)),
        ("pb", pltpu.VMEM((width, units), bf16)),
    ]
    for h in range(iters + 2):
        plan += [
            (f"hloc{h}", pltpu.VMEM((ACT_PAD, rows), f32)),
            (f"hrecv{h}", pltpu.VMEM((n_pa, HEAD_ROWS, lanes), f32)),
            (f"hgat{h}", pltpu.VMEM((ACT_PAD, rows), f32)),
        ] + [(f"hsem{h}_{i}", dma) for i in range(4)]
    for d in range(iters + 1):
        plan += [
            (f"drecv{d}", pltpu.VMEM((n_dp, width // n_dp, units), f32)),
            (f"dgat{d}", pltpu.VMEM((width, units), f32)),
        ] + [(f"dsem{d}_{i}", dma) for i in range(4)]
    for k in range(iters + 1):
        plan += [
            (f"stile{k}", pltpu.VMEM((8, 128), f32)),
            (f"srecv{k}", pltpu.VMEM((n_pa, 8, 128), f32)),
        ] + [(f"ssem{k}_{i}", dma) for i in range(2)]
    plan += [
        ("ktile", pltpu.VMEM((8, 128), f32)),
        ("krecv", pltpu.VMEM((n_dp, 8, 128), f32)),
        ("ksem0", dma),
        ("ksem1", dma),
    ]
    return plan


def _mega_kernel(names, n_dp, n_pa, iters, batch, *refs):
    (feat, wh, whtb, whtf, bmT, actT, adv, ivT, step_out, kl_out) = refs[:10]
    s = dict(zip(names, refs[10:]))
    rows, width = feat.shape
    units = wh.shape[1]
    groups = n_pa // (ACT_PAD // HEAD_ROWS)
    lanes = rows // groups
    cdp = width // n_dp
    md = lax.axis_index("dp")
    mp = lax.axis_index("param")
    dpeers = [lax.rem(md + j, n_dp) for j in range(1, n_dp)]
    ppeers = [lax.rem(mp + j, n_pa) for j in range(1, n_pa)]

    barrier = pltpu.get_barrier_semaphore()
    for p in dpeers:
        pl.semaphore_signal(barrier, inc=1, device_id=_device("dp", p), device_id_type=MESH)
    for p in ppeers:
        pl.semaphore_signal(barrier, inc=1, device_id=_device("param", p), device_id_type=MESH)
    pl.semaphore_wait(barrier, len(dpeers) + len(ppeers))

    def wait_all(buf, count, send_sem, recv_sem, axis):
        cp = pltpu.make_async_remote_copy(
            src_ref=buf.at[pl.ds(0, count)],
            dst_ref=buf.at[pl.ds(0, count)],
            send_sem=send_sem,
            recv_sem=recv_sem,
            device_id=_device(axis, lax.axis_index(axis)),
            device_id_type=MESH,
        )
        cp.wait_send()
        cp.wait_recv()

    def send(src, dst, send_sem, recv_sem, axis, peer):
        pltpu.make_async_remote_copy(
            src_ref=src, dst_ref=dst, send_sem=send_sem, recv_sem=recv_sem,
            device_id=_device(axis, peer), device_id_type=MESH,
        ).start()

    def hchunk(buf, k):
        r0 = pl.multiple_of((k // groups) * HEAD_ROWS, 8)
        l0 = pl.multiple_of(lax.rem(k, groups) * lanes, 128)
        return buf.at[pl.ds(r0, HEAD_ROWS), pl.ds(l0, lanes)]

    def head_allreduce(h, extra=None):
        loc, recv, gat = s[f"hloc{h}"], s[f"hrecv{h}"], s[f"hgat{h}"]
        sa, ra, sb, rb = (s[f"hsem{h}_{i}"] for i in range(4))
        for p in ppeers:
            send(hchunk(loc, p), recv.at[mp], sa, ra, "param", p)
        if extra is not None:
            tile, erecv = s[f"stile{extra}"], s[f"srecv{extra}"]
            es, er = s[f"ssem{extra}_0"], s[f"ssem{extra}_1"]
            for p in ppeers:
                send(tile, erecv.at[mp], es, er, "param", p)
        wait_all(recv, n_pa - 1, sa, ra, "param")
        recv[mp] = hchunk(loc, mp)[...]
        acc = recv[0]
        for i in range(1, n_pa):
            acc = acc + recv[i]
        hchunk(gat, mp)[...] = acc
        for p in ppeers:
            send(hchunk(gat, mp), hchunk(gat, mp), sb, rb, "param", p)
        total = None
        if extra is not None:
            wait_all(erecv, n_pa - 1, es, er, "param")
            erecv[mp] = tile[...]
            total = erecv[0]
            for i in range(1, n_pa):
                total = total + erecv[i]
        wait_all(recv, n_pa - 1, sb, rb, "param")
        return total

    def dp_allreduce(d):
        recv, gat = s[f"drecv{d}"], s[f"dgat{d}"]
        sa, ra, sb, rb = (s[f"dsem{d}_{i}"] for i in range(4))
        part = s["part"]
        for p in dpeers:
            send(part.at[pl.ds(pl.multiple_of(p * cdp, 8), cdp)], recv.at[md], sa, ra, "dp", p)
        wait_all(recv, n_dp - 1, sa, ra, "dp")
        mine = pl.ds(pl.multiple_of(md * cdp, 8), cdp)
        recv[md] = part[mine]
        acc = recv[0]
        for i in range(1, n_dp):
            acc = acc + recv[i]
        gat[mine] = acc
        for p in dpeers:
            send(gat.at[mine], gat.at[mine], sb, rb, "dp", p)
        wait_all(recv, n_dp - 1, sb, rb, "dp")
        return gat

    def param_round(k, values):
        tile, recv = s[f"stile{k}"], s[f"srecv{k}"]
        ss, sr = s[f"ssem{k}_0"], s[f"ssem{k}_1"]
        row = lax.broadcasted_iota(jnp.int32, (8, 128), 0)
        t = jnp.zeros((8, 128), jnp.float32)
        for i, v in enumerate(values):
            t = jnp.where(row == i, jnp.broadcast_to(v, (8, 128)), t)
        tile[...] = t
        for p in ppeers:
            send(tile, recv.at[mp], ss, sr, "param", p)
        wait_all(recv, n_pa - 1, ss, sr, "param")
        recv[mp] = tile[...]
        total = recv[0]
        for i in range(1, n_pa):
            total = total + recv[i]
        return [total[i:i + 1, 0:1] for i in range(len(values))]

    def expand(vec_b, out):
        blk = min(256, rows)

        def body(i, carry):
            r0 = pl.multiple_of(i * blk, blk)
            out[pl.ds(r0, blk), :] = jnp.dot(feat[pl.ds(r0, blk), :], vec_b[...], preferred_element_type=jnp.float32)
            return carry

        lax.fori_loop(0, rows // blk, body, 0)

    def rowsum(g):
        part = s["part"]
        blk = min(256, width)

        def body(i, carry):
            c0 = pl.multiple_of(i * blk, blk)
            part[pl.ds(c0, blk), :] = lax.dot_general(
                feat[:, pl.ds(c0, blk)], g[...], (((0,), (0,)), ((), ())), preferred_element_type=jnp.float32
            )
            return carry

        lax.fori_loop(0, width // blk, body, 0)

    def head_local(h, vals_b):
        s[f"hloc{h}"][...] = lax.dot_general(
            whtb[...], vals_b, (((1,), (1,)), ((), ())), preferred_element_type=jnp.float32
        )

    def pull(momentT):
        gb = s["gb"]
        prod = lax.dot_general(momentT, whtf[...], (((0,), (0,)), ((), ())), precision=HIGHEST,
                               preferred_element_type=jnp.float32)
        gb[...] = (prod * s["slope"][...] / batch).astype(jnp.bfloat16)
        return gb

    expand(wh, s["pre"])
    hidden = jnp.tanh(s["pre"][...])
    s["hid"][...] = hidden
    s["slope"][...] = 1.0 - hidden * hidden
    head_local(0, hidden.astype(jnp.bfloat16))
    head_allreduce(0)
    meanT = bmT[...] + s["hgat0"][...]
    deltaT = adv[...] * (actT[...] - meanT) * ivT[...]
    rowsum(pull(deltaT))
    grad = dp_allreduce(0)[...]
    s["grad"][...] = grad
    s["r"][...] = grad
    s["p"][...] = grad
    s["x"][...] = jnp.zeros_like(grad)
    s["pb"][...] = grad.astype(jnp.bfloat16)
    s["stile0"][...] = jnp.broadcast_to(_tile_sum(grad * grad), (8, 128))
    rr = None
    for t in range(iters):
        expand(s["pb"], s["chg"])
        dh = (s["chg"][...] * s["slope"][...]).astype(jnp.bfloat16)
        head_local(t + 1, dh)
        total = head_allreduce(t + 1, extra=0 if t == 0 else None)
        if t == 0:
            rr = total[0:1, 0:1]
        rowsum(pull(s[f"hgat{t + 1}"][...] * ivT[...]))
        direction = s["p"][...]
        resid = s["r"][...]
        image = dp_allreduce(t + 1)[...] + DAMPING * direction
        if t + 1 < iters:
            curv, r_img, img_img = param_round(
                t + 1, [_tile_sum(direction * image), _tile_sum(resid * image), _tile_sum(image * image)]
            )
            alpha = rr / curv
            s["x"][...] = s["x"][...] + alpha * direction
            r_new = resid - alpha * image
            s["r"][...] = r_new
            rr_next = rr - 2.0 * alpha * r_img + alpha * alpha * img_img
            p_new = r_new + rr_next / rr * direction
            s["p"][...] = p_new
            s["pb"][...] = p_new.astype(jnp.bfloat16)
            rr = rr_next
        else:
            sol = s["x"][...]
            gap = s["grad"][...] - resid
            curv, x_gap, x_img, p_gap = param_round(
                t + 1,
                [_tile_sum(direction * image), _tile_sum(sol * gap), _tile_sum(sol * image), _tile_sum(direction * gap)],
            )
            alpha = rr / curv
            x_new = sol + alpha * direction
            shs = x_gap + alpha * (x_img + p_gap) + alpha * alpha * curv
            s["x"][...] = x_new
            blk = step_out.shape[0]
            step_out[...] = s["x"][pl.ds(pl.multiple_of(md * blk, 8), blk)] * jnp.sqrt(D * UNITS / shs)
            reach = jnp.sqrt(2.0 * TRIAL_KL / shs)
            s["pb"][...] = (reach * x_new).astype(jnp.bfloat16)
    expand(s["pb"], s["chg"])
    shift = (jnp.tanh(s["pre"][...] + s["chg"][...]) - s["hid"][...]).astype(jnp.bfloat16)
    last = iters + 1
    head_local(last, shift)
    head_allreduce(last)
    dmeanT = s[f"hgat{last}"][...]
    ktile, krecv = s["ktile"], s["krecv"]
    ktile[...] = jnp.broadcast_to(_tile_sum(dmeanT * dmeanT * ivT[...]), (8, 128))
    for p in dpeers:
        send(ktile, krecv.at[md], s["ksem0"], s["ksem1"], "dp", p)
    wait_all(krecv, n_dp - 1, s["ksem0"], s["ksem1"], "dp")
    krecv[md] = ktile[...]
    ktot = krecv[0]
    for i in range(1, n_dp):
        ktot = ktot + krecv[i]
    kl_out[...] = ktot / (2.0 * batch) / TRIAL_KL


def shards(features, w_hidden, w_head, base_mean, actions, advantages, log_std):
    rows, width = features.shape
    units = w_hidden.shape[1]
    act = w_head.shape[1]
    dp_count = lax.axis_size("dp")
    param_count = lax.axis_size("param")
    batch = rows * dp_count
    inv_var = jnp.exp(-2.0 * log_std)
    padT = lambda a: jnp.pad(a.T, ((0, ACT_PAD - act), (0, 0)))
    whtb = padT(w_head)
    whtf = whtb.astype(jnp.float32)
    bmT = padT(base_mean)
    actT = padT(actions)
    ivT = jnp.pad(jnp.broadcast_to(inv_var[:, None], (act, rows)), ((0, ACT_PAD - act), (0, 0)))
    adv = advantages.reshape(1, rows)
    plan = _scratch_plan(dp_count, param_count, rows, width, units, ITERS)
    names = [name for name, _ in plan]
    vspec = pl.BlockSpec(memory_space=pltpu.VMEM)
    block = width // dp_count
    step_unit, kl_tile = pl.pallas_call(
        functools.partial(_mega_kernel, names, dp_count, param_count, ITERS, batch),
        out_shape=(jax.ShapeDtypeStruct((block, units), jnp.float32), jax.ShapeDtypeStruct((8, 128), jnp.float32)),
        in_specs=[vspec] * 8,
        out_specs=(vspec, vspec),
        scratch_shapes=[spec for _, spec in plan],
        compiler_params=pltpu.CompilerParams(collective_id=0, has_side_effects=True, vmem_limit_bytes=60 * 1024 * 1024),
        name="trust_region_step",
    )(features, w_hidden, whtb, whtf, bmT, actT, adv, ivT)
    return (step_unit, kl_tile[0, 0])


def solution(mesh):
    return jax.shard_map(
        shards,
        mesh=mesh,
        in_specs=(
            P("dp", None),
            P(None, "param"),
            P("param", None),
            P("dp", None),
            P("dp", None),
            P("dp"),
            P(),
        ),
        out_specs=(P("dp", "param"), P()),
        check_vma=False,
    )
```

```python
import functools

import jax
import jax.numpy as jnp
from jax import lax
from jax.experimental import pallas as pl
from jax.experimental.pallas import tpu as pltpu
from jax.sharding import PartitionSpec as P

D = 2048
UNITS = 2048
ITERS = 2


DAMPING = 0.01
TRIAL_KL = 4.0

MESH = pl.DeviceIdType.MESH
AXES = ("dp", "param")
ACT_PAD = 48
HEAD_ROWS = 24
HIGHEST = lax.Precision.HIGHEST


def _device(axis, partner):
    return tuple(partner if name == axis else lax.axis_index(name) for name in AXES)


def _tile_sum(x):
    return jnp.sum(jnp.sum(x, axis=0, keepdims=True), axis=1, keepdims=True)


def _scratch_plan(n_dp, n_pa, rows, width, units, iters):
    f32, bf16 = jnp.float32, jnp.bfloat16
    groups = n_pa // (ACT_PAD // HEAD_ROWS)
    lanes = rows // groups
    dma = pltpu.SemaphoreType.DMA(())
    plan = [
        ("pre", pltpu.VMEM((rows, units), f32)),
        ("hid", pltpu.VMEM((rows, units), f32)),
        ("slope", pltpu.VMEM((rows, units), f32)),
        ("gb", pltpu.VMEM((rows, units), bf16)),
        ("chg", pltpu.VMEM((rows, units), f32)),
        ("part", pltpu.VMEM((width, units), f32)),
        ("grad", pltpu.VMEM((width, units), f32)),
        ("x", pltpu.VMEM((width, units), f32)),
        ("r", pltpu.VMEM((width, units), f32)),
        ("p", pltpu.VMEM((width, units), f32)),
        ("pb", pltpu.VMEM((width, units), bf16)),
    ]
    for h in range(iters + 2):
        plan += [
            (f"hloc{h}", pltpu.VMEM((ACT_PAD, rows), f32)),
            (f"hrecv{h}", pltpu.VMEM((n_pa, HEAD_ROWS, lanes), f32)),
            (f"hgat{h}", pltpu.VMEM((ACT_PAD, rows), f32)),
        ] + [(f"hsem{h}_{i}", dma) for i in range(4)]
    for d in range(iters + 1):
        plan += [
            (f"drecv{d}", pltpu.VMEM((n_dp, width // n_dp, units), f32)),
            (f"dgat{d}", pltpu.VMEM((width, units), f32)),
        ] + [(f"dsem{d}_{i}", dma) for i in range(4)]
    for k in range(iters + 1):
        plan += [
            (f"stile{k}", pltpu.VMEM((8, 128), f32)),
            (f"srecv{k}", pltpu.VMEM((n_pa, 8, 128), f32)),
        ] + [(f"ssem{k}_{i}", dma) for i in range(2)]
    plan += [
        ("ktile", pltpu.VMEM((8, 128), f32)),
        ("krecv", pltpu.VMEM((n_dp, 8, 128), f32)),
        ("ksem0", dma),
        ("ksem1", dma),
    ]
    return plan


def _mega_kernel(names, n_dp, n_pa, iters, batch, *refs):
    (feat, wh, whtb, whtf, bmT, actT, adv, ivT, step_out, kl_out) = refs[:10]
    s = dict(zip(names, refs[10:]))
    rows, width = feat.shape
    units = wh.shape[1]
    groups = n_pa // (ACT_PAD // HEAD_ROWS)
    lanes = rows // groups
    cdp = width // n_dp
    md = lax.axis_index("dp")
    mp = lax.axis_index("param")
    dpeers = [lax.rem(md + j, n_dp) for j in range(1, n_dp)]
    ppeers = [lax.rem(mp + j, n_pa) for j in range(1, n_pa)]

    barrier = pltpu.get_barrier_semaphore()
    for p in dpeers:
        pl.semaphore_signal(barrier, inc=1, device_id=_device("dp", p), device_id_type=MESH)
    for p in ppeers:
        pl.semaphore_signal(barrier, inc=1, device_id=_device("param", p), device_id_type=MESH)
    pl.semaphore_wait(barrier, len(dpeers) + len(ppeers))

    def wait_all(buf, count, send_sem, recv_sem, axis):
        cp = pltpu.make_async_remote_copy(
            src_ref=buf.at[pl.ds(0, count)],
            dst_ref=buf.at[pl.ds(0, count)],
            send_sem=send_sem,
            recv_sem=recv_sem,
            device_id=_device(axis, lax.axis_index(axis)),
            device_id_type=MESH,
        )
        cp.wait_send()
        cp.wait_recv()

    def send(src, dst, send_sem, recv_sem, axis, peer):
        pltpu.make_async_remote_copy(
            src_ref=src, dst_ref=dst, send_sem=send_sem, recv_sem=recv_sem,
            device_id=_device(axis, peer), device_id_type=MESH,
        ).start()

    def hchunk(buf, k):
        r0 = pl.multiple_of((k // groups) * HEAD_ROWS, 8)
        l0 = pl.multiple_of(lax.rem(k, groups) * lanes, 128)
        return buf.at[pl.ds(r0, HEAD_ROWS), pl.ds(l0, lanes)]

    def head_allreduce(h, extra=None):
        loc, recv, gat = s[f"hloc{h}"], s[f"hrecv{h}"], s[f"hgat{h}"]
        sa, ra, sb, rb = (s[f"hsem{h}_{i}"] for i in range(4))
        if extra is not None:
            tile, erecv = s[f"stile{extra}"], s[f"srecv{extra}"]
            es, er = s[f"ssem{extra}_0"], s[f"ssem{extra}_1"]
        wait_all(recv, n_pa - 1, sa, ra, "param")
        recv[mp] = hchunk(loc, mp)[...]
        acc = recv[0]
        for i in range(1, n_pa):
            acc = acc + recv[i]
        hchunk(gat, mp)[...] = acc
        for p in ppeers:
            send(hchunk(gat, mp), hchunk(gat, mp), sb, rb, "param", p)
        total = None
        if extra is not None:
            wait_all(erecv, n_pa - 1, es, er, "param")
            erecv[mp] = tile[...]
            total = erecv[0]
            for i in range(1, n_pa):
                total = total + erecv[i]
        wait_all(recv, n_pa - 1, sb, rb, "param")
        return total

    def dp_allreduce(d):
        recv, gat = s[f"drecv{d}"], s[f"dgat{d}"]
        sa, ra, sb, rb = (s[f"dsem{d}_{i}"] for i in range(4))
        part = s["part"]
        wait_all(recv, n_dp - 1, sa, ra, "dp")
        mine = pl.ds(pl.multiple_of(md * cdp, 8), cdp)
        recv[md] = part[mine]
        acc = recv[0]
        for i in range(1, n_dp):
            acc = acc + recv[i]
        gat[mine] = acc
        for p in dpeers:
            send(gat.at[mine], gat.at[mine], sb, rb, "dp", p)
        wait_all(recv, n_dp - 1, sb, rb, "dp")
        return gat

    def param_round(k, values):
        tile, recv = s[f"stile{k}"], s[f"srecv{k}"]
        ss, sr = s[f"ssem{k}_0"], s[f"ssem{k}_1"]
        row = lax.broadcasted_iota(jnp.int32, (8, 128), 0)
        t = jnp.zeros((8, 128), jnp.float32)
        for i, v in enumerate(values):
            t = jnp.where(row == i, jnp.broadcast_to(v, (8, 128)), t)
        tile[...] = t
        for p in ppeers:
            send(tile, recv.at[mp], ss, sr, "param", p)
        wait_all(recv, n_pa - 1, ss, sr, "param")
        recv[mp] = tile[...]
        total = recv[0]
        for i in range(1, n_pa):
            total = total + recv[i]
        return [total[i:i + 1, 0:1] for i in range(len(values))]

    def expand_head(vec_b, out, make_vals, h, extra=None):
        loc, recv = s[f"hloc{h}"], s[f"hrecv{h}"]
        sa, ra = s[f"hsem{h}_0"], s[f"hsem{h}_1"]
        if extra is not None:
            tile, erecv = s[f"stile{extra}"], s[f"srecv{extra}"]
            es, er = s[f"ssem{extra}_0"], s[f"ssem{extra}_1"]
            for p in ppeers:
                send(tile, erecv.at[mp], es, er, "param", p)
        blk = max(lanes, 256)
        for b in range(rows // blk):
            r0 = b * blk
            out[pl.ds(r0, blk), :] = jnp.dot(feat[pl.ds(r0, blk), :], vec_b[...], preferred_element_type=jnp.float32)
            vals = make_vals(r0, blk)
            loc[:, pl.ds(r0, blk)] = lax.dot_general(
                whtb[...], vals, (((1,), (1,)), ((), ())), preferred_element_type=jnp.float32
            )
            for lg in range(r0 // lanes, (r0 + blk) // lanes):
                for rg in range(ACT_PAD // HEAD_ROWS):
                    k = rg * groups + lg

                    @pl.when(mp != k)
                    def _():
                        send(hchunk(loc, k), recv.at[mp], sa, ra, "param", k)

    def rowsum(g, d):
        part, recv = s["part"], s[f"drecv{d}"]
        sa, ra = s[f"dsem{d}_0"], s[f"dsem{d}_1"]
        blk = max(cdp, min(256, width))
        for b in range(width // blk):
            c0 = b * blk
            part[pl.ds(c0, blk), :] = lax.dot_general(
                feat[:, pl.ds(c0, blk)], g[...], (((0,), (0,)), ((), ())), preferred_element_type=jnp.float32
            )
            for k in range(c0 // cdp, (c0 + blk) // cdp):

                @pl.when(md != k)
                def _():
                    send(part.at[pl.ds(k * cdp, cdp)], recv.at[md], sa, ra, "dp", k)

    def pull(momentT):
        gb = s["gb"]
        prod = lax.dot_general(momentT, whtf[...], (((0,), (0,)), ((), ())), precision=HIGHEST,
                               preferred_element_type=jnp.float32)
        gb[...] = (prod * s["slope"][...] / batch).astype(jnp.bfloat16)
        return gb

    def hidden_vals(r0, blk):
        pre = s["pre"][pl.ds(r0, blk), :]
        hidden = jnp.tanh(pre)
        s["hid"][pl.ds(r0, blk), :] = hidden
        s["slope"][pl.ds(r0, blk), :] = 1.0 - hidden * hidden
        return hidden.astype(jnp.bfloat16)

    def change_vals(r0, blk):
        return (s["chg"][pl.ds(r0, blk), :] * s["slope"][pl.ds(r0, blk), :]).astype(jnp.bfloat16)

    def shift_vals(r0, blk):
        moved = jnp.tanh(s["pre"][pl.ds(r0, blk), :] + s["chg"][pl.ds(r0, blk), :])
        return (moved - s["hid"][pl.ds(r0, blk), :]).astype(jnp.bfloat16)

    expand_head(wh, s["pre"], hidden_vals, 0)
    head_allreduce(0)
    meanT = bmT[...] + s["hgat0"][...]
    deltaT = adv[...] * (actT[...] - meanT) * ivT[...]
    rowsum(pull(deltaT), 0)
    grad = dp_allreduce(0)[...]
    s["grad"][...] = grad
    s["r"][...] = grad
    s["p"][...] = grad
    s["x"][...] = jnp.zeros_like(grad)
    s["pb"][...] = grad.astype(jnp.bfloat16)
    s["stile0"][...] = jnp.broadcast_to(_tile_sum(grad * grad), (8, 128))
    rr = None
    for t in range(iters):
        expand_head(s["pb"], s["chg"], change_vals, t + 1, extra=0 if t == 0 else None)
        total = head_allreduce(t + 1, extra=0 if t == 0 else None)
        if t == 0:
            rr = total[0:1, 0:1]
        rowsum(pull(s[f"hgat{t + 1}"][...] * ivT[...]), t + 1)
        direction = s["p"][...]
        resid = s["r"][...]
        image = dp_allreduce(t + 1)[...] + DAMPING * direction
        if t + 1 < iters:
            curv, r_img, img_img = param_round(
                t + 1, [_tile_sum(direction * image), _tile_sum(resid * image), _tile_sum(image * image)]
            )
            alpha = rr / curv
            s["x"][...] = s["x"][...] + alpha * direction
            r_new = resid - alpha * image
            s["r"][...] = r_new
            rr_next = rr - 2.0 * alpha * r_img + alpha * alpha * img_img
            p_new = r_new + rr_next / rr * direction
            s["p"][...] = p_new
            s["pb"][...] = p_new.astype(jnp.bfloat16)
            rr = rr_next
        else:
            sol = s["x"][...]
            gap = s["grad"][...] - resid
            curv, x_gap, x_img, p_gap = param_round(
                t + 1,
                [_tile_sum(direction * image), _tile_sum(sol * gap), _tile_sum(sol * image), _tile_sum(direction * gap)],
            )
            alpha = rr / curv
            x_new = sol + alpha * direction
            shs = x_gap + alpha * (x_img + p_gap) + alpha * alpha * curv
            s["x"][...] = x_new
            blk = step_out.shape[0]
            step_out[...] = s["x"][pl.ds(pl.multiple_of(md * blk, 8), blk)] * jnp.sqrt(D * UNITS / shs)
            reach = jnp.sqrt(2.0 * TRIAL_KL / shs)
            s["pb"][...] = (reach * x_new).astype(jnp.bfloat16)
    last = iters + 1
    expand_head(s["pb"], s["chg"], shift_vals, last)
    head_allreduce(last)
    dmeanT = s[f"hgat{last}"][...]
    ktile, krecv = s["ktile"], s["krecv"]
    ktile[...] = jnp.broadcast_to(_tile_sum(dmeanT * dmeanT * ivT[...]), (8, 128))
    for p in dpeers:
        send(ktile, krecv.at[md], s["ksem0"], s["ksem1"], "dp", p)
    wait_all(krecv, n_dp - 1, s["ksem0"], s["ksem1"], "dp")
    krecv[md] = ktile[...]
    ktot = krecv[0]
    for i in range(1, n_dp):
        ktot = ktot + krecv[i]
    kl_out[...] = ktot / (2.0 * batch) / TRIAL_KL


def shards(features, w_hidden, w_head, base_mean, actions, advantages, log_std):
    rows, width = features.shape
    units = w_hidden.shape[1]
    act = w_head.shape[1]
    dp_count = lax.axis_size("dp")
    param_count = lax.axis_size("param")
    batch = rows * dp_count
    inv_var = jnp.exp(-2.0 * log_std)
    padT = lambda a: jnp.pad(a.T, ((0, ACT_PAD - act), (0, 0)))
    whtb = padT(w_head)
    whtf = whtb.astype(jnp.float32)
    bmT = padT(base_mean)
    actT = padT(actions)
    ivT = jnp.pad(jnp.broadcast_to(inv_var[:, None], (act, rows)), ((0, ACT_PAD - act), (0, 0)))
    adv = advantages.reshape(1, rows)
    plan = _scratch_plan(dp_count, param_count, rows, width, units, ITERS)
    names = [name for name, _ in plan]
    vspec = pl.BlockSpec(memory_space=pltpu.VMEM)
    block = width // dp_count
    step_unit, kl_tile = pl.pallas_call(
        functools.partial(_mega_kernel, names, dp_count, param_count, ITERS, batch),
        out_shape=(jax.ShapeDtypeStruct((block, units), jnp.float32), jax.ShapeDtypeStruct((8, 128), jnp.float32)),
        in_specs=[vspec] * 8,
        out_specs=(vspec, vspec),
        scratch_shapes=[spec for _, spec in plan],
        compiler_params=pltpu.CompilerParams(collective_id=0, has_side_effects=True, vmem_limit_bytes=60 * 1024 * 1024),
        name="trust_region_step",
    )(features, w_hidden, whtb, whtf, bmT, actT, adv, ivT)
    return (step_unit, kl_tile[0, 0])


def solution(mesh):
    return jax.shard_map(
        shards,
        mesh=mesh,
        in_specs=(
            P("dp", None),
            P(None, "param"),
            P("param", None),
            P("dp", None),
            P("dp", None),
            P("dp"),
            P(),
        ),
        out_specs=(P("dp", "param"), P()),
        check_vma=False,
    )
```

```python
import functools

import jax
import jax.numpy as jnp
from jax import lax
from jax.experimental import pallas as pl
from jax.experimental.pallas import tpu as pltpu
from jax.sharding import PartitionSpec as P

D = 2048
UNITS = 2048
ITERS = 2


DAMPING = 0.01
TRIAL_KL = 4.0

MESH = pl.DeviceIdType.MESH
AXES = ("dp", "param")
ACT_PAD = 48
HEAD_ROWS = 24
HIGHEST = lax.Precision.HIGHEST


def _device(axis, partner):
    return tuple(partner if name == axis else lax.axis_index(name) for name in AXES)


def _tile_sum(x):
    return jnp.sum(jnp.sum(x, axis=0, keepdims=True), axis=1, keepdims=True)


def _scratch_plan(n_dp, n_pa, rows, width, units, iters):
    f32, bf16 = jnp.float32, jnp.bfloat16
    groups = n_pa // (ACT_PAD // HEAD_ROWS)
    lanes = rows // groups
    dma = pltpu.SemaphoreType.DMA(())
    plan = [
        ("pre", pltpu.VMEM((rows, units), f32)),
        ("hid", pltpu.VMEM((rows, units), f32)),
        ("slope", pltpu.VMEM((rows, units), f32)),
        ("gb", pltpu.VMEM((rows, units), bf16)),
        ("chg", pltpu.VMEM((rows, units), f32)),
        ("part", pltpu.VMEM((width, units), f32)),
        ("grad", pltpu.VMEM((width, units), f32)),
        ("x", pltpu.VMEM((width, units), f32)),
        ("r", pltpu.VMEM((width, units), f32)),
        ("p", pltpu.VMEM((width, units), f32)),
        ("pb", pltpu.VMEM((width, units), bf16)),
    ]
    for h in range(iters + 2):
        plan += [
            (f"hloc{h}", pltpu.VMEM((ACT_PAD, rows), f32)),
            (f"hrecv{h}", pltpu.VMEM((n_pa, HEAD_ROWS, lanes), f32)),
            (f"hgat{h}", pltpu.VMEM((ACT_PAD, rows), f32)),
        ] + [(f"hsem{h}_{i}", dma) for i in range(4)]
    for d in range(iters):
        plan += [
            (f"drecv{d}", pltpu.VMEM((n_dp, width // n_dp, units), f32)),
            (f"dgat{d}", pltpu.VMEM((width, units), f32)),
        ] + [(f"dsem{d}_{i}", dma) for i in range(4)]
    for k in range(iters + 1):
        plan += [
            (f"stile{k}", pltpu.VMEM((8, 128), f32)),
            (f"srecv{k}", pltpu.VMEM((n_pa, 8, 128), f32)),
        ] + [(f"ssem{k}_{i}", dma) for i in range(2)]
    plan += [
        ("ltile", pltpu.VMEM((8, 128), f32)),
        ("lrecv", pltpu.VMEM((n_dp, 8, 128), f32)),
        ("lsem0", dma),
        ("lsem1", dma),
        ("ktile", pltpu.VMEM((8, 128), f32)),
        ("krecv", pltpu.VMEM((n_dp, 8, 128), f32)),
        ("ksem0", dma),
        ("ksem1", dma),
    ]
    return plan


def _mega_kernel(names, n_dp, n_pa, iters, batch, *refs):
    (feat, wh, whtb, whtf, bmT, actT, adv, ivT, step_out, kl_out) = refs[:10]
    s = dict(zip(names, refs[10:]))
    rows, width = feat.shape
    units = wh.shape[1]
    groups = n_pa // (ACT_PAD // HEAD_ROWS)
    lanes = rows // groups
    cdp = width // n_dp
    md = lax.axis_index("dp")
    mp = lax.axis_index("param")
    dpeers = [lax.rem(md + j, n_dp) for j in range(1, n_dp)]
    ppeers = [lax.rem(mp + j, n_pa) for j in range(1, n_pa)]

    barrier = pltpu.get_barrier_semaphore()
    for p in dpeers:
        pl.semaphore_signal(barrier, inc=1, device_id=_device("dp", p), device_id_type=MESH)
    for p in ppeers:
        pl.semaphore_signal(barrier, inc=1, device_id=_device("param", p), device_id_type=MESH)

    def wait_all(buf, count, send_sem, recv_sem, axis):
        cp = pltpu.make_async_remote_copy(
            src_ref=buf.at[pl.ds(0, count)],
            dst_ref=buf.at[pl.ds(0, count)],
            send_sem=send_sem,
            recv_sem=recv_sem,
            device_id=_device(axis, lax.axis_index(axis)),
            device_id_type=MESH,
        )
        cp.wait_send()
        cp.wait_recv()

    def send(src, dst, send_sem, recv_sem, axis, peer):
        pltpu.make_async_remote_copy(
            src_ref=src, dst_ref=dst, send_sem=send_sem, recv_sem=recv_sem,
            device_id=_device(axis, peer), device_id_type=MESH,
        ).start()

    def hchunk(buf, k):
        r0 = pl.multiple_of((k // groups) * HEAD_ROWS, 8)
        l0 = pl.multiple_of(lax.rem(k, groups) * lanes, 128)
        return buf.at[pl.ds(r0, HEAD_ROWS), pl.ds(l0, lanes)]

    def head_allreduce(h, extra=None):
        loc, recv, gat = s[f"hloc{h}"], s[f"hrecv{h}"], s[f"hgat{h}"]
        sa, ra, sb, rb = (s[f"hsem{h}_{i}"] for i in range(4))
        if extra is not None:
            tile, erecv = s[f"stile{extra}"], s[f"srecv{extra}"]
            es, er = s[f"ssem{extra}_0"], s[f"ssem{extra}_1"]
        wait_all(recv, n_pa - 1, sa, ra, "param")
        recv[mp] = hchunk(loc, mp)[...]
        acc = recv[0]
        for i in range(1, n_pa):
            acc = acc + recv[i]
        hchunk(gat, mp)[...] = acc
        for p in ppeers:
            send(hchunk(gat, mp), hchunk(gat, mp), sb, rb, "param", p)
        total = None
        if extra is not None:
            wait_all(erecv, n_pa - 1, es, er, "param")
            erecv[mp] = tile[...]
            total = erecv[0]
            for i in range(1, n_pa):
                total = total + erecv[i]
        wait_all(recv, n_pa - 1, sb, rb, "param")
        return total

    def dp_allreduce(d):
        recv, gat = s[f"drecv{d}"], s[f"dgat{d}"]
        sa, ra, sb, rb = (s[f"dsem{d}_{i}"] for i in range(4))
        part = s["part"]
        wait_all(recv, n_dp - 1, sa, ra, "dp")
        mine = pl.ds(pl.multiple_of(md * cdp, 8), cdp)
        recv[md] = part[mine]
        acc = recv[0]
        for i in range(1, n_dp):
            acc = acc + recv[i]
        gat[mine] = acc
        for p in dpeers:
            send(gat.at[mine], gat.at[mine], sb, rb, "dp", p)
        wait_all(recv, n_dp - 1, sb, rb, "dp")
        return gat

    def param_start(k, values):
        tile, recv = s[f"stile{k}"], s[f"srecv{k}"]
        ss, sr = s[f"ssem{k}_0"], s[f"ssem{k}_1"]
        row = lax.broadcasted_iota(jnp.int32, (8, 128), 0)
        t = jnp.zeros((8, 128), jnp.float32)
        for i, v in enumerate(values):
            t = jnp.where(row == i, jnp.broadcast_to(v, (8, 128)), t)
        tile[...] = t
        for p in ppeers:
            send(tile, recv.at[mp], ss, sr, "param", p)

    def param_finish(k, count):
        tile, recv = s[f"stile{k}"], s[f"srecv{k}"]
        ss, sr = s[f"ssem{k}_0"], s[f"ssem{k}_1"]
        wait_all(recv, n_pa - 1, ss, sr, "param")
        recv[mp] = tile[...]
        total = recv[0]
        for i in range(1, n_pa):
            total = total + recv[i]
        return [total[i:i + 1, 0:1] for i in range(count)]

    def param_round(k, values):
        param_start(k, values)
        return param_finish(k, len(values))

    def expand_head(vec_b, out, make_vals, h, extra=None, entry=False):
        loc, recv = s[f"hloc{h}"], s[f"hrecv{h}"]
        sa, ra = s[f"hsem{h}_0"], s[f"hsem{h}_1"]
        if extra is not None:
            tile, erecv = s[f"stile{extra}"], s[f"srecv{extra}"]
            es, er = s[f"ssem{extra}_0"], s[f"ssem{extra}_1"]
            for p in ppeers:
                send(tile, erecv.at[mp], es, er, "param", p)
        blk = max(lanes, 256)
        for b in range(rows // blk):
            r0 = b * blk
            out[pl.ds(r0, blk), :] = jnp.dot(feat[pl.ds(r0, blk), :], vec_b[...], preferred_element_type=jnp.float32)
            vals = make_vals(r0, blk)
            loc[:, pl.ds(r0, blk)] = lax.dot_general(
                whtb[...], vals, (((1,), (1,)), ((), ())), preferred_element_type=jnp.float32
            )
            if entry:
                continue
            for lg in range(r0 // lanes, (r0 + blk) // lanes):
                for rg in range(ACT_PAD // HEAD_ROWS):
                    k = rg * groups + lg

                    @pl.when(mp != k)
                    def _():
                        send(hchunk(loc, k), recv.at[mp], sa, ra, "param", k)
        if entry:
            pl.semaphore_wait(barrier, len(dpeers) + len(ppeers))
            for p in ppeers:
                send(hchunk(loc, p), recv.at[mp], sa, ra, "param", p)

    def rowsum(g, d=None):
        part = s["part"]
        blk = max(cdp, min(256, width))
        for b in range(width // blk):
            c0 = b * blk
            part[pl.ds(c0, blk), :] = lax.dot_general(
                feat[:, pl.ds(c0, blk)], g[...], (((0,), (0,)), ((), ())), preferred_element_type=jnp.float32
            )
            if d is None:
                continue
            recv, sa, ra = s[f"drecv{d}"], s[f"dsem{d}_0"], s[f"dsem{d}_1"]
            for k in range(c0 // cdp, (c0 + blk) // cdp):

                @pl.when(md != k)
                def _():
                    send(part.at[pl.ds(k * cdp, cdp)], recv.at[md], sa, ra, "dp", k)

    def pull(momentT):
        gb = s["gb"]
        prod = lax.dot_general(momentT, whtf[...], (((0,), (0,)), ((), ())), precision=HIGHEST,
                               preferred_element_type=jnp.float32)
        gb[...] = (prod * s["slope"][...] / batch).astype(jnp.bfloat16)
        return gb

    def hidden_vals(r0, blk):
        pre = s["pre"][pl.ds(r0, blk), :]
        hidden = jnp.tanh(pre)
        s["hid"][pl.ds(r0, blk), :] = hidden
        s["slope"][pl.ds(r0, blk), :] = 1.0 - hidden * hidden
        return hidden.astype(jnp.bfloat16)

    def change_vals(r0, blk):
        return (s["chg"][pl.ds(r0, blk), :] * s["slope"][pl.ds(r0, blk), :]).astype(jnp.bfloat16)

    def shift_vals(r0, blk):
        moved = jnp.tanh(s["pre"][pl.ds(r0, blk), :] + s["chg"][pl.ds(r0, blk), :])
        return (moved - s["hid"][pl.ds(r0, blk), :]).astype(jnp.bfloat16)

    expand_head(wh, s["pre"], hidden_vals, 0, entry=True)
    head_allreduce(0)
    meanT = bmT[...] + s["hgat0"][...]
    deltaT = adv[...] * (actT[...] - meanT) * ivT[...]
    rowsum(pull(deltaT), 0)
    grad = dp_allreduce(0)[...]
    s["grad"][...] = grad
    s["r"][...] = grad
    s["p"][...] = grad
    s["x"][...] = jnp.zeros_like(grad)
    s["pb"][...] = grad.astype(jnp.bfloat16)
    s["stile0"][...] = jnp.broadcast_to(_tile_sum(grad * grad), (8, 128))
    rr = None
    for t in range(iters):
        expand_head(s["pb"], s["chg"], change_vals, t + 1, extra=0 if t == 0 else None)
        total = head_allreduce(t + 1, extra=0 if t == 0 else None)
        if t == 0:
            rr = total[0:1, 0:1]
        rowsum(pull(s[f"hgat{t + 1}"][...] * ivT[...]), t + 1 if t + 1 < iters else None)
        direction = s["p"][...]
        resid = s["r"][...]
        if t + 1 == iters:
            part = s["part"][...]
            sol = s["x"][...]
            row = lax.broadcasted_iota(jnp.int32, (8, 128), 0)
            lt = jnp.where(row == 0, jnp.broadcast_to(_tile_sum(direction * part), (8, 128)),
                           jnp.broadcast_to(_tile_sum(sol * part), (8, 128)))
            s["ltile"][...] = lt
            for p in dpeers:
                send(s["ltile"], s["lrecv"].at[md], s["lsem0"], s["lsem1"], "dp", p)
            wait_all(s["lrecv"], n_dp - 1, s["lsem0"], s["lsem1"], "dp")
            s["lrecv"][md] = s["ltile"][...]
            lsum = s["lrecv"][0]
            for i in range(1, n_dp):
                lsum = lsum + s["lrecv"][i]
            gap = s["grad"][...] - resid
            param_start(t + 1, [
                lsum[0:1, 0:1] + DAMPING * _tile_sum(direction * direction),
                _tile_sum(sol * gap),
                lsum[1:2, 0:1] + DAMPING * _tile_sum(sol * direction),
                _tile_sum(direction * gap),
            ])
            curv, x_gap, x_img, p_gap = param_finish(t + 1, 4)
            alpha = rr / curv
            x_new = sol + alpha * direction
            shs = x_gap + alpha * (x_img + p_gap) + alpha * alpha * curv
            s["x"][...] = x_new
            blk = step_out.shape[0]
            step_out[...] = s["x"][pl.ds(pl.multiple_of(md * blk, 8), blk)] * jnp.sqrt(D * UNITS / shs)
            reach = jnp.sqrt(2.0 * TRIAL_KL / shs)
            s["pb"][...] = (reach * x_new).astype(jnp.bfloat16)
            continue
        image = dp_allreduce(t + 1)[...] + DAMPING * direction
        if t + 1 < iters:
            curv, r_img, img_img = param_round(
                t + 1, [_tile_sum(direction * image), _tile_sum(resid * image), _tile_sum(image * image)]
            )
            alpha = rr / curv
            s["x"][...] = s["x"][...] + alpha * direction
            r_new = resid - alpha * image
            s["r"][...] = r_new
            rr_next = rr - 2.0 * alpha * r_img + alpha * alpha * img_img
            p_new = r_new + rr_next / rr * direction
            s["p"][...] = p_new
            s["pb"][...] = p_new.astype(jnp.bfloat16)
            rr = rr_next
    last = iters + 1
    expand_head(s["pb"], s["chg"], shift_vals, last)
    head_allreduce(last)
    dmeanT = s[f"hgat{last}"][...]
    ktile, krecv = s["ktile"], s["krecv"]
    ktile[...] = jnp.broadcast_to(_tile_sum(dmeanT * dmeanT * ivT[...]), (8, 128))
    for p in dpeers:
        send(ktile, krecv.at[md], s["ksem0"], s["ksem1"], "dp", p)
    wait_all(krecv, n_dp - 1, s["ksem0"], s["ksem1"], "dp")
    krecv[md] = ktile[...]
    ktot = krecv[0]
    for i in range(1, n_dp):
        ktot = ktot + krecv[i]
    kl_out[...] = ktot / (2.0 * batch) / TRIAL_KL


def shards(features, w_hidden, w_head, base_mean, actions, advantages, log_std):
    rows, width = features.shape
    units = w_hidden.shape[1]
    act = w_head.shape[1]
    dp_count = lax.axis_size("dp")
    param_count = lax.axis_size("param")
    batch = rows * dp_count
    inv_var = jnp.exp(-2.0 * log_std)
    padT = lambda a: jnp.pad(a.T, ((0, ACT_PAD - act), (0, 0)))
    whtb = padT(w_head)
    whtf = whtb.astype(jnp.float32)
    bmT = padT(base_mean)
    actT = padT(actions)
    ivT = jnp.pad(jnp.broadcast_to(inv_var[:, None], (act, rows)), ((0, ACT_PAD - act), (0, 0)))
    adv = advantages.reshape(1, rows)
    plan = _scratch_plan(dp_count, param_count, rows, width, units, ITERS)
    names = [name for name, _ in plan]
    vspec = pl.BlockSpec(memory_space=pltpu.VMEM)
    block = width // dp_count
    step_unit, kl_tile = pl.pallas_call(
        functools.partial(_mega_kernel, names, dp_count, param_count, ITERS, batch),
        out_shape=(jax.ShapeDtypeStruct((block, units), jnp.float32), jax.ShapeDtypeStruct((8, 128), jnp.float32)),
        in_specs=[vspec] * 8,
        out_specs=(vspec, vspec),
        scratch_shapes=[spec for _, spec in plan],
        compiler_params=pltpu.CompilerParams(collective_id=0, has_side_effects=True, vmem_limit_bytes=60 * 1024 * 1024),
        name="trust_region_step",
    )(features, w_hidden, whtb, whtf, bmT, actT, adv, ivT)
    return (step_unit, kl_tile[0, 0])


def solution(mesh):
    return jax.shard_map(
        shards,
        mesh=mesh,
        in_specs=(
            P("dp", None),
            P(None, "param"),
            P("param", None),
            P("dp", None),
            P("dp", None),
            P("dp"),
            P(),
        ),
        out_specs=(P("dp", "param"), P()),
        check_vma=False,
    )
```

```python
import functools

import jax
import jax.numpy as jnp
from jax import lax
from jax.experimental import pallas as pl
from jax.experimental.pallas import tpu as pltpu
from jax.sharding import PartitionSpec as P

D = 2048
UNITS = 2048
ITERS = 2


DAMPING = 0.01
TRIAL_KL = 4.0

MESH = pl.DeviceIdType.MESH
AXES = ("dp", "param")
ACT_PAD = 48
HEAD_ROWS = 24
HIGHEST = lax.Precision.HIGHEST


def _device(axis, partner):
    return tuple(partner if name == axis else lax.axis_index(name) for name in AXES)


def _tile_sum(x):
    return jnp.sum(jnp.sum(x, axis=0, keepdims=True), axis=1, keepdims=True)


def _scratch_plan(n_dp, n_pa, rows, width, units, iters):
    f32, bf16 = jnp.float32, jnp.bfloat16
    groups = n_pa // (ACT_PAD // HEAD_ROWS)
    lanes = rows // groups
    dma = pltpu.SemaphoreType.DMA(())
    plan = [
        ("pre", pltpu.VMEM((rows, units), f32)),
        ("hid", pltpu.VMEM((rows, units), f32)),
        ("slope", pltpu.VMEM((rows, units), f32)),
        ("gb", pltpu.VMEM((rows, units), bf16)),
        ("chg", pltpu.VMEM((rows, units), f32)),
        ("part", pltpu.VMEM((width, units), f32)),
        ("featT", pltpu.VMEM((width, rows), bf16)),
        ("grad", pltpu.VMEM((width, units), f32)),
        ("x", pltpu.VMEM((width, units), f32)),
        ("r", pltpu.VMEM((width, units), f32)),
        ("p", pltpu.VMEM((width, units), f32)),
        ("pb", pltpu.VMEM((width, units), bf16)),
    ]
    for h in range(iters + 2):
        plan += [
            (f"hloc{h}", pltpu.VMEM((ACT_PAD, rows), f32)),
            (f"hrecv{h}", pltpu.VMEM((n_pa, HEAD_ROWS, lanes), f32)),
            (f"hgat{h}", pltpu.VMEM((ACT_PAD, rows), f32)),
        ] + [(f"hsem{h}_{i}", dma) for i in range(4)]
    for d in range(iters):
        plan += [
            (f"drecv{d}", pltpu.VMEM((n_dp, width // n_dp, units), f32)),
            (f"dgat{d}", pltpu.VMEM((width, units), f32)),
        ] + [(f"dsem{d}_{i}", dma) for i in range(4)]
    for k in range(iters + 1):
        plan += [
            (f"stile{k}", pltpu.VMEM((8, 128), f32)),
            (f"srecv{k}", pltpu.VMEM((n_pa, 8, 128), f32)),
        ] + [(f"ssem{k}_{i}", dma) for i in range(2)]
    plan += [
        ("ltile", pltpu.VMEM((8, 128), f32)),
        ("lrecv", pltpu.VMEM((n_dp, 8, 128), f32)),
        ("lsem0", dma),
        ("lsem1", dma),
        ("ktile", pltpu.VMEM((8, 128), f32)),
        ("krecv", pltpu.VMEM((n_dp, 8, 128), f32)),
        ("ksem0", dma),
        ("ksem1", dma),
    ]
    return plan


def _mega_kernel(names, n_dp, n_pa, iters, batch, *refs):
    (feat, wh, whtb, whtf, bmT, actT, adv, ivT, step_out, kl_out) = refs[:10]
    s = dict(zip(names, refs[10:]))
    rows, width = feat.shape
    units = wh.shape[1]
    groups = n_pa // (ACT_PAD // HEAD_ROWS)
    lanes = rows // groups
    cdp = width // n_dp
    md = lax.axis_index("dp")
    mp = lax.axis_index("param")
    dpeers = [lax.rem(md + j, n_dp) for j in range(1, n_dp)]
    ppeers = [lax.rem(mp + j, n_pa) for j in range(1, n_pa)]

    barrier = pltpu.get_barrier_semaphore()
    for p in dpeers:
        pl.semaphore_signal(barrier, inc=1, device_id=_device("dp", p), device_id_type=MESH)
    for p in ppeers:
        pl.semaphore_signal(barrier, inc=1, device_id=_device("param", p), device_id_type=MESH)

    def wait_all(buf, count, send_sem, recv_sem, axis):
        cp = pltpu.make_async_remote_copy(
            src_ref=buf.at[pl.ds(0, count)],
            dst_ref=buf.at[pl.ds(0, count)],
            send_sem=send_sem,
            recv_sem=recv_sem,
            device_id=_device(axis, lax.axis_index(axis)),
            device_id_type=MESH,
        )
        cp.wait_send()
        cp.wait_recv()

    def send(src, dst, send_sem, recv_sem, axis, peer):
        pltpu.make_async_remote_copy(
            src_ref=src, dst_ref=dst, send_sem=send_sem, recv_sem=recv_sem,
            device_id=_device(axis, peer), device_id_type=MESH,
        ).start()

    def hchunk(buf, k):
        r0 = pl.multiple_of((k // groups) * HEAD_ROWS, 8)
        l0 = pl.multiple_of(lax.rem(k, groups) * lanes, 128)
        return buf.at[pl.ds(r0, HEAD_ROWS), pl.ds(l0, lanes)]

    def head_allreduce(h, extra=None):
        loc, recv, gat = s[f"hloc{h}"], s[f"hrecv{h}"], s[f"hgat{h}"]
        sa, ra, sb, rb = (s[f"hsem{h}_{i}"] for i in range(4))
        if extra is not None:
            tile, erecv = s[f"stile{extra}"], s[f"srecv{extra}"]
            es, er = s[f"ssem{extra}_0"], s[f"ssem{extra}_1"]
        wait_all(recv, n_pa - 1, sa, ra, "param")
        recv[mp] = hchunk(loc, mp)[...]
        acc = recv[0]
        for i in range(1, n_pa):
            acc = acc + recv[i]
        hchunk(gat, mp)[...] = acc
        for p in ppeers:
            send(hchunk(gat, mp), hchunk(gat, mp), sb, rb, "param", p)
        total = None
        if extra is not None:
            wait_all(erecv, n_pa - 1, es, er, "param")
            erecv[mp] = tile[...]
            total = erecv[0]
            for i in range(1, n_pa):
                total = total + erecv[i]
        wait_all(recv, n_pa - 1, sb, rb, "param")
        return total

    def dp_allreduce(d):
        recv, gat = s[f"drecv{d}"], s[f"dgat{d}"]
        sa, ra, sb, rb = (s[f"dsem{d}_{i}"] for i in range(4))
        part = s["part"]
        wait_all(recv, n_dp - 1, sa, ra, "dp")
        mine = pl.ds(pl.multiple_of(md * cdp, 8), cdp)
        recv[md] = part[mine]
        acc = recv[0]
        for i in range(1, n_dp):
            acc = acc + recv[i]
        gat[mine] = acc
        for p in dpeers:
            send(gat.at[mine], gat.at[mine], sb, rb, "dp", p)
        wait_all(recv, n_dp - 1, sb, rb, "dp")
        return gat

    def param_start(k, values):
        tile, recv = s[f"stile{k}"], s[f"srecv{k}"]
        ss, sr = s[f"ssem{k}_0"], s[f"ssem{k}_1"]
        row = lax.broadcasted_iota(jnp.int32, (8, 128), 0)
        t = jnp.zeros((8, 128), jnp.float32)
        for i, v in enumerate(values):
            t = jnp.where(row == i, jnp.broadcast_to(v, (8, 128)), t)
        tile[...] = t
        for p in ppeers:
            send(tile, recv.at[mp], ss, sr, "param", p)

    def param_finish(k, count):
        tile, recv = s[f"stile{k}"], s[f"srecv{k}"]
        ss, sr = s[f"ssem{k}_0"], s[f"ssem{k}_1"]
        wait_all(recv, n_pa - 1, ss, sr, "param")
        recv[mp] = tile[...]
        total = recv[0]
        for i in range(1, n_pa):
            total = total + recv[i]
        return [total[i:i + 1, 0:1] for i in range(count)]

    def param_round(k, values):
        param_start(k, values)
        return param_finish(k, len(values))

    def expand_head(vec_b, out, make_vals, h, extra=None, entry=False):
        loc, recv = s[f"hloc{h}"], s[f"hrecv{h}"]
        sa, ra = s[f"hsem{h}_0"], s[f"hsem{h}_1"]
        if extra is not None:
            tile, erecv = s[f"stile{extra}"], s[f"srecv{extra}"]
            es, er = s[f"ssem{extra}_0"], s[f"ssem{extra}_1"]
            for p in ppeers:
                send(tile, erecv.at[mp], es, er, "param", p)
        blk = max(lanes, 256)
        for b in range(rows // blk):
            r0 = b * blk
            out[pl.ds(r0, blk), :] = jnp.dot(feat[pl.ds(r0, blk), :], vec_b[...], preferred_element_type=jnp.float32)
            vals = make_vals(r0, blk)
            loc[:, pl.ds(r0, blk)] = lax.dot_general(
                whtb[...], vals, (((1,), (1,)), ((), ())), preferred_element_type=jnp.float32
            )
            if entry:
                continue
            for lg in range(r0 // lanes, (r0 + blk) // lanes):
                for rg in range(ACT_PAD // HEAD_ROWS):
                    k = rg * groups + lg

                    @pl.when(mp != k)
                    def _():
                        send(hchunk(loc, k), recv.at[mp], sa, ra, "param", k)
        if entry:
            pl.semaphore_wait(barrier, len(dpeers) + len(ppeers))
            for p in ppeers:
                send(hchunk(loc, p), recv.at[mp], sa, ra, "param", p)

    def rowsum(g, d=None):
        part = s["part"]
        blk = max(cdp, min(256, width))
        for b in range(width // blk):
            c0 = b * blk
            part[pl.ds(c0, blk), :] = jnp.dot(
                s["featT"][pl.ds(c0, blk), :], g[...], preferred_element_type=jnp.float32
            )
            if d is None:
                continue
            recv, sa, ra = s[f"drecv{d}"], s[f"dsem{d}_0"], s[f"dsem{d}_1"]
            for k in range(c0 // cdp, (c0 + blk) // cdp):

                @pl.when(md != k)
                def _():
                    send(part.at[pl.ds(k * cdp, cdp)], recv.at[md], sa, ra, "dp", k)

    def pull(momentT):
        gb = s["gb"]
        prod = lax.dot_general(momentT, whtf[...], (((0,), (0,)), ((), ())), precision=HIGHEST,
                               preferred_element_type=jnp.float32)
        gb[...] = (prod * s["slope"][...] / batch).astype(jnp.bfloat16)
        return gb

    def hidden_vals(r0, blk):
        pre = s["pre"][pl.ds(r0, blk), :]
        hidden = jnp.tanh(pre)
        s["hid"][pl.ds(r0, blk), :] = hidden
        s["slope"][pl.ds(r0, blk), :] = 1.0 - hidden * hidden
        return hidden.astype(jnp.bfloat16)

    def change_vals(r0, blk):
        return (s["chg"][pl.ds(r0, blk), :] * s["slope"][pl.ds(r0, blk), :]).astype(jnp.bfloat16)

    def shift_vals(r0, blk):
        moved = jnp.tanh(s["pre"][pl.ds(r0, blk), :] + s["chg"][pl.ds(r0, blk), :])
        return (moved - s["hid"][pl.ds(r0, blk), :]).astype(jnp.bfloat16)

    tblk = min(256, width)
    for c in range(width // tblk):
        s["featT"][pl.ds(c * tblk, tblk), :] = feat[:, pl.ds(c * tblk, tblk)].T
    expand_head(wh, s["pre"], hidden_vals, 0, entry=True)
    head_allreduce(0)
    meanT = bmT[...] + s["hgat0"][...]
    deltaT = adv[...] * (actT[...] - meanT) * ivT[...]
    rowsum(pull(deltaT), 0)
    grad = dp_allreduce(0)[...]
    s["grad"][...] = grad
    s["r"][...] = grad
    s["p"][...] = grad
    s["x"][...] = jnp.zeros_like(grad)
    s["pb"][...] = grad.astype(jnp.bfloat16)
    s["stile0"][...] = jnp.broadcast_to(_tile_sum(grad * grad), (8, 128))
    rr = None
    for t in range(iters):
        expand_head(s["pb"], s["chg"], change_vals, t + 1, extra=0 if t == 0 else None)
        total = head_allreduce(t + 1, extra=0 if t == 0 else None)
        if t == 0:
            rr = total[0:1, 0:1]
        rowsum(pull(s[f"hgat{t + 1}"][...] * ivT[...]), t + 1 if t + 1 < iters else None)
        direction = s["p"][...]
        resid = s["r"][...]
        if t + 1 == iters:
            part = s["part"][...]
            sol = s["x"][...]
            row = lax.broadcasted_iota(jnp.int32, (8, 128), 0)
            lt = jnp.where(row == 0, jnp.broadcast_to(_tile_sum(direction * part), (8, 128)),
                           jnp.broadcast_to(_tile_sum(sol * part), (8, 128)))
            s["ltile"][...] = lt
            for p in dpeers:
                send(s["ltile"], s["lrecv"].at[md], s["lsem0"], s["lsem1"], "dp", p)
            wait_all(s["lrecv"], n_dp - 1, s["lsem0"], s["lsem1"], "dp")
            s["lrecv"][md] = s["ltile"][...]
            lsum = s["lrecv"][0]
            for i in range(1, n_dp):
                lsum = lsum + s["lrecv"][i]
            gap = s["grad"][...] - resid
            param_start(t + 1, [
                lsum[0:1, 0:1] + DAMPING * _tile_sum(direction * direction),
                _tile_sum(sol * gap),
                lsum[1:2, 0:1] + DAMPING * _tile_sum(sol * direction),
                _tile_sum(direction * gap),
            ])
            curv, x_gap, x_img, p_gap = param_finish(t + 1, 4)
            alpha = rr / curv
            x_new = sol + alpha * direction
            shs = x_gap + alpha * (x_img + p_gap) + alpha * alpha * curv
            s["x"][...] = x_new
            blk = step_out.shape[0]
            step_out[...] = s["x"][pl.ds(pl.multiple_of(md * blk, 8), blk)] * jnp.sqrt(D * UNITS / shs)
            reach = jnp.sqrt(2.0 * TRIAL_KL / shs)
            s["pb"][...] = (reach * x_new).astype(jnp.bfloat16)
            continue
        image = dp_allreduce(t + 1)[...] + DAMPING * direction
        if t + 1 < iters:
            curv, r_img, img_img = param_round(
                t + 1, [_tile_sum(direction * image), _tile_sum(resid * image), _tile_sum(image * image)]
            )
            alpha = rr / curv
            s["x"][...] = s["x"][...] + alpha * direction
            r_new = resid - alpha * image
            s["r"][...] = r_new
            rr_next = rr - 2.0 * alpha * r_img + alpha * alpha * img_img
            p_new = r_new + rr_next / rr * direction
            s["p"][...] = p_new
            s["pb"][...] = p_new.astype(jnp.bfloat16)
            rr = rr_next
    last = iters + 1
    expand_head(s["pb"], s["chg"], shift_vals, last)
    head_allreduce(last)
    dmeanT = s[f"hgat{last}"][...]
    ktile, krecv = s["ktile"], s["krecv"]
    ktile[...] = jnp.broadcast_to(_tile_sum(dmeanT * dmeanT * ivT[...]), (8, 128))
    for p in dpeers:
        send(ktile, krecv.at[md], s["ksem0"], s["ksem1"], "dp", p)
    wait_all(krecv, n_dp - 1, s["ksem0"], s["ksem1"], "dp")
    krecv[md] = ktile[...]
    ktot = krecv[0]
    for i in range(1, n_dp):
        ktot = ktot + krecv[i]
    kl_out[...] = ktot / (2.0 * batch) / TRIAL_KL


def shards(features, w_hidden, w_head, base_mean, actions, advantages, log_std):
    rows, width = features.shape
    units = w_hidden.shape[1]
    act = w_head.shape[1]
    dp_count = lax.axis_size("dp")
    param_count = lax.axis_size("param")
    batch = rows * dp_count
    inv_var = jnp.exp(-2.0 * log_std)
    padT = lambda a: jnp.pad(a.T, ((0, ACT_PAD - act), (0, 0)))
    whtb = padT(w_head)
    whtf = whtb.astype(jnp.float32)
    bmT = padT(base_mean)
    actT = padT(actions)
    ivT = jnp.pad(jnp.broadcast_to(inv_var[:, None], (act, rows)), ((0, ACT_PAD - act), (0, 0)))
    adv = advantages.reshape(1, rows)
    plan = _scratch_plan(dp_count, param_count, rows, width, units, ITERS)
    names = [name for name, _ in plan]
    vspec = pl.BlockSpec(memory_space=pltpu.VMEM)
    block = width // dp_count
    step_unit, kl_tile = pl.pallas_call(
        functools.partial(_mega_kernel, names, dp_count, param_count, ITERS, batch),
        out_shape=(jax.ShapeDtypeStruct((block, units), jnp.float32), jax.ShapeDtypeStruct((8, 128), jnp.float32)),
        in_specs=[vspec] * 8,
        out_specs=(vspec, vspec),
        scratch_shapes=[spec for _, spec in plan],
        compiler_params=pltpu.CompilerParams(collective_id=0, has_side_effects=True, vmem_limit_bytes=60 * 1024 * 1024),
        name="trust_region_step",
    )(features, w_hidden, whtb, whtf, bmT, actT, adv, ivT)
    return (step_unit, kl_tile[0, 0])


def solution(mesh):
    return jax.shard_map(
        shards,
        mesh=mesh,
        in_specs=(
            P("dp", None),
            P(None, "param"),
            P("param", None),
            P("dp", None),
            P("dp", None),
            P("dp"),
            P(),
        ),
        out_specs=(P("dp", "param"), P()),
        check_vma=False,
    )
```

```python
import functools

import jax
import jax.numpy as jnp
from jax import lax
from jax.experimental import pallas as pl
from jax.experimental.pallas import tpu as pltpu
from jax.sharding import PartitionSpec as P

D = 2048
UNITS = 2048
ITERS = 2


DAMPING = 0.01
TRIAL_KL = 4.0

MESH = pl.DeviceIdType.MESH
AXES = ("dp", "param")
ACT_PAD = 48
HEAD_ROWS = 24
HIGHEST = lax.Precision.HIGHEST


def _device(axis, partner):
    return tuple(partner if name == axis else lax.axis_index(name) for name in AXES)


def _tile_sum(x):
    return jnp.sum(jnp.sum(x, axis=0, keepdims=True), axis=1, keepdims=True)


def _scratch_plan(n_dp, n_pa, rows, width, units, iters):
    f32, bf16 = jnp.float32, jnp.bfloat16
    groups = n_pa // (ACT_PAD // HEAD_ROWS)
    lanes = rows // groups
    dma = pltpu.SemaphoreType.DMA(())
    plan = [
        ("pre", pltpu.VMEM((rows, units), f32)),
        ("hid", pltpu.VMEM((rows, units), f32)),
        ("slope", pltpu.VMEM((rows, units), f32)),
        ("gb", pltpu.VMEM((rows, units), bf16)),
        ("chg", pltpu.VMEM((rows, units), f32)),
        ("part", pltpu.VMEM((width, units), f32)),
        ("featT", pltpu.VMEM((width, rows), bf16)),
        ("grad", pltpu.VMEM((width, units), f32)),
        ("x", pltpu.VMEM((width, units), f32)),
        ("r", pltpu.VMEM((width, units), f32)),
        ("p", pltpu.VMEM((width, units), f32)),
        ("pb", pltpu.VMEM((width, units), bf16)),
    ]
    for h in range(iters + 2):
        plan += [
            (f"hloc{h}", pltpu.VMEM((ACT_PAD, rows), f32)),
            (f"hrecv{h}", pltpu.VMEM((n_pa, HEAD_ROWS, lanes), f32)),
            (f"hgat{h}", pltpu.VMEM((ACT_PAD, rows), f32)),
        ] + [(f"hsem{h}_{i}", dma) for i in range(4)]
    for d in range(iters):
        plan += [
            (f"drecv{d}", pltpu.VMEM((n_dp, width // n_dp, units), f32)),
            (f"dgat{d}", pltpu.VMEM((width, units), f32)),
        ] + [(f"dsem{d}_{i}", dma) for i in range(4)]
    for k in range(iters + 2):
        plan += [
            (f"stile{k}", pltpu.VMEM((8, 128), f32)),
            (f"srecv{k}", pltpu.VMEM((n_pa, 8, 128), f32)),
        ] + [(f"ssem{k}_{i}", dma) for i in range(2)]
    plan += [
        ("ltile", pltpu.VMEM((8, 128), f32)),
        ("lrecv", pltpu.VMEM((n_dp, 8, 128), f32)),
        ("lsem0", dma),
        ("lsem1", dma),
        ("ktile", pltpu.VMEM((8, 128), f32)),
        ("krecv", pltpu.VMEM((n_dp, 8, 128), f32)),
        ("ksem0", dma),
        ("ksem1", dma),
    ]
    return plan


def _mega_kernel(names, n_dp, n_pa, iters, batch, *refs):
    (feat, wh, whtb, whtf, bmT, actT, adv, ivT, step_out, kl_out) = refs[:10]
    s = dict(zip(names, refs[10:]))
    rows, width = feat.shape
    units = wh.shape[1]
    groups = n_pa // (ACT_PAD // HEAD_ROWS)
    lanes = rows // groups
    cdp = width // n_dp
    md = lax.axis_index("dp")
    mp = lax.axis_index("param")
    dpeers = [lax.rem(md + j, n_dp) for j in range(1, n_dp)]
    ppeers = [lax.rem(mp + j, n_pa) for j in range(1, n_pa)]

    barrier = pltpu.get_barrier_semaphore()
    for p in dpeers:
        pl.semaphore_signal(barrier, inc=1, device_id=_device("dp", p), device_id_type=MESH)
    for p in ppeers:
        pl.semaphore_signal(barrier, inc=1, device_id=_device("param", p), device_id_type=MESH)

    def wait_all(buf, count, send_sem, recv_sem, axis):
        cp = pltpu.make_async_remote_copy(
            src_ref=buf.at[pl.ds(0, count)],
            dst_ref=buf.at[pl.ds(0, count)],
            send_sem=send_sem,
            recv_sem=recv_sem,
            device_id=_device(axis, lax.axis_index(axis)),
            device_id_type=MESH,
        )
        cp.wait_send()
        cp.wait_recv()

    def send(src, dst, send_sem, recv_sem, axis, peer):
        pltpu.make_async_remote_copy(
            src_ref=src, dst_ref=dst, send_sem=send_sem, recv_sem=recv_sem,
            device_id=_device(axis, peer), device_id_type=MESH,
        ).start()

    def hchunk(buf, k):
        r0 = pl.multiple_of((k // groups) * HEAD_ROWS, 8)
        l0 = pl.multiple_of(lax.rem(k, groups) * lanes, 128)
        return buf.at[pl.ds(r0, HEAD_ROWS), pl.ds(l0, lanes)]

    def head_allreduce(h, extra=None):
        loc, recv, gat = s[f"hloc{h}"], s[f"hrecv{h}"], s[f"hgat{h}"]
        sa, ra, sb, rb = (s[f"hsem{h}_{i}"] for i in range(4))
        if extra is not None:
            tile, erecv = s[f"stile{extra}"], s[f"srecv{extra}"]
            es, er = s[f"ssem{extra}_0"], s[f"ssem{extra}_1"]
        wait_all(recv, n_pa - 1, sa, ra, "param")
        recv[mp] = hchunk(loc, mp)[...]
        acc = recv[0]
        for i in range(1, n_pa):
            acc = acc + recv[i]
        hchunk(gat, mp)[...] = acc
        for p in ppeers:
            send(hchunk(gat, mp), hchunk(gat, mp), sb, rb, "param", p)
        total = None
        if extra is not None:
            wait_all(erecv, n_pa - 1, es, er, "param")
            erecv[mp] = tile[...]
            total = erecv[0]
            for i in range(1, n_pa):
                total = total + erecv[i]
        wait_all(recv, n_pa - 1, sb, rb, "param")
        return total

    def dp_allreduce(d):
        recv, gat = s[f"drecv{d}"], s[f"dgat{d}"]
        sa, ra, sb, rb = (s[f"dsem{d}_{i}"] for i in range(4))
        part = s["part"]
        wait_all(recv, n_dp - 1, sa, ra, "dp")
        mine = pl.ds(pl.multiple_of(md * cdp, 8), cdp)
        recv[md] = part[mine]
        acc = recv[0]
        for i in range(1, n_dp):
            acc = acc + recv[i]
        gat[mine] = acc
        for p in dpeers:
            send(gat.at[mine], gat.at[mine], sb, rb, "dp", p)
        wait_all(recv, n_dp - 1, sb, rb, "dp")
        return gat

    def param_start(k, values):
        tile, recv = s[f"stile{k}"], s[f"srecv{k}"]
        ss, sr = s[f"ssem{k}_0"], s[f"ssem{k}_1"]
        row = lax.broadcasted_iota(jnp.int32, (8, 128), 0)
        t = jnp.zeros((8, 128), jnp.float32)
        for i, v in enumerate(values):
            t = jnp.where(row == i, jnp.broadcast_to(v, (8, 128)), t)
        tile[...] = t
        for p in ppeers:
            send(tile, recv.at[mp], ss, sr, "param", p)

    def param_finish(k, count):
        tile, recv = s[f"stile{k}"], s[f"srecv{k}"]
        ss, sr = s[f"ssem{k}_0"], s[f"ssem{k}_1"]
        wait_all(recv, n_pa - 1, ss, sr, "param")
        recv[mp] = tile[...]
        total = recv[0]
        for i in range(1, n_pa):
            total = total + recv[i]
        return [total[i:i + 1, 0:1] for i in range(count)]

    def param_round(k, values):
        param_start(k, values)
        return param_finish(k, len(values))

    def expand_head(vec_b, out, make_vals, h, extra=None, entry=False):
        loc, recv = s[f"hloc{h}"], s[f"hrecv{h}"]
        sa, ra = s[f"hsem{h}_0"], s[f"hsem{h}_1"]
        if extra is not None:
            tile, erecv = s[f"stile{extra}"], s[f"srecv{extra}"]
            es, er = s[f"ssem{extra}_0"], s[f"ssem{extra}_1"]
            for p in ppeers:
                send(tile, erecv.at[mp], es, er, "param", p)
        blk = max(lanes, 256)
        for b in range(rows // blk):
            r0 = b * blk
            out[pl.ds(r0, blk), :] = jnp.dot(feat[pl.ds(r0, blk), :], vec_b[...], preferred_element_type=jnp.float32)
            vals = make_vals(r0, blk)
            loc[:, pl.ds(r0, blk)] = lax.dot_general(
                whtb[...], vals, (((1,), (1,)), ((), ())), preferred_element_type=jnp.float32
            )
            if entry:
                continue
            for lg in range(r0 // lanes, (r0 + blk) // lanes):
                for rg in range(ACT_PAD // HEAD_ROWS):
                    k = rg * groups + lg

                    @pl.when(mp != k)
                    def _():
                        send(hchunk(loc, k), recv.at[mp], sa, ra, "param", k)
        if entry:
            pl.semaphore_wait(barrier, len(dpeers) + len(ppeers))
            for p in ppeers:
                send(hchunk(loc, p), recv.at[mp], sa, ra, "param", p)

    def rowsum(g, d=None):
        part = s["part"]
        blk = max(cdp, min(256, width))
        for b in range(width // blk):
            c0 = b * blk
            part[pl.ds(c0, blk), :] = jnp.dot(
                s["featT"][pl.ds(c0, blk), :], g[...], preferred_element_type=jnp.float32
            )
            if d is None:
                continue
            recv, sa, ra = s[f"drecv{d}"], s[f"dsem{d}_0"], s[f"dsem{d}_1"]
            for k in range(c0 // cdp, (c0 + blk) // cdp):

                @pl.when(md != k)
                def _():
                    send(part.at[pl.ds(k * cdp, cdp)], recv.at[md], sa, ra, "dp", k)

    def pull(momentT):
        gb = s["gb"]
        prod = lax.dot_general(momentT, whtf[...], (((0,), (0,)), ((), ())), precision=HIGHEST,
                               preferred_element_type=jnp.float32)
        gb[...] = (prod * s["slope"][...] / batch).astype(jnp.bfloat16)
        return gb

    def hidden_vals(r0, blk):
        pre = s["pre"][pl.ds(r0, blk), :]
        hidden = jnp.tanh(pre)
        s["hid"][pl.ds(r0, blk), :] = hidden
        s["slope"][pl.ds(r0, blk), :] = 1.0 - hidden * hidden
        return hidden.astype(jnp.bfloat16)

    def change_vals(r0, blk):
        return (s["chg"][pl.ds(r0, blk), :] * s["slope"][pl.ds(r0, blk), :]).astype(jnp.bfloat16)

    def shift_vals(r0, blk):
        moved = jnp.tanh(s["pre"][pl.ds(r0, blk), :] + s["chg"][pl.ds(r0, blk), :])
        return (moved - s["hid"][pl.ds(r0, blk), :]).astype(jnp.bfloat16)

    tblk = min(256, width)
    for c in range(width // tblk):
        s["featT"][pl.ds(c * tblk, tblk), :] = feat[:, pl.ds(c * tblk, tblk)].T
    expand_head(wh, s["pre"], hidden_vals, 0, entry=True)
    head_allreduce(0)
    meanT = bmT[...] + s["hgat0"][...]
    deltaT = adv[...] * (actT[...] - meanT) * ivT[...]
    rowsum(pull(deltaT), 0)
    grad = dp_allreduce(0)[...]
    s["grad"][...] = grad
    s["r"][...] = grad
    s["p"][...] = grad
    s["x"][...] = jnp.zeros_like(grad)
    s["pb"][...] = grad.astype(jnp.bfloat16)
    s["stile0"][...] = jnp.broadcast_to(_tile_sum(grad * grad), (8, 128))
    rr = None
    for t in range(iters):
        expand_head(s["pb"], s["chg"], change_vals, t + 1, extra=0 if t == 0 else None)
        total = head_allreduce(t + 1, extra=0 if t == 0 else None)
        if t == 0:
            rr = total[0:1, 0:1]
        rowsum(pull(s[f"hgat{t + 1}"][...] * ivT[...]), t + 1 if t + 1 < iters else None)
        direction = s["p"][...]
        resid = s["r"][...]
        if t + 1 == iters:
            part = s["part"][...]
            sol = s["x"][...]
            row = lax.broadcasted_iota(jnp.int32, (8, 128), 0)
            lt = jnp.where(row == 0, jnp.broadcast_to(_tile_sum(direction * part), (8, 128)),
                           jnp.broadcast_to(_tile_sum(sol * part), (8, 128)))
            s["ltile"][...] = lt
            for p in dpeers:
                send(s["ltile"], s["lrecv"].at[md], s["lsem0"], s["lsem1"], "dp", p)
            wait_all(s["lrecv"], n_dp - 1, s["lsem0"], s["lsem1"], "dp")
            s["lrecv"][md] = s["ltile"][...]
            lsum = s["lrecv"][0]
            for i in range(1, n_dp):
                lsum = lsum + s["lrecv"][i]
            gap = s["grad"][...] - resid
            param_start(t + 1, [
                lsum[0:1, 0:1] + DAMPING * _tile_sum(direction * direction),
                _tile_sum(sol * gap),
                lsum[1:2, 0:1] + DAMPING * _tile_sum(sol * direction),
                _tile_sum(direction * gap),
            ])
            curv, x_gap, x_img, p_gap = param_finish(t + 1, 4)
            alpha = rr / curv
            x_new = sol + alpha * direction
            shs = x_gap + alpha * (x_img + p_gap) + alpha * alpha * curv
            s["x"][...] = x_new
            blk = step_out.shape[0]
            step_out[...] = s["x"][pl.ds(pl.multiple_of(md * blk, 8), blk)] * jnp.sqrt(D * UNITS / shs)
            reach = jnp.sqrt(2.0 * TRIAL_KL / shs)
            s["pb"][...] = (reach * x_new).astype(jnp.bfloat16)
            continue
        image = dp_allreduce(t + 1)[...] + DAMPING * direction
        if t + 1 < iters:
            curv, r_img, img_img = param_round(
                t + 1, [_tile_sum(direction * image), _tile_sum(resid * image), _tile_sum(image * image)]
            )
            alpha = rr / curv
            s["x"][...] = s["x"][...] + alpha * direction
            r_new = resid - alpha * image
            s["r"][...] = r_new
            rr_next = rr - 2.0 * alpha * r_img + alpha * alpha * img_img
            p_new = r_new + rr_next / rr * direction
            s["p"][...] = p_new
            s["pb"][...] = p_new.astype(jnp.bfloat16)
            rr = rr_next
    last = iters + 1
    expand_head(s["pb"], s["chg"], shift_vals, last)
    loc, recv = s[f"hloc{last}"], s[f"hrecv{last}"]
    wait_all(recv, n_pa - 1, s[f"hsem{last}_0"], s[f"hsem{last}_1"], "param")
    recv[mp] = hchunk(loc, mp)[...]
    acc = recv[0]
    for i in range(1, n_pa):
        acc = acc + recv[i]
    (kpart,) = param_round(iters + 1, [_tile_sum(acc * acc * hchunk(ivT, mp)[...])])
    ktile, krecv = s["ktile"], s["krecv"]
    ktile[...] = jnp.broadcast_to(kpart, (8, 128))
    for p in dpeers:
        send(ktile, krecv.at[md], s["ksem0"], s["ksem1"], "dp", p)
    wait_all(krecv, n_dp - 1, s["ksem0"], s["ksem1"], "dp")
    krecv[md] = ktile[...]
    ktot = krecv[0]
    for i in range(1, n_dp):
        ktot = ktot + krecv[i]
    kl_out[...] = ktot / (2.0 * batch) / TRIAL_KL


def shards(features, w_hidden, w_head, base_mean, actions, advantages, log_std):
    rows, width = features.shape
    units = w_hidden.shape[1]
    act = w_head.shape[1]
    dp_count = lax.axis_size("dp")
    param_count = lax.axis_size("param")
    batch = rows * dp_count
    inv_var = jnp.exp(-2.0 * log_std)
    padT = lambda a: jnp.pad(a.T, ((0, ACT_PAD - act), (0, 0)))
    whtb = padT(w_head)
    whtf = whtb.astype(jnp.float32)
    bmT = padT(base_mean)
    actT = padT(actions)
    ivT = jnp.pad(jnp.broadcast_to(inv_var[:, None], (act, rows)), ((0, ACT_PAD - act), (0, 0)))
    adv = advantages.reshape(1, rows)
    plan = _scratch_plan(dp_count, param_count, rows, width, units, ITERS)
    names = [name for name, _ in plan]
    vspec = pl.BlockSpec(memory_space=pltpu.VMEM)
    block = width // dp_count
    step_unit, kl_tile = pl.pallas_call(
        functools.partial(_mega_kernel, names, dp_count, param_count, ITERS, batch),
        out_shape=(jax.ShapeDtypeStruct((block, units), jnp.float32), jax.ShapeDtypeStruct((8, 128), jnp.float32)),
        in_specs=[vspec] * 8,
        out_specs=(vspec, vspec),
        scratch_shapes=[spec for _, spec in plan],
        compiler_params=pltpu.CompilerParams(collective_id=0, has_side_effects=True, vmem_limit_bytes=60 * 1024 * 1024),
        name="trust_region_step",
    )(features, w_hidden, whtb, whtf, bmT, actT, adv, ivT)
    return (step_unit, kl_tile[0, 0])


def solution(mesh):
    return jax.shard_map(
        shards,
        mesh=mesh,
        in_specs=(
            P("dp", None),
            P(None, "param"),
            P("param", None),
            P("dp", None),
            P("dp", None),
            P("dp"),
            P(),
        ),
        out_specs=(P("dp", "param"), P()),
        check_vma=False,
    )
```

```python
import functools

import jax
import jax.numpy as jnp
from jax import lax
from jax.experimental import pallas as pl
from jax.experimental.pallas import tpu as pltpu
from jax.sharding import PartitionSpec as P

D = 2048
UNITS = 2048
ITERS = 2


DAMPING = 0.01
TRIAL_KL = 4.0

MESH = pl.DeviceIdType.MESH
AXES = ("dp", "param")
ACT_PAD = 48
HEAD_ROWS = 24
HIGHEST = lax.Precision.HIGHEST


def _device(axis, partner):
    return tuple(partner if name == axis else lax.axis_index(name) for name in AXES)


def _tile_sum(x):
    return jnp.sum(jnp.sum(x, axis=0, keepdims=True), axis=1, keepdims=True)


def _scratch_plan(n_dp, n_pa, rows, width, units, iters):
    f32, bf16 = jnp.float32, jnp.bfloat16
    groups = n_pa // (ACT_PAD // HEAD_ROWS)
    lanes = rows // groups
    dma = pltpu.SemaphoreType.DMA(())
    plan = [
        ("pre", pltpu.VMEM((rows, units), f32)),
        ("hid", pltpu.VMEM((rows, units), f32)),
        ("slope", pltpu.VMEM((rows, units), f32)),
        ("gb", pltpu.VMEM((rows, units), bf16)),
        ("chg", pltpu.VMEM((rows, units), f32)),
        ("part", pltpu.VMEM((width, units), f32)),
        ("featT", pltpu.VMEM((width, rows), bf16)),
        ("grad", pltpu.VMEM((width, units), f32)),
        ("x", pltpu.VMEM((width, units), f32)),
        ("r", pltpu.VMEM((width, units), f32)),
        ("p", pltpu.VMEM((width, units), f32)),
        ("pb", pltpu.VMEM((width, units), bf16)),
    ]
    for h in range(iters + 2):
        plan += [
            (f"hloc{h}", pltpu.VMEM((ACT_PAD, rows), f32)),
            (f"hrecv{h}", pltpu.VMEM((n_pa, HEAD_ROWS, lanes), f32)),
            (f"hgat{h}", pltpu.VMEM((ACT_PAD, rows), f32)),
        ] + [(f"hsem{h}_{i}", dma) for i in range(4)]
    for d in range(iters):
        plan += [
            (f"drecv{d}", pltpu.VMEM((n_dp, width // n_dp, units), f32)),
            (f"dgat{d}", pltpu.VMEM((width, units), f32)),
        ] + [(f"dsem{d}_{i}", dma) for i in range(4)]
    for k in range(iters + 2):
        plan += [
            (f"stile{k}", pltpu.VMEM((8, 128), f32)),
            (f"srecv{k}", pltpu.VMEM((n_pa, 8, 128), f32)),
        ] + [(f"ssem{k}_{i}", dma) for i in range(2)]
    plan += [
        ("ltile", pltpu.VMEM((8, 128), f32)),
        ("lrecv", pltpu.VMEM((n_dp, 8, 128), f32)),
        ("lsem0", dma),
        ("lsem1", dma),
        ("ktile", pltpu.VMEM((8, 128), f32)),
        ("krecv", pltpu.VMEM((n_dp, 8, 128), f32)),
        ("ksem0", dma),
        ("ksem1", dma),
    ]
    return plan


def _mega_kernel(names, n_dp, n_pa, iters, batch, *refs):
    (feat, wh, whtb, whtf, bmT, actT, adv, ivT, step_out, kl_out) = refs[:10]
    s = dict(zip(names, refs[10:]))
    rows, width = feat.shape
    units = wh.shape[1]
    groups = n_pa // (ACT_PAD // HEAD_ROWS)
    lanes = rows // groups
    cdp = width // n_dp
    md = lax.axis_index("dp")
    mp = lax.axis_index("param")
    order = lambda n: sorted(range(1, n), key=lambda j: (min(j, n - j), j))
    dpeers = [lax.rem(md + j, n_dp) for j in order(n_dp)]
    ppeers = [lax.rem(mp + j, n_pa) for j in order(n_pa)]

    barrier = pltpu.get_barrier_semaphore()
    for p in dpeers:
        pl.semaphore_signal(barrier, inc=1, device_id=_device("dp", p), device_id_type=MESH)
    for p in ppeers:
        pl.semaphore_signal(barrier, inc=1, device_id=_device("param", p), device_id_type=MESH)

    def wait_all(buf, count, send_sem, recv_sem, axis):
        cp = pltpu.make_async_remote_copy(
            src_ref=buf.at[pl.ds(0, count)],
            dst_ref=buf.at[pl.ds(0, count)],
            send_sem=send_sem,
            recv_sem=recv_sem,
            device_id=_device(axis, lax.axis_index(axis)),
            device_id_type=MESH,
        )
        cp.wait_send()
        cp.wait_recv()

    def send(src, dst, send_sem, recv_sem, axis, peer):
        pltpu.make_async_remote_copy(
            src_ref=src, dst_ref=dst, send_sem=send_sem, recv_sem=recv_sem,
            device_id=_device(axis, peer), device_id_type=MESH,
        ).start()

    def hchunk(buf, k):
        r0 = pl.multiple_of((k // groups) * HEAD_ROWS, 8)
        l0 = pl.multiple_of(lax.rem(k, groups) * lanes, 128)
        return buf.at[pl.ds(r0, HEAD_ROWS), pl.ds(l0, lanes)]

    def head_allreduce(h, extra=None):
        loc, recv, gat = s[f"hloc{h}"], s[f"hrecv{h}"], s[f"hgat{h}"]
        sa, ra, sb, rb = (s[f"hsem{h}_{i}"] for i in range(4))
        if extra is not None:
            tile, erecv = s[f"stile{extra}"], s[f"srecv{extra}"]
            es, er = s[f"ssem{extra}_0"], s[f"ssem{extra}_1"]
        wait_all(recv, n_pa - 1, sa, ra, "param")
        recv[mp] = hchunk(loc, mp)[...]
        acc = recv[0]
        for i in range(1, n_pa):
            acc = acc + recv[i]
        hchunk(gat, mp)[...] = acc
        for p in ppeers:
            send(hchunk(gat, mp), hchunk(gat, mp), sb, rb, "param", p)
        total = None
        if extra is not None:
            wait_all(erecv, n_pa - 1, es, er, "param")
            erecv[mp] = tile[...]
            total = erecv[0]
            for i in range(1, n_pa):
                total = total + erecv[i]
        wait_all(recv, n_pa - 1, sb, rb, "param")
        return total

    def dp_allreduce(d):
        recv, gat = s[f"drecv{d}"], s[f"dgat{d}"]
        sa, ra, sb, rb = (s[f"dsem{d}_{i}"] for i in range(4))
        part = s["part"]
        wait_all(recv, n_dp - 1, sa, ra, "dp")
        mine = pl.ds(pl.multiple_of(md * cdp, 8), cdp)
        recv[md] = part[mine]
        acc = recv[0]
        for i in range(1, n_dp):
            acc = acc + recv[i]
        gat[mine] = acc
        for p in dpeers:
            send(gat.at[mine], gat.at[mine], sb, rb, "dp", p)
        wait_all(recv, n_dp - 1, sb, rb, "dp")
        return gat

    def param_start(k, values):
        tile, recv = s[f"stile{k}"], s[f"srecv{k}"]
        ss, sr = s[f"ssem{k}_0"], s[f"ssem{k}_1"]
        row = lax.broadcasted_iota(jnp.int32, (8, 128), 0)
        t = jnp.zeros((8, 128), jnp.float32)
        for i, v in enumerate(values):
            t = jnp.where(row == i, jnp.broadcast_to(v, (8, 128)), t)
        tile[...] = t
        for p in ppeers:
            send(tile, recv.at[mp], ss, sr, "param", p)

    def param_finish(k, count):
        tile, recv = s[f"stile{k}"], s[f"srecv{k}"]
        ss, sr = s[f"ssem{k}_0"], s[f"ssem{k}_1"]
        wait_all(recv, n_pa - 1, ss, sr, "param")
        recv[mp] = tile[...]
        total = recv[0]
        for i in range(1, n_pa):
            total = total + recv[i]
        return [total[i:i + 1, 0:1] for i in range(count)]

    def param_round(k, values):
        param_start(k, values)
        return param_finish(k, len(values))

    def expand_head(vec_b, out, make_vals, h, extra=None, entry=False):
        loc, recv = s[f"hloc{h}"], s[f"hrecv{h}"]
        sa, ra = s[f"hsem{h}_0"], s[f"hsem{h}_1"]
        if extra is not None:
            tile, erecv = s[f"stile{extra}"], s[f"srecv{extra}"]
            es, er = s[f"ssem{extra}_0"], s[f"ssem{extra}_1"]
            for p in ppeers:
                send(tile, erecv.at[mp], es, er, "param", p)
        blk = max(lanes, 256)
        for b in range(rows // blk):
            r0 = b * blk
            out[pl.ds(r0, blk), :] = jnp.dot(feat[pl.ds(r0, blk), :], vec_b[...], preferred_element_type=jnp.float32)
            vals = make_vals(r0, blk)
            loc[:, pl.ds(r0, blk)] = lax.dot_general(
                whtb[...], vals, (((1,), (1,)), ((), ())), preferred_element_type=jnp.float32
            )
            if entry:
                continue
            for lg in range(r0 // lanes, (r0 + blk) // lanes):
                for rg in range(ACT_PAD // HEAD_ROWS):
                    k = rg * groups + lg

                    @pl.when(mp != k)
                    def _():
                        send(hchunk(loc, k), recv.at[mp], sa, ra, "param", k)
        if entry:
            pl.semaphore_wait(barrier, len(dpeers) + len(ppeers))
            for p in ppeers:
                send(hchunk(loc, p), recv.at[mp], sa, ra, "param", p)

    def rowsum(g, d=None):
        part = s["part"]
        blk = max(cdp, min(256, width))
        for b in range(width // blk):
            c0 = b * blk
            part[pl.ds(c0, blk), :] = jnp.dot(
                s["featT"][pl.ds(c0, blk), :], g[...], preferred_element_type=jnp.float32
            )
            if d is None:
                continue
            recv, sa, ra = s[f"drecv{d}"], s[f"dsem{d}_0"], s[f"dsem{d}_1"]
            for k in range(c0 // cdp, (c0 + blk) // cdp):

                @pl.when(md != k)
                def _():
                    send(part.at[pl.ds(k * cdp, cdp)], recv.at[md], sa, ra, "dp", k)

    def pull(momentT):
        gb = s["gb"]
        prod = lax.dot_general(momentT, whtf[...], (((0,), (0,)), ((), ())), precision=HIGHEST,
                               preferred_element_type=jnp.float32)
        gb[...] = (prod * s["slope"][...] / batch).astype(jnp.bfloat16)
        return gb

    def hidden_vals(r0, blk):
        pre = s["pre"][pl.ds(r0, blk), :]
        hidden = jnp.tanh(pre)
        s["hid"][pl.ds(r0, blk), :] = hidden
        s["slope"][pl.ds(r0, blk), :] = 1.0 - hidden * hidden
        return hidden.astype(jnp.bfloat16)

    def change_vals(r0, blk):
        return (s["chg"][pl.ds(r0, blk), :] * s["slope"][pl.ds(r0, blk), :]).astype(jnp.bfloat16)

    def shift_vals(r0, blk):
        moved = jnp.tanh(s["pre"][pl.ds(r0, blk), :] + s["chg"][pl.ds(r0, blk), :])
        return (moved - s["hid"][pl.ds(r0, blk), :]).astype(jnp.bfloat16)

    tblk = min(256, width)
    for c in range(width // tblk):
        s["featT"][pl.ds(c * tblk, tblk), :] = feat[:, pl.ds(c * tblk, tblk)].T
    expand_head(wh, s["pre"], hidden_vals, 0, entry=True)
    head_allreduce(0)
    meanT = bmT[...] + s["hgat0"][...]
    deltaT = adv[...] * (actT[...] - meanT) * ivT[...]
    rowsum(pull(deltaT), 0)
    grad = dp_allreduce(0)[...]
    s["grad"][...] = grad
    s["r"][...] = grad
    s["p"][...] = grad
    s["x"][...] = jnp.zeros_like(grad)
    s["pb"][...] = grad.astype(jnp.bfloat16)
    s["stile0"][...] = jnp.broadcast_to(_tile_sum(grad * grad), (8, 128))
    rr = None
    for t in range(iters):
        expand_head(s["pb"], s["chg"], change_vals, t + 1, extra=0 if t == 0 else None)
        total = head_allreduce(t + 1, extra=0 if t == 0 else None)
        if t == 0:
            rr = total[0:1, 0:1]
        rowsum(pull(s[f"hgat{t + 1}"][...] * ivT[...]), t + 1 if t + 1 < iters else None)
        direction = s["p"][...]
        resid = s["r"][...]
        if t + 1 == iters:
            part = s["part"][...]
            sol = s["x"][...]
            row = lax.broadcasted_iota(jnp.int32, (8, 128), 0)
            lt = jnp.where(row == 0, jnp.broadcast_to(_tile_sum(direction * part), (8, 128)),
                           jnp.broadcast_to(_tile_sum(sol * part), (8, 128)))
            s["ltile"][...] = lt
            for p in dpeers:
                send(s["ltile"], s["lrecv"].at[md], s["lsem0"], s["lsem1"], "dp", p)
            wait_all(s["lrecv"], n_dp - 1, s["lsem0"], s["lsem1"], "dp")
            s["lrecv"][md] = s["ltile"][...]
            lsum = s["lrecv"][0]
            for i in range(1, n_dp):
                lsum = lsum + s["lrecv"][i]
            gap = s["grad"][...] - resid
            param_start(t + 1, [
                lsum[0:1, 0:1] + DAMPING * _tile_sum(direction * direction),
                _tile_sum(sol * gap),
                lsum[1:2, 0:1] + DAMPING * _tile_sum(sol * direction),
                _tile_sum(direction * gap),
            ])
            curv, x_gap, x_img, p_gap = param_finish(t + 1, 4)
            alpha = rr / curv
            x_new = sol + alpha * direction
            shs = x_gap + alpha * (x_img + p_gap) + alpha * alpha * curv
            s["x"][...] = x_new
            blk = step_out.shape[0]
            step_out[...] = s["x"][pl.ds(pl.multiple_of(md * blk, 8), blk)] * jnp.sqrt(D * UNITS / shs)
            reach = jnp.sqrt(2.0 * TRIAL_KL / shs)
            s["pb"][...] = (reach * x_new).astype(jnp.bfloat16)
            continue
        image = dp_allreduce(t + 1)[...] + DAMPING * direction
        if t + 1 < iters:
            curv, r_img, img_img = param_round(
                t + 1, [_tile_sum(direction * image), _tile_sum(resid * image), _tile_sum(image * image)]
            )
            alpha = rr / curv
            s["x"][...] = s["x"][...] + alpha * direction
            r_new = resid - alpha * image
            s["r"][...] = r_new
            rr_next = rr - 2.0 * alpha * r_img + alpha * alpha * img_img
            p_new = r_new + rr_next / rr * direction
            s["p"][...] = p_new
            s["pb"][...] = p_new.astype(jnp.bfloat16)
            rr = rr_next
    last = iters + 1
    expand_head(s["pb"], s["chg"], shift_vals, last)
    loc, recv = s[f"hloc{last}"], s[f"hrecv{last}"]
    wait_all(recv, n_pa - 1, s[f"hsem{last}_0"], s[f"hsem{last}_1"], "param")
    recv[mp] = hchunk(loc, mp)[...]
    acc = recv[0]
    for i in range(1, n_pa):
        acc = acc + recv[i]
    (kpart,) = param_round(iters + 1, [_tile_sum(acc * acc * hchunk(ivT, mp)[...])])
    ktile, krecv = s["ktile"], s["krecv"]
    ktile[...] = jnp.broadcast_to(kpart, (8, 128))
    for p in dpeers:
        send(ktile, krecv.at[md], s["ksem0"], s["ksem1"], "dp", p)
    wait_all(krecv, n_dp - 1, s["ksem0"], s["ksem1"], "dp")
    krecv[md] = ktile[...]
    ktot = krecv[0]
    for i in range(1, n_dp):
        ktot = ktot + krecv[i]
    kl_out[...] = ktot / (2.0 * batch) / TRIAL_KL


def shards(features, w_hidden, w_head, base_mean, actions, advantages, log_std):
    rows, width = features.shape
    units = w_hidden.shape[1]
    act = w_head.shape[1]
    dp_count = lax.axis_size("dp")
    param_count = lax.axis_size("param")
    batch = rows * dp_count
    inv_var = jnp.exp(-2.0 * log_std)
    padT = lambda a: jnp.pad(a.T, ((0, ACT_PAD - act), (0, 0)))
    whtb = padT(w_head)
    whtf = whtb.astype(jnp.float32)
    bmT = padT(base_mean)
    actT = padT(actions)
    ivT = jnp.pad(jnp.broadcast_to(inv_var[:, None], (act, rows)), ((0, ACT_PAD - act), (0, 0)))
    adv = advantages.reshape(1, rows)
    plan = _scratch_plan(dp_count, param_count, rows, width, units, ITERS)
    names = [name for name, _ in plan]
    vspec = pl.BlockSpec(memory_space=pltpu.VMEM)
    block = width // dp_count
    step_unit, kl_tile = pl.pallas_call(
        functools.partial(_mega_kernel, names, dp_count, param_count, ITERS, batch),
        out_shape=(jax.ShapeDtypeStruct((block, units), jnp.float32), jax.ShapeDtypeStruct((8, 128), jnp.float32)),
        in_specs=[vspec] * 8,
        out_specs=(vspec, vspec),
        scratch_shapes=[spec for _, spec in plan],
        compiler_params=pltpu.CompilerParams(collective_id=0, has_side_effects=True, vmem_limit_bytes=60 * 1024 * 1024),
        name="trust_region_step",
    )(features, w_hidden, whtb, whtf, bmT, actT, adv, ivT)
    return (step_unit, kl_tile[0, 0])


def solution(mesh):
    return jax.shard_map(
        shards,
        mesh=mesh,
        in_specs=(
            P("dp", None),
            P(None, "param"),
            P("param", None),
            P("dp", None),
            P("dp", None),
            P("dp"),
            P(),
        ),
        out_specs=(P("dp", "param"), P()),
        check_vma=False,
    )
```

```python
import functools

import jax
import jax.numpy as jnp
from jax import lax
from jax.experimental import pallas as pl
from jax.experimental.pallas import tpu as pltpu
from jax.sharding import PartitionSpec as P

D = 2048
UNITS = 2048
ITERS = 2


DAMPING = 0.01
TRIAL_KL = 4.0

MESH = pl.DeviceIdType.MESH
AXES = ("dp", "param")
ACT_PAD = 48
HEAD_ROWS = 24
HIGHEST = lax.Precision.HIGHEST


def _device(axis, partner):
    return tuple(partner if name == axis else lax.axis_index(name) for name in AXES)


def _tile_sum(x):
    return jnp.sum(jnp.sum(x, axis=0, keepdims=True), axis=1, keepdims=True)


def _scratch_plan(n_dp, n_pa, rows, width, units, iters):
    f32, bf16 = jnp.float32, jnp.bfloat16
    groups = n_pa // (ACT_PAD // HEAD_ROWS)
    lanes = rows // groups
    dma = pltpu.SemaphoreType.DMA(())
    plan = [
        ("pre", pltpu.VMEM((rows, units), f32)),
        ("hid", pltpu.VMEM((rows, units), f32)),
        ("slope", pltpu.VMEM((rows, units), f32)),
        ("gb", pltpu.VMEM((rows, units), bf16)),
        ("chg", pltpu.VMEM((rows, units), f32)),
        ("part", pltpu.VMEM((width, units), f32)),
        ("featT", pltpu.VMEM((width, rows), bf16)),
        ("grad", pltpu.VMEM((width, units), f32)),
        ("x", pltpu.VMEM((width, units), f32)),
        ("r", pltpu.VMEM((width, units), f32)),
        ("p", pltpu.VMEM((width, units), f32)),
        ("pb", pltpu.VMEM((width, units), bf16)),
    ]
    for h in range(iters + 2):
        plan += [
            (f"hloc{h}", pltpu.VMEM((ACT_PAD, rows), f32)),
            (f"hrecv{h}", pltpu.VMEM((n_pa, HEAD_ROWS, lanes), f32)),
            (f"hgat{h}", pltpu.VMEM((ACT_PAD, rows), f32)),
        ] + [(f"hsem{h}_{i}", dma) for i in range(4)]
    for d in range(iters):
        plan += [
            (f"drecv{d}", pltpu.VMEM((n_dp, width // n_dp, units), f32)),
            (f"dgat{d}", pltpu.VMEM((width, units), f32)),
        ] + [(f"dsem{d}_{i}", dma) for i in range(4)]
    for k in range(iters + 2):
        plan += [
            (f"stile{k}", pltpu.VMEM((8, 128), f32)),
            (f"srecv{k}", pltpu.VMEM((n_pa, 8, 128), f32)),
        ] + [(f"ssem{k}_{i}", dma) for i in range(2)]
    plan += [
        ("ltile", pltpu.VMEM((8, 128), f32)),
        ("lrecv", pltpu.VMEM((n_dp, 8, 128), f32)),
        ("lsem0", dma),
        ("lsem1", dma),
        ("ktile", pltpu.VMEM((8, 128), f32)),
        ("krecv", pltpu.VMEM((n_dp, 8, 128), f32)),
        ("ksem0", dma),
        ("ksem1", dma),
    ]
    return plan


def _mega_kernel(names, n_dp, n_pa, iters, batch, *refs):
    (feat, wh, whtb, whtf, bmT, actT, adv, ivT, step_out, kl_out) = refs[:10]
    s = dict(zip(names, refs[10:]))
    rows, width = feat.shape
    units = wh.shape[1]
    groups = n_pa // (ACT_PAD // HEAD_ROWS)
    lanes = rows // groups
    cdp = width // n_dp
    md = lax.axis_index("dp")
    mp = lax.axis_index("param")
    order = lambda n: sorted(range(1, n), key=lambda j: (min(j, n - j), j))
    dpeers = [lax.rem(md + j, n_dp) for j in order(n_dp)]
    ppeers = [lax.rem(mp + j, n_pa) for j in order(n_pa)]

    barrier = pltpu.get_barrier_semaphore()
    for p in dpeers:
        pl.semaphore_signal(barrier, inc=1, device_id=_device("dp", p), device_id_type=MESH)
    for p in ppeers:
        pl.semaphore_signal(barrier, inc=1, device_id=_device("param", p), device_id_type=MESH)

    def wait_all(buf, count, send_sem, recv_sem, axis):
        cp = pltpu.make_async_remote_copy(
            src_ref=buf.at[pl.ds(0, count)],
            dst_ref=buf.at[pl.ds(0, count)],
            send_sem=send_sem,
            recv_sem=recv_sem,
            device_id=_device(axis, lax.axis_index(axis)),
            device_id_type=MESH,
        )
        cp.wait_send()
        cp.wait_recv()

    def send(src, dst, send_sem, recv_sem, axis, peer):
        pltpu.make_async_remote_copy(
            src_ref=src, dst_ref=dst, send_sem=send_sem, recv_sem=recv_sem,
            device_id=_device(axis, peer), device_id_type=MESH,
        ).start()

    def hchunk(buf, k):
        r0 = pl.multiple_of((k // groups) * HEAD_ROWS, 8)
        l0 = pl.multiple_of(lax.rem(k, groups) * lanes, 128)
        return buf.at[pl.ds(r0, HEAD_ROWS), pl.ds(l0, lanes)]

    def head_allreduce(h, extra=None):
        loc, recv, gat = s[f"hloc{h}"], s[f"hrecv{h}"], s[f"hgat{h}"]
        sa, ra, sb, rb = (s[f"hsem{h}_{i}"] for i in range(4))
        if extra is not None:
            tile, erecv = s[f"stile{extra}"], s[f"srecv{extra}"]
            es, er = s[f"ssem{extra}_0"], s[f"ssem{extra}_1"]
        wait_all(recv, n_pa - 1, sa, ra, "param")
        recv[mp] = hchunk(loc, mp)[...]
        acc = recv[0]
        for i in range(1, n_pa):
            acc = acc + recv[i]
        hchunk(gat, mp)[...] = acc
        for p in ppeers:
            send(hchunk(gat, mp), hchunk(gat, mp), sb, rb, "param", p)
        total = None
        if extra is not None:
            wait_all(erecv, n_pa - 1, es, er, "param")
            erecv[mp] = tile[...]
            total = erecv[0]
            for i in range(1, n_pa):
                total = total + erecv[i]
        wait_all(recv, n_pa - 1, sb, rb, "param")
        return total

    def dp_allreduce(d):
        recv, gat = s[f"drecv{d}"], s[f"dgat{d}"]
        sa, ra, sb, rb = (s[f"dsem{d}_{i}"] for i in range(4))
        part = s["part"]
        wait_all(recv, n_dp - 1, sa, ra, "dp")
        mine = pl.ds(pl.multiple_of(md * cdp, 8), cdp)
        recv[md] = part[mine]
        acc = recv[0]
        for i in range(1, n_dp):
            acc = acc + recv[i]
        gat[mine] = acc
        for p in dpeers:
            send(gat.at[mine], gat.at[mine], sb, rb, "dp", p)
        wait_all(recv, n_dp - 1, sb, rb, "dp")
        return gat

    def param_start(k, values):
        tile, recv = s[f"stile{k}"], s[f"srecv{k}"]
        ss, sr = s[f"ssem{k}_0"], s[f"ssem{k}_1"]
        row = lax.broadcasted_iota(jnp.int32, (8, 128), 0)
        t = jnp.zeros((8, 128), jnp.float32)
        for i, v in enumerate(values):
            t = jnp.where(row == i, jnp.broadcast_to(v, (8, 128)), t)
        tile[...] = t
        for p in ppeers:
            send(tile, recv.at[mp], ss, sr, "param", p)

    def param_finish(k, count):
        tile, recv = s[f"stile{k}"], s[f"srecv{k}"]
        ss, sr = s[f"ssem{k}_0"], s[f"ssem{k}_1"]
        wait_all(recv, n_pa - 1, ss, sr, "param")
        recv[mp] = tile[...]
        total = recv[0]
        for i in range(1, n_pa):
            total = total + recv[i]
        return [total[i:i + 1, 0:1] for i in range(count)]

    def param_round(k, values):
        param_start(k, values)
        return param_finish(k, len(values))

    def expand_head(vec_b, out, make_vals, h, extra=None, entry=False):
        loc, recv = s[f"hloc{h}"], s[f"hrecv{h}"]
        sa, ra = s[f"hsem{h}_0"], s[f"hsem{h}_1"]
        if extra is not None:
            tile, erecv = s[f"stile{extra}"], s[f"srecv{extra}"]
            es, er = s[f"ssem{extra}_0"], s[f"ssem{extra}_1"]
            for p in ppeers:
                send(tile, erecv.at[mp], es, er, "param", p)
        blk = max(lanes, 256)
        nb = rows // blk
        per = blk // lanes
        for b in range(nb):
            bb = lax.rem(b + lax.rem(mp, groups) // per + 1, nb)
            r0 = pl.multiple_of(bb * blk, blk)
            out[pl.ds(r0, blk), :] = jnp.dot(feat[pl.ds(r0, blk), :], vec_b[...], preferred_element_type=jnp.float32)
            vals = make_vals(r0, blk)
            loc[:, pl.ds(r0, blk)] = lax.dot_general(
                whtb[...], vals, (((1,), (1,)), ((), ())), preferred_element_type=jnp.float32
            )
            if entry:
                continue
            for i in range(per):
                for rg in range(ACT_PAD // HEAD_ROWS):
                    k = rg * groups + bb * per + i

                    @pl.when(mp != k)
                    def _():
                        send(hchunk(loc, k), recv.at[mp], sa, ra, "param", k)
        if entry:
            pl.semaphore_wait(barrier, len(dpeers) + len(ppeers))
            for p in ppeers:
                send(hchunk(loc, p), recv.at[mp], sa, ra, "param", p)

    def rowsum(g, d=None):
        part = s["part"]
        blk = max(cdp, min(256, width))
        nb = width // blk
        per = blk // cdp
        for b in range(nb):
            bb = lax.rem(b + md // per + 1, nb)
            c0 = pl.multiple_of(bb * blk, blk)
            part[pl.ds(c0, blk), :] = jnp.dot(
                s["featT"][pl.ds(c0, blk), :], g[...], preferred_element_type=jnp.float32
            )
            if d is None:
                continue
            recv, sa, ra = s[f"drecv{d}"], s[f"dsem{d}_0"], s[f"dsem{d}_1"]
            for i in range(per):
                k = bb * per + i

                @pl.when(md != k)
                def _():
                    send(part.at[pl.ds(k * cdp, cdp)], recv.at[md], sa, ra, "dp", k)

    def pull(momentT):
        gb = s["gb"]
        prod = lax.dot_general(momentT, whtf[...], (((0,), (0,)), ((), ())), precision=HIGHEST,
                               preferred_element_type=jnp.float32)
        gb[...] = (prod * s["slope"][...] / batch).astype(jnp.bfloat16)
        return gb

    def hidden_vals(r0, blk):
        pre = s["pre"][pl.ds(r0, blk), :]
        hidden = jnp.tanh(pre)
        s["hid"][pl.ds(r0, blk), :] = hidden
        s["slope"][pl.ds(r0, blk), :] = 1.0 - hidden * hidden
        return hidden.astype(jnp.bfloat16)

    def change_vals(r0, blk):
        return (s["chg"][pl.ds(r0, blk), :] * s["slope"][pl.ds(r0, blk), :]).astype(jnp.bfloat16)

    def shift_vals(r0, blk):
        moved = jnp.tanh(s["pre"][pl.ds(r0, blk), :] + s["chg"][pl.ds(r0, blk), :])
        return (moved - s["hid"][pl.ds(r0, blk), :]).astype(jnp.bfloat16)

    tblk = min(256, width)
    for c in range(width // tblk):
        s["featT"][pl.ds(c * tblk, tblk), :] = feat[:, pl.ds(c * tblk, tblk)].T
    expand_head(wh, s["pre"], hidden_vals, 0, entry=True)
    head_allreduce(0)
    meanT = bmT[...] + s["hgat0"][...]
    deltaT = adv[...] * (actT[...] - meanT) * ivT[...]
    rowsum(pull(deltaT), 0)
    grad = dp_allreduce(0)[...]
    s["grad"][...] = grad
    s["r"][...] = grad
    s["p"][...] = grad
    s["x"][...] = jnp.zeros_like(grad)
    s["pb"][...] = grad.astype(jnp.bfloat16)
    s["stile0"][...] = jnp.broadcast_to(_tile_sum(grad * grad), (8, 128))
    rr = None
    for t in range(iters):
        expand_head(s["pb"], s["chg"], change_vals, t + 1, extra=0 if t == 0 else None)
        total = head_allreduce(t + 1, extra=0 if t == 0 else None)
        if t == 0:
            rr = total[0:1, 0:1]
        rowsum(pull(s[f"hgat{t + 1}"][...] * ivT[...]), t + 1 if t + 1 < iters else None)
        direction = s["p"][...]
        resid = s["r"][...]
        if t + 1 == iters:
            part = s["part"][...]
            sol = s["x"][...]
            row = lax.broadcasted_iota(jnp.int32, (8, 128), 0)
            lt = jnp.where(row == 0, jnp.broadcast_to(_tile_sum(direction * part), (8, 128)),
                           jnp.broadcast_to(_tile_sum(sol * part), (8, 128)))
            s["ltile"][...] = lt
            for p in dpeers:
                send(s["ltile"], s["lrecv"].at[md], s["lsem0"], s["lsem1"], "dp", p)
            wait_all(s["lrecv"], n_dp - 1, s["lsem0"], s["lsem1"], "dp")
            s["lrecv"][md] = s["ltile"][...]
            lsum = s["lrecv"][0]
            for i in range(1, n_dp):
                lsum = lsum + s["lrecv"][i]
            gap = s["grad"][...] - resid
            param_start(t + 1, [
                lsum[0:1, 0:1] + DAMPING * _tile_sum(direction * direction),
                _tile_sum(sol * gap),
                lsum[1:2, 0:1] + DAMPING * _tile_sum(sol * direction),
                _tile_sum(direction * gap),
            ])
            curv, x_gap, x_img, p_gap = param_finish(t + 1, 4)
            alpha = rr / curv
            x_new = sol + alpha * direction
            shs = x_gap + alpha * (x_img + p_gap) + alpha * alpha * curv
            s["x"][...] = x_new
            blk = step_out.shape[0]
            step_out[...] = s["x"][pl.ds(pl.multiple_of(md * blk, 8), blk)] * jnp.sqrt(D * UNITS / shs)
            reach = jnp.sqrt(2.0 * TRIAL_KL / shs)
            s["pb"][...] = (reach * x_new).astype(jnp.bfloat16)
            continue
        image = dp_allreduce(t + 1)[...] + DAMPING * direction
        if t + 1 < iters:
            curv, r_img, img_img = param_round(
                t + 1, [_tile_sum(direction * image), _tile_sum(resid * image), _tile_sum(image * image)]
            )
            alpha = rr / curv
            s["x"][...] = s["x"][...] + alpha * direction
            r_new = resid - alpha * image
            s["r"][...] = r_new
            rr_next = rr - 2.0 * alpha * r_img + alpha * alpha * img_img
            p_new = r_new + rr_next / rr * direction
            s["p"][...] = p_new
            s["pb"][...] = p_new.astype(jnp.bfloat16)
            rr = rr_next
    last = iters + 1
    expand_head(s["pb"], s["chg"], shift_vals, last)
    loc, recv = s[f"hloc{last}"], s[f"hrecv{last}"]
    wait_all(recv, n_pa - 1, s[f"hsem{last}_0"], s[f"hsem{last}_1"], "param")
    recv[mp] = hchunk(loc, mp)[...]
    acc = recv[0]
    for i in range(1, n_pa):
        acc = acc + recv[i]
    (kpart,) = param_round(iters + 1, [_tile_sum(acc * acc * hchunk(ivT, mp)[...])])
    ktile, krecv = s["ktile"], s["krecv"]
    ktile[...] = jnp.broadcast_to(kpart, (8, 128))
    for p in dpeers:
        send(ktile, krecv.at[md], s["ksem0"], s["ksem1"], "dp", p)
    wait_all(krecv, n_dp - 1, s["ksem0"], s["ksem1"], "dp")
    krecv[md] = ktile[...]
    ktot = krecv[0]
    for i in range(1, n_dp):
        ktot = ktot + krecv[i]
    kl_out[...] = ktot / (2.0 * batch) / TRIAL_KL


def shards(features, w_hidden, w_head, base_mean, actions, advantages, log_std):
    rows, width = features.shape
    units = w_hidden.shape[1]
    act = w_head.shape[1]
    dp_count = lax.axis_size("dp")
    param_count = lax.axis_size("param")
    batch = rows * dp_count
    inv_var = jnp.exp(-2.0 * log_std)
    padT = lambda a: jnp.pad(a.T, ((0, ACT_PAD - act), (0, 0)))
    whtb = padT(w_head)
    whtf = whtb.astype(jnp.float32)
    bmT = padT(base_mean)
    actT = padT(actions)
    ivT = jnp.pad(jnp.broadcast_to(inv_var[:, None], (act, rows)), ((0, ACT_PAD - act), (0, 0)))
    adv = advantages.reshape(1, rows)
    plan = _scratch_plan(dp_count, param_count, rows, width, units, ITERS)
    names = [name for name, _ in plan]
    vspec = pl.BlockSpec(memory_space=pltpu.VMEM)
    block = width // dp_count
    step_unit, kl_tile = pl.pallas_call(
        functools.partial(_mega_kernel, names, dp_count, param_count, ITERS, batch),
        out_shape=(jax.ShapeDtypeStruct((block, units), jnp.float32), jax.ShapeDtypeStruct((8, 128), jnp.float32)),
        in_specs=[vspec] * 8,
        out_specs=(vspec, vspec),
        scratch_shapes=[spec for _, spec in plan],
        compiler_params=pltpu.CompilerParams(collective_id=0, has_side_effects=True, vmem_limit_bytes=60 * 1024 * 1024),
        name="trust_region_step",
    )(features, w_hidden, whtb, whtf, bmT, actT, adv, ivT)
    return (step_unit, kl_tile[0, 0])


def solution(mesh):
    return jax.shard_map(
        shards,
        mesh=mesh,
        in_specs=(
            P("dp", None),
            P(None, "param"),
            P("param", None),
            P("dp", None),
            P("dp", None),
            P("dp"),
            P(),
        ),
        out_specs=(P("dp", "param"), P()),
        check_vma=False,
    )
```

```python
import functools

import jax
import jax.numpy as jnp
from jax import lax
from jax.experimental import pallas as pl
from jax.experimental.pallas import tpu as pltpu
from jax.sharding import PartitionSpec as P

D = 2048
UNITS = 2048
ITERS = 2


DAMPING = 0.01
TRIAL_KL = 4.0

MESH = pl.DeviceIdType.MESH
AXES = ("dp", "param")
ACT_PAD = 48
HEAD_ROWS = 24
HIGHEST = lax.Precision.HIGHEST


def _device(axis, partner):
    return tuple(partner if name == axis else lax.axis_index(name) for name in AXES)


def _tile_sum(x):
    return jnp.sum(jnp.sum(x, axis=0, keepdims=True), axis=1, keepdims=True)


def _scratch_plan(n_dp, n_pa, rows, width, units, iters):
    f32, bf16 = jnp.float32, jnp.bfloat16
    groups = n_pa // (ACT_PAD // HEAD_ROWS)
    lanes = rows // groups
    dma = pltpu.SemaphoreType.DMA(())
    plan = [
        ("fvm", pltpu.VMEM((rows, width), bf16)),
        ("fsem", dma),
        ("pre", pltpu.VMEM((rows, units), f32)),
        ("hid", pltpu.VMEM((rows, units), f32)),
        ("slope", pltpu.VMEM((rows, units), f32)),
        ("gb", pltpu.VMEM((rows, units), bf16)),
        ("chg", pltpu.VMEM((rows, units), f32)),
        ("part", pltpu.VMEM((width, units), f32)),
        ("featT", pltpu.VMEM((width, rows), bf16)),
        ("grad", pltpu.VMEM((width, units), f32)),
        ("x", pltpu.VMEM((width, units), f32)),
        ("r", pltpu.VMEM((width, units), f32)),
        ("p", pltpu.VMEM((width, units), f32)),
        ("pb", pltpu.VMEM((width, units), bf16)),
    ]
    for h in range(iters + 2):
        plan += [
            (f"hloc{h}", pltpu.VMEM((ACT_PAD, rows), f32)),
            (f"hrecv{h}", pltpu.VMEM((n_pa, HEAD_ROWS, lanes), f32)),
            (f"hgat{h}", pltpu.VMEM((ACT_PAD, rows), f32)),
        ] + [(f"hsem{h}_{i}", dma) for i in range(4)]
    for d in range(iters):
        plan += [
            (f"drecv{d}", pltpu.VMEM((n_dp, width // n_dp, units), f32)),
            (f"dgat{d}", pltpu.VMEM((width, units), f32)),
        ] + [(f"dsem{d}_{i}", dma) for i in range(4)]
    for k in range(iters + 2):
        plan += [
            (f"stile{k}", pltpu.VMEM((8, 128), f32)),
            (f"srecv{k}", pltpu.VMEM((n_pa, 8, 128), f32)),
        ] + [(f"ssem{k}_{i}", dma) for i in range(2)]
    plan += [
        ("ltile", pltpu.VMEM((8, 128), f32)),
        ("lrecv", pltpu.VMEM((n_dp, 8, 128), f32)),
        ("lsem0", dma),
        ("lsem1", dma),
        ("ktile", pltpu.VMEM((8, 128), f32)),
        ("krecv", pltpu.VMEM((n_dp, 8, 128), f32)),
        ("ksem0", dma),
        ("ksem1", dma),
    ]
    return plan


def _mega_kernel(names, n_dp, n_pa, iters, batch, *refs):
    (feat_hbm, wh, whtb, whtf, bmT, actT, adv, ivT, step_out, kl_out) = refs[:10]
    s = dict(zip(names, refs[10:]))
    feat = s["fvm"]
    rows, width = feat.shape
    units = wh.shape[1]
    groups = n_pa // (ACT_PAD // HEAD_ROWS)
    lanes = rows // groups
    cdp = width // n_dp
    md = lax.axis_index("dp")
    mp = lax.axis_index("param")
    order = lambda n: sorted(range(1, n), key=lambda j: (min(j, n - j), j))
    dpeers = [lax.rem(md + j, n_dp) for j in order(n_dp)]
    ppeers = [lax.rem(mp + j, n_pa) for j in order(n_pa)]

    barrier = pltpu.get_barrier_semaphore()
    for p in dpeers:
        pl.semaphore_signal(barrier, inc=1, device_id=_device("dp", p), device_id_type=MESH)
    for p in ppeers:
        pl.semaphore_signal(barrier, inc=1, device_id=_device("param", p), device_id_type=MESH)
    fcopy = pltpu.make_async_copy(feat_hbm, feat, s["fsem"])
    fcopy.start()
    fcopy.wait()

    def wait_all(buf, count, send_sem, recv_sem, axis):
        cp = pltpu.make_async_remote_copy(
            src_ref=buf.at[pl.ds(0, count)],
            dst_ref=buf.at[pl.ds(0, count)],
            send_sem=send_sem,
            recv_sem=recv_sem,
            device_id=_device(axis, lax.axis_index(axis)),
            device_id_type=MESH,
        )
        cp.wait_send()
        cp.wait_recv()

    def send(src, dst, send_sem, recv_sem, axis, peer):
        pltpu.make_async_remote_copy(
            src_ref=src, dst_ref=dst, send_sem=send_sem, recv_sem=recv_sem,
            device_id=_device(axis, peer), device_id_type=MESH,
        ).start()

    def hchunk(buf, k):
        r0 = pl.multiple_of((k // groups) * HEAD_ROWS, 8)
        l0 = pl.multiple_of(lax.rem(k, groups) * lanes, 128)
        return buf.at[pl.ds(r0, HEAD_ROWS), pl.ds(l0, lanes)]

    def head_allreduce(h, extra=None):
        loc, recv, gat = s[f"hloc{h}"], s[f"hrecv{h}"], s[f"hgat{h}"]
        sa, ra, sb, rb = (s[f"hsem{h}_{i}"] for i in range(4))
        if extra is not None:
            tile, erecv = s[f"stile{extra}"], s[f"srecv{extra}"]
            es, er = s[f"ssem{extra}_0"], s[f"ssem{extra}_1"]
        wait_all(recv, n_pa - 1, sa, ra, "param")
        recv[mp] = hchunk(loc, mp)[...]
        acc = recv[0]
        for i in range(1, n_pa):
            acc = acc + recv[i]
        hchunk(gat, mp)[...] = acc
        for p in ppeers:
            send(hchunk(gat, mp), hchunk(gat, mp), sb, rb, "param", p)
        total = None
        if extra is not None:
            wait_all(erecv, n_pa - 1, es, er, "param")
            erecv[mp] = tile[...]
            total = erecv[0]
            for i in range(1, n_pa):
                total = total + erecv[i]
        wait_all(recv, n_pa - 1, sb, rb, "param")
        return total

    def dp_allreduce(d):
        recv, gat = s[f"drecv{d}"], s[f"dgat{d}"]
        sa, ra, sb, rb = (s[f"dsem{d}_{i}"] for i in range(4))
        part = s["part"]
        wait_all(recv, n_dp - 1, sa, ra, "dp")
        mine = pl.ds(pl.multiple_of(md * cdp, 8), cdp)
        recv[md] = part[mine]
        acc = recv[0]
        for i in range(1, n_dp):
            acc = acc + recv[i]
        gat[mine] = acc
        for p in dpeers:
            send(gat.at[mine], gat.at[mine], sb, rb, "dp", p)
        wait_all(recv, n_dp - 1, sb, rb, "dp")
        return gat

    def param_start(k, values):
        tile, recv = s[f"stile{k}"], s[f"srecv{k}"]
        ss, sr = s[f"ssem{k}_0"], s[f"ssem{k}_1"]
        row = lax.broadcasted_iota(jnp.int32, (8, 128), 0)
        t = jnp.zeros((8, 128), jnp.float32)
        for i, v in enumerate(values):
            t = jnp.where(row == i, jnp.broadcast_to(v, (8, 128)), t)
        tile[...] = t
        for p in ppeers:
            send(tile, recv.at[mp], ss, sr, "param", p)

    def param_finish(k, count):
        tile, recv = s[f"stile{k}"], s[f"srecv{k}"]
        ss, sr = s[f"ssem{k}_0"], s[f"ssem{k}_1"]
        wait_all(recv, n_pa - 1, ss, sr, "param")
        recv[mp] = tile[...]
        total = recv[0]
        for i in range(1, n_pa):
            total = total + recv[i]
        return [total[i:i + 1, 0:1] for i in range(count)]

    def param_round(k, values):
        param_start(k, values)
        return param_finish(k, len(values))

    def expand_head(vec_b, out, make_vals, h, extra=None, entry=False):
        loc, recv = s[f"hloc{h}"], s[f"hrecv{h}"]
        sa, ra = s[f"hsem{h}_0"], s[f"hsem{h}_1"]
        if extra is not None:
            tile, erecv = s[f"stile{extra}"], s[f"srecv{extra}"]
            es, er = s[f"ssem{extra}_0"], s[f"ssem{extra}_1"]
            for p in ppeers:
                send(tile, erecv.at[mp], es, er, "param", p)
        blk = max(lanes, 256)
        for b in range(rows // blk):
            r0 = b * blk
            out[pl.ds(r0, blk), :] = jnp.dot(feat[pl.ds(r0, blk), :], vec_b[...], preferred_element_type=jnp.float32)
            vals = make_vals(r0, blk)
            loc[:, pl.ds(r0, blk)] = lax.dot_general(
                whtb[...], vals, (((1,), (1,)), ((), ())), preferred_element_type=jnp.float32
            )
            if entry:
                continue
            for lg in range(r0 // lanes, (r0 + blk) // lanes):
                for rg in range(ACT_PAD // HEAD_ROWS):
                    k = rg * groups + lg

                    @pl.when(mp != k)
                    def _():
                        send(hchunk(loc, k), recv.at[mp], sa, ra, "param", k)
        if entry:
            pl.semaphore_wait(barrier, len(dpeers) + len(ppeers))
            for p in ppeers:
                send(hchunk(loc, p), recv.at[mp], sa, ra, "param", p)

    def rowsum(g, d=None):
        part = s["part"]
        blk = max(cdp, min(256, width))
        for b in range(width // blk):
            c0 = b * blk
            part[pl.ds(c0, blk), :] = jnp.dot(
                s["featT"][pl.ds(c0, blk), :], g[...], preferred_element_type=jnp.float32
            )
            if d is None:
                continue
            recv, sa, ra = s[f"drecv{d}"], s[f"dsem{d}_0"], s[f"dsem{d}_1"]
            for k in range(c0 // cdp, (c0 + blk) // cdp):

                @pl.when(md != k)
                def _():
                    send(part.at[pl.ds(k * cdp, cdp)], recv.at[md], sa, ra, "dp", k)

    def pull(momentT):
        gb = s["gb"]
        prod = lax.dot_general(momentT, whtf[...], (((0,), (0,)), ((), ())), precision=HIGHEST,
                               preferred_element_type=jnp.float32)
        gb[...] = (prod * s["slope"][...] / batch).astype(jnp.bfloat16)
        return gb

    def hidden_vals(r0, blk):
        pre = s["pre"][pl.ds(r0, blk), :]
        hidden = jnp.tanh(pre)
        s["hid"][pl.ds(r0, blk), :] = hidden
        s["slope"][pl.ds(r0, blk), :] = 1.0 - hidden * hidden
        return hidden.astype(jnp.bfloat16)

    def change_vals(r0, blk):
        return (s["chg"][pl.ds(r0, blk), :] * s["slope"][pl.ds(r0, blk), :]).astype(jnp.bfloat16)

    def shift_vals(r0, blk):
        moved = jnp.tanh(s["pre"][pl.ds(r0, blk), :] + s["chg"][pl.ds(r0, blk), :])
        return (moved - s["hid"][pl.ds(r0, blk), :]).astype(jnp.bfloat16)

    tblk = min(256, width)
    for c in range(width // tblk):
        s["featT"][pl.ds(c * tblk, tblk), :] = feat[:, pl.ds(c * tblk, tblk)].T
    expand_head(wh, s["pre"], hidden_vals, 0, entry=True)
    head_allreduce(0)
    meanT = bmT[...] + s["hgat0"][...]
    deltaT = adv[...] * (actT[...] - meanT) * ivT[...]
    rowsum(pull(deltaT), 0)
    grad = dp_allreduce(0)[...]
    s["grad"][...] = grad
    s["r"][...] = grad
    s["p"][...] = grad
    s["x"][...] = jnp.zeros_like(grad)
    s["pb"][...] = grad.astype(jnp.bfloat16)
    s["stile0"][...] = jnp.broadcast_to(_tile_sum(grad * grad), (8, 128))
    rr = None
    for t in range(iters):
        expand_head(s["pb"], s["chg"], change_vals, t + 1, extra=0 if t == 0 else None)
        total = head_allreduce(t + 1, extra=0 if t == 0 else None)
        if t == 0:
            rr = total[0:1, 0:1]
        rowsum(pull(s[f"hgat{t + 1}"][...] * ivT[...]), t + 1 if t + 1 < iters else None)
        direction = s["p"][...]
        resid = s["r"][...]
        if t + 1 == iters:
            part = s["part"][...]
            sol = s["x"][...]
            row = lax.broadcasted_iota(jnp.int32, (8, 128), 0)
            lt = jnp.where(row == 0, jnp.broadcast_to(_tile_sum(direction * part), (8, 128)),
                           jnp.broadcast_to(_tile_sum(sol * part), (8, 128)))
            s["ltile"][...] = lt
            for p in dpeers:
                send(s["ltile"], s["lrecv"].at[md], s["lsem0"], s["lsem1"], "dp", p)
            wait_all(s["lrecv"], n_dp - 1, s["lsem0"], s["lsem1"], "dp")
            s["lrecv"][md] = s["ltile"][...]
            lsum = s["lrecv"][0]
            for i in range(1, n_dp):
                lsum = lsum + s["lrecv"][i]
            gap = s["grad"][...] - resid
            param_start(t + 1, [
                lsum[0:1, 0:1] + DAMPING * _tile_sum(direction * direction),
                _tile_sum(sol * gap),
                lsum[1:2, 0:1] + DAMPING * _tile_sum(sol * direction),
                _tile_sum(direction * gap),
            ])
            curv, x_gap, x_img, p_gap = param_finish(t + 1, 4)
            alpha = rr / curv
            x_new = sol + alpha * direction
            shs = x_gap + alpha * (x_img + p_gap) + alpha * alpha * curv
            s["x"][...] = x_new
            blk = step_out.shape[0]
            step_out[...] = s["x"][pl.ds(pl.multiple_of(md * blk, 8), blk)] * jnp.sqrt(D * UNITS / shs)
            reach = jnp.sqrt(2.0 * TRIAL_KL / shs)
            s["pb"][...] = (reach * x_new).astype(jnp.bfloat16)
            continue
        image = dp_allreduce(t + 1)[...] + DAMPING * direction
        if t + 1 < iters:
            curv, r_img, img_img = param_round(
                t + 1, [_tile_sum(direction * image), _tile_sum(resid * image), _tile_sum(image * image)]
            )
            alpha = rr / curv
            s["x"][...] = s["x"][...] + alpha * direction
            r_new = resid - alpha * image
            s["r"][...] = r_new
            rr_next = rr - 2.0 * alpha * r_img + alpha * alpha * img_img
            p_new = r_new + rr_next / rr * direction
            s["p"][...] = p_new
            s["pb"][...] = p_new.astype(jnp.bfloat16)
            rr = rr_next
    last = iters + 1
    expand_head(s["pb"], s["chg"], shift_vals, last)
    loc, recv = s[f"hloc{last}"], s[f"hrecv{last}"]
    wait_all(recv, n_pa - 1, s[f"hsem{last}_0"], s[f"hsem{last}_1"], "param")
    recv[mp] = hchunk(loc, mp)[...]
    acc = recv[0]
    for i in range(1, n_pa):
        acc = acc + recv[i]
    (kpart,) = param_round(iters + 1, [_tile_sum(acc * acc * hchunk(ivT, mp)[...])])
    ktile, krecv = s["ktile"], s["krecv"]
    ktile[...] = jnp.broadcast_to(kpart, (8, 128))
    for p in dpeers:
        send(ktile, krecv.at[md], s["ksem0"], s["ksem1"], "dp", p)
    wait_all(krecv, n_dp - 1, s["ksem0"], s["ksem1"], "dp")
    krecv[md] = ktile[...]
    ktot = krecv[0]
    for i in range(1, n_dp):
        ktot = ktot + krecv[i]
    kl_out[...] = ktot / (2.0 * batch) / TRIAL_KL


def shards(features, w_hidden, w_head, base_mean, actions, advantages, log_std):
    rows, width = features.shape
    units = w_hidden.shape[1]
    act = w_head.shape[1]
    dp_count = lax.axis_size("dp")
    param_count = lax.axis_size("param")
    batch = rows * dp_count
    inv_var = jnp.exp(-2.0 * log_std)
    padT = lambda a: jnp.pad(a.T, ((0, ACT_PAD - act), (0, 0)))
    whtb = padT(w_head)
    whtf = whtb.astype(jnp.float32)
    bmT = padT(base_mean)
    actT = padT(actions)
    ivT = jnp.pad(jnp.broadcast_to(inv_var[:, None], (act, rows)), ((0, ACT_PAD - act), (0, 0)))
    adv = advantages.reshape(1, rows)
    plan = _scratch_plan(dp_count, param_count, rows, width, units, ITERS)
    names = [name for name, _ in plan]
    vspec = pl.BlockSpec(memory_space=pltpu.VMEM)
    block = width // dp_count
    step_unit, kl_tile = pl.pallas_call(
        functools.partial(_mega_kernel, names, dp_count, param_count, ITERS, batch),
        out_shape=(jax.ShapeDtypeStruct((block, units), jnp.float32), jax.ShapeDtypeStruct((8, 128), jnp.float32)),
        in_specs=[pl.BlockSpec(memory_space=pl.ANY)] + [vspec] * 7,
        out_specs=(vspec, vspec),
        scratch_shapes=[spec for _, spec in plan],
        compiler_params=pltpu.CompilerParams(collective_id=0, has_side_effects=True, vmem_limit_bytes=60 * 1024 * 1024),
        name="trust_region_step",
    )(features, w_hidden, whtb, whtf, bmT, actT, adv, ivT)
    return (step_unit, kl_tile[0, 0])


def solution(mesh):
    return jax.shard_map(
        shards,
        mesh=mesh,
        in_specs=(
            P("dp", None),
            P(None, "param"),
            P("param", None),
            P("dp", None),
            P("dp", None),
            P("dp"),
            P(),
        ),
        out_specs=(P("dp", "param"), P()),
        check_vma=False,
    )
```
